32 devices in a mesh: fsdp: 4 (over y, x), context: 4 (over z), tensor: 2 (over core).
Axes of the slice: x: 2, y: 2, z: 4, core: 2. Of those that a mesh axis runs over, the one named last changes fastest.
Arguments:
- inputs: bfloat16 [2048, 1024], P(('fsdp', 'context')), may hold values from -6 to 6
- seq_lengths: int32 [4, 2], P('fsdp'), may hold values from 170 to 342, as said below
- norm_gains: bfloat16 [2, 1024], P(None, ('fsdp', 'context')), may hold values from 0.5 to 1.5
- mamba_in: bfloat16 [1024, 2, 1536], P(('fsdp', 'context'), None, 'tensor'), may hold values from -0.1875 to 0.1875
- dt_proj: bfloat16 [1024, 24], P(('fsdp', 'context'), 'tensor'), may hold values from -0.1875 to 0.1875
- bc_proj: bfloat16 [1024, 256], P(('fsdp', 'context')), may hold values from -0.1875 to 0.1875
- mamba_chan: bfloat16 [24, 384], P('tensor', ('fsdp', 'context')), may hold values from -0.5 to 1.25
- bc_conv: bfloat16 [5, 256], P(None, ('fsdp', 'context')), may hold values from -0.5 to 0.5
- head_params: float32 [3, 24], P(None, 'tensor'), may hold values from -10 to 3, as said below
- query_proj: bfloat16 [1024, 512], P(('fsdp', 'context'), 'tensor'), may hold values from -0.1875 to 0.1875
- kv_proj: bfloat16 [1024, 2, 128], P(('fsdp', 'context'), None, 'tensor'), may hold values from -0.1875 to 0.1875
- attn_out: bfloat16 [512, 1024], P('tensor', ('fsdp', 'context')), may hold values from -3 to 3
- mamba_out: bfloat16 [1536, 1024], P('tensor', ('fsdp', 'context')), may hold values from -0.15625 to 0.15625
- mlp_in: bfloat16 [1024, 2, 2048], P(('fsdp', 'context'), None, 'tensor'), may hold values from -0.1875 to 0.1875
- mlp_out: bfloat16 [2048, 1024], P('tensor', ('fsdp', 'context')), may hold values from -0.125 to 0.125
- out_grad: bfloat16 [2048, 1024], P(('fsdp', 'context')), may hold values from -6 to 6
Outputs:
- output: bfloat16 [2048, 1024], P(('fsdp', 'context'))
- input_grad: float32 [2048, 1024], P(('fsdp', 'context'))
- grad_norm_gains: float32 [2, 1024], P(None, ('fsdp', 'context'))
- grad_mamba_in: float32 [1024, 2, 1536], P(('fsdp', 'context'), None, 'tensor')
- grad_dt_proj: float32 [1024, 24], P(('fsdp', 'context'), 'tensor')
- grad_bc_proj: float32 [1024, 256], P(('fsdp', 'context'))
- grad_mamba_chan: float32 [24, 384], P('tensor', ('fsdp', 'context'))
- grad_bc_conv: float32 [5, 256], P(None, ('fsdp', 'context'))
- grad_head_params: float32 [3, 24], P(None, 'tensor')
- grad_query_proj: float32 [1024, 512], P(('fsdp', 'context'), 'tensor')
- grad_kv_proj: float32 [1024, 2, 128], P(('fsdp', 'context'), None, 'tensor')
- grad_attn_out: float32 [512, 1024], P('tensor', ('fsdp', 'context'))
- grad_mamba_out: float32 [1536, 1024], P('tensor', ('fsdp', 'context'))
- grad_mlp_in: float32 [1024, 2, 2048], P(('fsdp', 'context'), None, 'tensor')
- grad_mlp_out: float32 [2048, 1024], P('tensor', ('fsdp', 'context'))
The draws below stay inside these ranges and needn't reach their ends.
Inputs may be any that keep to these rules, and one draw needn't show every extreme that they name: `seq_lengths`: row g lists, in order, the lengths of the 2 sequences that fill the 512 rows of token group g; they sum to 512. `head_params`: rows are step bias, log decay rate and skip weight of a head.
All inputs are finite; a program needn't handle non-finite values.
Results may differ from the reference program's by a relative error of at most 0.018.
Values may be sent and summed in bfloat16 or wider, within the bound.
No kernel may reach another device: no remote copies, remote signals or barrier semaphores. Data moves between devices by JAX's collectives and lax.ppermute only.
A program may use at most 128 MiB of HBM per device.

```python
import math
import jax
import jax.numpy as jnp
from jax import lax

D = 1024
FF = 2048
MH = 24
HDIM = 64
NSTATE = 128
KCONV = 4
QH = 8
KVH = 2
TOK_DEV = 128
GROUP = 512
MIN_LEN = 170
NSEQ = 2
TOKENS = 2048
N_FSDP = 4
N_CONTEXT = 4


def draw_seq_lengths(key, part):
    extra = GROUP - NSEQ * MIN_LEN
    own_key = jax.random.fold_in(key, 7331)
    cuts = jnp.sort(jax.random.randint(own_key, (N_FSDP, NSEQ - 1), 0, extra + 1), axis=1)
    cuts = cuts.at[0].set(extra)
    edges = jnp.concatenate([jnp.zeros((N_FSDP, 1), jnp.int32), cuts.astype(jnp.int32), jnp.full((N_FSDP, 1), extra, jnp.int32)], axis=1)
    return (MIN_LEN + edges[:, 1:] - edges[:, :-1]).astype(jnp.int32)


def draw_head_params(key, part):
    key_step, key_rate, key_skip = jax.random.split(key, 3)
    dt_step = jnp.exp(jax.random.uniform(key_step, (MH,), jnp.float32, math.log(0.001), math.log(0.1)))
    rates = jnp.exp(jax.random.uniform(key_rate, (MH,), jnp.float32, 0.0, math.log(16.0)))
    skips = jax.random.uniform(key_skip, (MH,), jnp.float32, 0.5, 1.5)
    step_bias = dt_step + jnp.log(-jnp.expm1(-dt_step))
    return jnp.stack([step_bias, jnp.log(rates), skips], axis=0).astype(jnp.float32)


def draw_mamba_chan(key, part):
    key_taps, key_bias, key_gain = jax.random.split(key, 3)
    conv_taps = jax.random.uniform(key_taps, (MH, KCONV * HDIM), jnp.float32, -0.5, 0.5)
    conv_bias = jax.random.uniform(key_bias, (MH, HDIM), jnp.float32, -0.5, 0.5)
    gain_vals = 1.0 + 0.1 * jnp.clip(jax.random.normal(key_gain, (MH, HDIM), jnp.float32), -2.0, 2.0)
    return jnp.concatenate([conv_taps, conv_bias, gain_vals], axis=1).astype(jnp.bfloat16)


def shard_levels(stream_key, extent, cuts, least, high):
    gain, own = 1.0, jax.random.fold_in(stream_key, 6)
    for position, blocks in cuts:
        draws = jnp.exp(jax.random.uniform(jax.random.fold_in(own, position), (blocks,), jnp.float32, least / len(cuts), high / len(cuts)))
        gain = gain * jnp.repeat(draws, extent[position] // blocks).reshape([-1 if axis == position else 1 for axis in range(len(extent))])
    return gain


def normal_values(stream_key, dims, spread, most, cuts=(), kind=jnp.bfloat16):
    result = jax.random.normal(stream_key, dims, jnp.float32) * spread
    if len(cuts) > 0:
        result = shard_levels(stream_key, dims, cuts, -0.22, 0.18) * result
    return jnp.clip(result, min=-most, max=most).astype(kind)


def setup_inputs(seed: int = 0) -> dict:
    splits = jax.random.split(jax.random.key(seed), 17)
    inputs = normal_values(splits[0], (TOKENS, D), 1.0, 6.0, ((0, 16),))
    seq_lengths = draw_seq_lengths(jax.random.fold_in(splits[16], 71), 0)
    norm_gains = jnp.clip(1.0 + 0.1 * jax.random.normal(splits[2], (2, D), jnp.float32), 0.5, 1.5).astype(jnp.bfloat16)
    mamba_in = normal_values(splits[3], (D, 2, MH * HDIM), D ** -0.5, 0.1875, ((0, 16), (2, 2)))
    dt_proj = normal_values(splits[4], (D, MH), D ** -0.5, 0.1875, ((0, 16), (1, 2)))
    bc_proj = normal_values(splits[5], (D, 2 * NSTATE), D ** -0.5, 0.1875, ((0, 16),))
    mamba_chan = draw_mamba_chan(jax.random.fold_in(splits[16], 71), 0)
    bc_conv = jnp.clip(jax.random.uniform(splits[7], (KCONV + 1, 2 * NSTATE), jnp.float32, -0.5, 0.5) * shard_levels(splits[7], (KCONV + 1, 2 * NSTATE), ((1, 16),), -0.4, 0.0), -0.5, 0.5).astype(jnp.bfloat16)
    head_params = draw_head_params(jax.random.fold_in(splits[16], 71), 0)
    query_proj = normal_values(splits[9], (D, QH * HDIM), D ** -0.5, 0.1875, ((0, 16), (1, 2)))
    kv_proj = normal_values(splits[10], (D, 2, KVH * HDIM), D ** -0.5, 0.1875, ((0, 16), (2, 2)))
    attn_out = normal_values(splits[11], (QH * HDIM, D), (max(1, QH * HDIM // 128)) ** -0.5, 3.0, ((0, 2), (1, 16)))
    mamba_out = normal_values(splits[12], (MH * HDIM, D), (MH * HDIM) ** -0.5, 0.15625, ((0, 2), (1, 16)))
    mlp_in = normal_values(splits[13], (D, 2, FF), D ** -0.5, 0.1875, ((0, 16), (2, 2)))
    mlp_out = normal_values(splits[14], (FF, D), FF ** -0.5, 0.125, ((0, 2), (1, 16)))
    out_grad = normal_values(splits[15], (TOKENS, D), 1.0, 6.0, ((0, 16),))
    return {"inputs": inputs, "seq_lengths": seq_lengths, "norm_gains": norm_gains, "mamba_in": mamba_in, "dt_proj": dt_proj, "bc_proj": bc_proj, "mamba_chan": mamba_chan, "bc_conv": bc_conv, "head_params": head_params, "query_proj": query_proj, "kv_proj": kv_proj, "attn_out": attn_out, "mamba_out": mamba_out, "mlp_in": mlp_in, "mlp_out": mlp_out, "out_grad": out_grad}


NORM_EPS = 1e-05
ROPE_BASE = 100000000000.0
PRECISE = lax.Precision.HIGHEST

def silu_grad(values):
    sigma = jax.nn.sigmoid(values)
    return sigma * (1.0 + values * (1.0 - sigma))

def rms_forward(values):
    inv_rms = lax.rsqrt(lax.optimization_barrier(jnp.mean(values * values, axis=-1, keepdims=True)) + NORM_EPS)
    return (values * inv_rms, inv_rms)

def rms_backward(grad_out, normed, inv_rms, gain_vec):
    grad_normed = grad_out * gain_vec[None, :]
    grad_values = inv_rms * (grad_normed - normed * lax.optimization_barrier(jnp.mean(grad_normed * normed, axis=-1, keepdims=True)))
    return (grad_values, lax.optimization_barrier(jnp.sum(grad_out * normed, axis=0)))

def rope_tables(positions, head_width):
    half_width = head_width // 2
    freqs = jnp.power(ROPE_BASE, -jnp.arange(half_width).astype(jnp.float32) * (2.0 / head_width))
    angles = positions.astype(jnp.float32)[:, None] * freqs[None, :]
    angles = jnp.concatenate([angles, angles], axis=1)
    return (jnp.cos(angles), jnp.sin(angles))

def rotate_half(values):
    half_width = values.shape[-1] // 2
    return jnp.concatenate([-values[..., half_width:], values[..., :half_width]], axis=-1)

def apply_rope(values, cosine, sine):
    return values * cosine[:, None, :] + rotate_half(values) * sine[:, None, :]

def undo_rope(grads, cosine, sine):
    return grads * cosine[:, None, :] - rotate_half(grads) * sine[:, None, :]

def sequence_layout(lengths_row, row_start, row_count):
    starts = jnp.cumsum(lengths_row) - lengths_row
    row_ids = row_start + jnp.arange(row_count, dtype=jnp.int32)
    inside = row_ids[:, None] >= starts[None, :]
    seq_ids = lax.optimization_barrier(jnp.sum(inside.astype(jnp.int32), axis=1)) - 1
    seq_start = lax.optimization_barrier(jnp.max(jnp.where(inside, starts[None, :], 0), axis=1))
    return (seq_ids.astype(jnp.int32), (row_ids - seq_start).astype(jnp.int32))

def conv_block(extended, conv_taps, conv_bias, ids_ext):
    num_taps = conv_taps.shape[0]
    row_count = extended.shape[0] - num_taps + 1
    current = ids_ext[num_taps - 1:]
    total = jnp.zeros((row_count, extended.shape[1]), jnp.float32) + conv_bias[None, :]
    for offset in range(num_taps):
        same_seq = (ids_ext[offset:offset + row_count] == current).astype(jnp.float32)
        total = total + conv_taps[offset][None, :] * extended[offset:offset + row_count] * same_seq[:, None]
    return total

def unpack_chan(chan_all, conv_all):
    num_heads = chan_all.shape[0]
    head_width = chan_all.shape[1] // (KCONV + 2)
    chan_wide = chan_all.astype(jnp.float32)
    conv_wide = conv_all.astype(jnp.float32)
    taps_x = jnp.transpose(chan_wide[:, :KCONV * head_width].reshape(num_heads, KCONV, head_width), (1, 0, 2)).reshape(KCONV, num_heads * head_width)
    bias_x = chan_wide[:, KCONV * head_width:(KCONV + 1) * head_width].reshape(-1)
    norm_gain = chan_wide[:, (KCONV + 1) * head_width:].reshape(-1)
    return (jnp.concatenate([taps_x, conv_wide[:KCONV]], axis=1), jnp.concatenate([bias_x, conv_wide[KCONV]]), norm_gain)

def pack_chan_grads(grad_taps, grad_bias, grad_gain, num_heads):
    chan_x = grad_gain.shape[0]
    head_width = chan_x // num_heads
    taps_x = jnp.transpose(grad_taps[:, :chan_x].reshape(KCONV, num_heads, head_width), (1, 0, 2)).reshape(num_heads, KCONV * head_width)
    chan_grad = jnp.concatenate([taps_x, grad_bias[:chan_x].reshape(num_heads, head_width), grad_gain.reshape(num_heads, head_width)], axis=1)
    conv_grad = jnp.concatenate([grad_taps[:, chan_x:], grad_bias[chan_x:][None, :]], axis=0)
    return (chan_grad, conv_grad)

def head_rates(dt_raw, head_vec):
    dt_step = jax.nn.softplus(dt_raw + head_vec[0][None, :])
    log_cum = jnp.cumsum(-dt_step * jnp.exp(head_vec[1])[None, :], axis=0)
    return (dt_step, log_cum)

def ssd_output(ssm_x, b_rows, c_rows, dt_raw, head_vec, seq_ids, prev_id, state_in):
    dt_step, log_cum = head_rates(dt_raw, head_vec)
    row_order = jnp.arange(ssm_x.shape[0])
    linked = (seq_ids[:, None] == seq_ids[None, :]) & (row_order[:, None] >= row_order[None, :])
    log_gaps = log_cum.T[:, :, None] - log_cum.T[:, None, :]
    decays = jnp.exp(jnp.where(linked[None, :, :], log_gaps, -1e+30))
    c_dot_b = jnp.dot(c_rows, b_rows.T, precision=PRECISE, preferred_element_type=jnp.float32)
    mixing = decays * c_dot_b[None, :, :] * dt_step.T[:, None, :]
    within = jnp.einsum('hts,shp->thp', mixing, ssm_x, precision=PRECISE)
    carried = jnp.einsum('tn,hpn->thp', c_rows, state_in, precision=PRECISE)
    entry_decay = jnp.exp(log_cum) * (seq_ids == prev_id).astype(jnp.float32)[:, None]
    return within + carried * entry_decay[:, :, None] + head_vec[2][None, :, None] * ssm_x

def ssd_state(ssm_x, b_rows, dt_raw, head_vec, seq_ids, prev_id, state_in):
    dt_step, log_cum = head_rates(dt_raw, head_vec)
    log_last = log_cum[-1]
    same_last = (seq_ids == seq_ids[-1])[:, None]
    tail_decay = jnp.exp(jnp.where(same_last, log_last[None, :] - log_cum, -1e+30)) * dt_step
    fresh_state = jnp.einsum('sh,shp,sn->hpn', tail_decay, ssm_x, b_rows, precision=PRECISE)
    through = jnp.exp(log_last) * (seq_ids[-1] == prev_id).astype(jnp.float32)
    return fresh_state + through[:, None, None] * state_in

def attend_forward(queries, key_rows, value_rows, allowed):
    score_scale = queries.shape[-1] ** (-0.5)
    scores = jnp.dot(queries, key_rows.T, preferred_element_type=jnp.float32) * score_scale
    scores = jnp.where(allowed, scores, -1e+30)
    row_max = lax.optimization_barrier(jnp.max(scores, axis=1, keepdims=True))
    exp_scores = jnp.exp(scores - row_max)
    row_total = lax.optimization_barrier(jnp.sum(exp_scores, axis=1, keepdims=True))
    attn_prob = (exp_scores / row_total).astype(jnp.bfloat16)
    attended = jnp.dot(attn_prob, value_rows, preferred_element_type=jnp.float32)
    return (attended, row_max[:, 0] + jnp.log(row_total[:, 0]))

def attend_backward(queries, key_rows, value_rows, allowed, lse_rows, grad_rows, delta_rows):
    score_scale = queries.shape[-1] ** (-0.5)
    scores = jnp.dot(queries, key_rows.T, preferred_element_type=jnp.float32) * score_scale
    attn_prob = jnp.exp(jnp.where(allowed, scores, -1e+30) - lse_rows[:, None])
    grad_prob = jnp.dot(grad_rows, value_rows.T, preferred_element_type=jnp.float32)
    grad_scores = (attn_prob * (grad_prob - delta_rows[:, None])).astype(jnp.bfloat16)
    grad_q = jnp.dot(grad_scores, key_rows, preferred_element_type=jnp.float32) * score_scale
    grad_k = jnp.dot(grad_scores.T, queries, preferred_element_type=jnp.float32) * score_scale
    grad_v = jnp.dot(attn_prob.astype(jnp.bfloat16).T, grad_rows, preferred_element_type=jnp.float32)
    return (grad_q, grad_k, grad_v)

def block_shape(num_q, num_kv):
    group_size = num_q // num_kv
    per_block = 2 if group_size % 2 == 0 else 1
    return (group_size, per_block, group_size // per_block)

def to_blocks(array, kv_head, group_size, num_blocks):
    picked = array[:, kv_head * group_size:(kv_head + 1) * group_size]
    moved = jnp.moveaxis(picked, 1, 0)
    return moved.reshape((num_blocks, -1) + moved.shape[2:])

def from_blocks(array, group_size, row_count):
    return jnp.moveaxis(array.reshape((group_size, row_count) + array.shape[2:]), 0, 1)

def attention_forward(queries, key_vals, allowed):
    row_count, num_q, head_width = queries.shape
    num_kv = key_vals.shape[1] // 2
    group_size, per_block, num_blocks = block_shape(num_q, num_kv)
    mask_rows = jnp.tile(allowed, (per_block, 1))
    out_list = []
    lse_list = []
    for kv_head in range(num_kv):
        key_rows = key_vals[:, kv_head]
        value_rows = key_vals[:, num_kv + kv_head]

        def one_block(q_block):
            return attend_forward(q_block, key_rows, value_rows, mask_rows)
        attn_blocks, lse_blocks = lax.map(one_block, to_blocks(queries, kv_head, group_size, num_blocks))
        out_list.append(from_blocks(attn_blocks, group_size, row_count))
        lse_list.append(from_blocks(lse_blocks, group_size, row_count))
    return (jnp.concatenate(out_list, axis=1), jnp.concatenate(lse_list, axis=1))

def attention_backward(queries, key_vals, allowed, attn_lse, grad_attn, row_delta):
    row_count, num_q, head_width = queries.shape
    num_kv = key_vals.shape[1] // 2
    group_size, per_block, num_blocks = block_shape(num_q, num_kv)
    mask_rows = jnp.tile(allowed, (per_block, 1))
    key_count = key_vals.shape[0]
    grad_q_list = []
    grad_k_list = []
    grad_v_list = []
    for kv_head in range(num_kv):
        key_rows = key_vals[:, kv_head]
        value_rows = key_vals[:, num_kv + kv_head]

        def one_block(sums, block_items):
            q_block, lse_block, grad_block, delta_block = block_items
            grad_q, grad_k, grad_v = attend_backward(q_block, key_rows, value_rows, mask_rows, lse_block, grad_block, delta_block)
            return ((sums[0] + grad_k, sums[1] + grad_v), grad_q)
        start_sums = (jnp.zeros((key_count, head_width), jnp.float32), jnp.zeros((key_count, head_width), jnp.float32))
        block_items = (to_blocks(queries, kv_head, group_size, num_blocks), to_blocks(attn_lse, kv_head, group_size, num_blocks), to_blocks(grad_attn, kv_head, group_size, num_blocks), to_blocks(row_delta, kv_head, group_size, num_blocks))
        kv_sums, grad_q_blocks = lax.scan(one_block, start_sums, block_items)
        grad_q_list.append(from_blocks(grad_q_blocks, group_size, row_count))
        grad_k_list.append(kv_sums[0][:, None, :])
        grad_v_list.append(kv_sums[1][:, None, :])
    return (jnp.concatenate(grad_q_list, axis=1), jnp.concatenate(grad_k_list + grad_v_list, axis=1))

def reference(inputs, seq_lengths, norm_gains, mamba_in, dt_proj, bc_proj, mamba_chan, bc_conv, head_params, query_proj, kv_proj, attn_out, mamba_out, mlp_in, mlp_out, out_grad):
    conv_taps, conv_bias, norm_gain = unpack_chan(mamba_chan, bc_conv)
    head_vec = head_params.astype(jnp.float32)
    gain_mix = norm_gains[0].astype(jnp.float32)
    gain_mlp = norm_gains[1].astype(jnp.float32)
    chan_x = MH * HDIM
    w_inner = mamba_in.reshape(D, 2 * chan_x)
    w_pair = kv_proj.reshape(D, 2 * KVH * HDIM)
    w_mlpin = mlp_in.reshape(D, 2 * FF)
    w_state = bc_proj.astype(jnp.float32)
    rim_rows = KCONV - 1
    row_ids = jnp.arange(GROUP, dtype=jnp.int32)
    zero_state = jnp.zeros((MH, HDIM, NSTATE), jnp.float32)

    def in_blocks(array):
        return array.reshape((N_CONTEXT, TOK_DEV) + array.shape[1:])

    def group_pass(grad_sums, group_items):
        rows_in, lengths_row, grad_rows = group_items
        ids_ext, pos_ext = sequence_layout(lengths_row, -rim_rows, GROUP + rim_rows)
        seq_ids = ids_ext[rim_rows:]
        positions = pos_ext[rim_rows:]
        prev_ids = ids_ext[(rim_rows - 1 + TOK_DEV * jnp.arange(N_CONTEXT, dtype=jnp.int32)).astype(jnp.int32)]
        allowed = (seq_ids[None, :] == seq_ids[:, None]) & (row_ids[None, :] <= row_ids[:, None])
        values_in = rows_in.astype(jnp.float32)
        normed_one, scale_one = rms_forward(values_in)
        norm_one = (normed_one * gain_mix[None, :]).astype(jnp.bfloat16)
        inner_vals = jnp.dot(norm_one, w_inner, preferred_element_type=jnp.float32).astype(jnp.bfloat16).reshape(GROUP, 2, chan_x)
        z_gate = inner_vals[:, 0].astype(jnp.float32)
        dt_raw = jnp.dot(norm_one, dt_proj, preferred_element_type=jnp.float32)
        bc_raw = jnp.dot(norm_one, bc_proj, preferred_element_type=jnp.float32).astype(jnp.bfloat16)
        conv_in = jnp.concatenate([inner_vals[:, 1], bc_raw], axis=1)
        extended = jnp.concatenate([jnp.zeros((rim_rows, conv_in.shape[1]), jnp.bfloat16), conv_in], axis=0).astype(jnp.float32)
        pre_act = conv_block(extended, conv_taps, conv_bias, ids_ext)
        activated = jax.nn.silu(pre_act)
        ssm_in = activated[:, :chan_x].reshape(GROUP, MH, HDIM)
        state_b = activated[:, chan_x:chan_x + NSTATE]
        state_c = activated[:, chan_x + NSTATE:]
        chain_items = (in_blocks(ssm_in), in_blocks(state_b), in_blocks(state_c), in_blocks(dt_raw), in_blocks(seq_ids), prev_ids)

        def chain_step(state_val, block_items):
            ssm_blk, b_block, c_block, dt_block, id_block, prev_block = block_items
            out_block = ssd_output(ssm_blk, b_block, c_block, dt_block, head_vec, id_block, prev_block, state_val)
            return (ssd_state(ssm_blk, b_block, dt_block, head_vec, id_block, prev_block, state_val), (out_block, state_val))
        chain_out = lax.scan(chain_step, zero_state, chain_items)[1]
        ssm_out = chain_out[0].reshape(GROUP, chan_x)
        states_in = chain_out[1]
        silu_z = jax.nn.silu(z_gate)
        gated_out = ssm_out * silu_z
        sum_squares = lax.optimization_barrier(jnp.sum(gated_out * gated_out, axis=1))
        norm_in = (gated_out * norm_gain[None, :]).astype(jnp.bfloat16)
        mamba_part = jnp.dot(norm_in, mamba_out, preferred_element_type=jnp.float32)
        cosine, sine = rope_tables(positions, HDIM)
        query_vals = jnp.dot(norm_one, query_proj, preferred_element_type=jnp.float32).reshape(GROUP, QH, HDIM)
        pair_vals = jnp.dot(norm_one, w_pair, preferred_element_type=jnp.float32).reshape(GROUP, 2, KVH, HDIM)
        q_rot = apply_rope(query_vals, cosine, sine).astype(jnp.bfloat16)
        key_vals = jnp.concatenate([apply_rope(pair_vals[:, 0], cosine, sine), pair_vals[:, 1]], axis=1).astype(jnp.bfloat16)
        attn_vals, attn_lse = attention_forward(q_rot, key_vals, allowed)
        attn_round = attn_vals.astype(jnp.bfloat16)
        attn_flat = attn_round.reshape(GROUP, QH * HDIM)
        attn_part = jnp.dot(attn_flat, attn_out, preferred_element_type=jnp.float32)
        row_scale = lax.rsqrt(sum_squares / (MH * HDIM) + NORM_EPS)
        residual = values_in + row_scale[:, None] * mamba_part + attn_part
        normed_two, scale_two = rms_forward(residual)
        norm_two = (normed_two * gain_mlp[None, :]).astype(jnp.bfloat16)
        up_gate = jnp.dot(norm_two, w_mlpin, preferred_element_type=jnp.float32).reshape(GROUP, 2, FF)
        gate_val = up_gate[:, 0]
        up_val = up_gate[:, 1]
        mlp_act = (jax.nn.silu(gate_val) * up_val).astype(jnp.bfloat16)
        down_sum = jnp.dot(mlp_act, mlp_out, preferred_element_type=jnp.float32)
        output_rows = (residual + down_sum).astype(jnp.bfloat16)
        grad_top = grad_rows.astype(jnp.float32)
        grad_act = jnp.dot(grad_rows, mlp_out.T, preferred_element_type=jnp.float32)
        g_mlpout = jnp.dot(mlp_act.T, grad_rows, preferred_element_type=jnp.float32)
        grad_upgate = jnp.stack([grad_act * up_val * silu_grad(gate_val), grad_act * jax.nn.silu(gate_val)], axis=1).astype(jnp.bfloat16).reshape(GROUP, 2 * FF)
        g_mlpin = jnp.dot(norm_two.T, grad_upgate, preferred_element_type=jnp.float32)
        grad_norm_two = jnp.dot(grad_upgate, w_mlpin.T, preferred_element_type=jnp.float32)
        grad_res_two, g_gain_mlp = rms_backward(grad_norm_two, normed_two, scale_two, gain_mlp)
        grad_residual = grad_top + grad_res_two
        grad_round = grad_residual.astype(jnp.bfloat16)
        grad_attn = jnp.dot(grad_round, attn_out.T, preferred_element_type=jnp.float32).reshape(GROUP, QH, HDIM)
        g_attnout = jnp.dot(attn_flat.T, grad_round, preferred_element_type=jnp.float32)
        row_delta = lax.optimization_barrier(jnp.sum(grad_attn * attn_round.astype(jnp.float32), axis=2))
        grad_q, grad_kv = attention_backward(q_rot, key_vals, allowed, attn_lse, grad_attn.astype(jnp.bfloat16), row_delta)
        grad_query = undo_rope(grad_q, cosine, sine).astype(jnp.bfloat16).reshape(GROUP, QH * HDIM)
        grad_pair = jnp.stack([undo_rope(grad_kv[:, :KVH], cosine, sine), grad_kv[:, KVH:]], axis=1).astype(jnp.bfloat16).reshape(GROUP, 2 * KVH * HDIM)
        grad_scaled = (row_scale[:, None] * grad_residual).astype(jnp.bfloat16)
        g_mambaout = jnp.dot(norm_in.T, grad_scaled, preferred_element_type=jnp.float32)
        grad_norm_in = jnp.dot(grad_scaled, mamba_out.T, preferred_element_type=jnp.float32)
        grad_rs = lax.optimization_barrier(jnp.sum(grad_residual * mamba_part, axis=1))
        g_normgain = lax.optimization_barrier(jnp.sum(grad_norm_in * gated_out, axis=0))
        grad_gated = grad_norm_in * norm_gain[None, :] - gated_out * (grad_rs * row_scale ** 3 / (MH * HDIM))[:, None]
        grad_ssm = (grad_gated * silu_z).reshape(GROUP, MH, HDIM)
        grad_z = grad_gated * ssm_out * silu_grad(z_gate)
        back_items = chain_items + (states_in, in_blocks(grad_ssm))

        def back_step(state_grad, block_items):
            ssm_blk, b_block, c_block, dt_block, id_block, prev_block, state_val, grad_block = block_items

            def output_map(ssm_rows, b_rows, c_rows, dt_rows, vec_rows, state_rows):
                return ssd_output(ssm_rows, b_rows, c_rows, dt_rows, vec_rows, id_block, prev_block, state_rows)

            def state_map(ssm_rows, b_rows, dt_rows, vec_rows, state_rows):
                return ssd_state(ssm_rows, b_rows, dt_rows, vec_rows, id_block, prev_block, state_rows)
            grads_out = jax.vjp(output_map, ssm_blk, b_block, c_block, dt_block, head_vec, state_val)[1](grad_block)
            grads_state = jax.vjp(state_map, ssm_blk, b_block, dt_block, head_vec, state_val)[1](state_grad)
            return (grads_out[5] + grads_state[4], (grads_out[0] + grads_state[0], grads_out[1] + grads_state[1], grads_out[2], grads_out[3] + grads_state[2], grads_out[4] + grads_state[3]))
        back_out = lax.scan(back_step, zero_state, back_items, reverse=True)[1]
        grad_activated = jnp.concatenate([back_out[0].reshape(GROUP, chan_x), back_out[1].reshape(GROUP, NSTATE), back_out[2].reshape(GROUP, NSTATE)], axis=1)
        grad_dt_raw = back_out[3].reshape(GROUP, MH)
        g_head = lax.optimization_barrier(jnp.sum(back_out[4], axis=0))
        grad_pre = grad_activated * silu_grad(pre_act)

        def conv_map(ext_rows, taps_in, bias_in):
            return conv_block(ext_rows, taps_in, bias_in, ids_ext)
        grad_ext, g_taps, g_cbias = jax.vjp(conv_map, extended, conv_taps, conv_bias)[1](grad_pre)
        grad_conv_in = grad_ext[rim_rows:]
        grad_inner = jnp.stack([grad_z, grad_conv_in[:, :chan_x]], axis=1).astype(jnp.bfloat16).reshape(GROUP, 2 * chan_x)
        grad_bc = grad_conv_in[:, chan_x:]
        grad_step = grad_dt_raw.astype(jnp.bfloat16)
        g_inner = jnp.dot(norm_one.T, grad_inner, preferred_element_type=jnp.float32)
        g_dt = jnp.dot(norm_one.T, grad_step, preferred_element_type=jnp.float32)
        g_state = jnp.dot(norm_one.astype(jnp.float32).T, grad_bc, precision=PRECISE, preferred_element_type=jnp.float32)
        g_query = jnp.dot(norm_one.T, grad_query, preferred_element_type=jnp.float32)
        g_pair = jnp.dot(norm_one.T, grad_pair, preferred_element_type=jnp.float32)
        grad_norm_one = jnp.dot(grad_inner, w_inner.T, preferred_element_type=jnp.float32)
        grad_norm_one = grad_norm_one + jnp.dot(grad_step, dt_proj.T, preferred_element_type=jnp.float32)
        grad_norm_one = grad_norm_one + jnp.dot(grad_query, query_proj.T, preferred_element_type=jnp.float32)
        grad_norm_one = grad_norm_one + jnp.dot(grad_pair, w_pair.T, preferred_element_type=jnp.float32)
        grad_norm_one = grad_norm_one + jnp.dot(grad_bc, w_state.T, precision=PRECISE, preferred_element_type=jnp.float32)
        grad_res_one, g_gain_mix = rms_backward(grad_norm_one, normed_one, scale_one, gain_mix)
        input_rows = grad_residual + grad_res_one
        group_grads = (jnp.stack([g_gain_mix, g_gain_mlp], axis=0), g_inner, g_dt, g_state, g_taps, g_cbias, g_normgain, g_head, g_query, g_pair, g_attnout, g_mambaout, g_mlpin, g_mlpout)
        new_sums = tuple((total + part for total, part in zip(grad_sums, group_grads)))
        return (new_sums, (output_rows, input_rows))
    start_sums = (jnp.zeros((2, D), jnp.float32), jnp.zeros((D, 2 * chan_x), jnp.float32), jnp.zeros((D, MH), jnp.float32), jnp.zeros((D, 2 * NSTATE), jnp.float32), jnp.zeros((KCONV, chan_x + 2 * NSTATE), jnp.float32), jnp.zeros((chan_x + 2 * NSTATE,), jnp.float32), jnp.zeros((chan_x,), jnp.float32), jnp.zeros((3, MH), jnp.float32), jnp.zeros((D, QH * HDIM), jnp.float32), jnp.zeros((D, 2 * KVH * HDIM), jnp.float32), jnp.zeros((QH * HDIM, D), jnp.float32), jnp.zeros((chan_x, D), jnp.float32), jnp.zeros((D, 2 * FF), jnp.float32), jnp.zeros((FF, D), jnp.float32))
    group_items = (inputs.reshape(N_FSDP, GROUP, D), seq_lengths, out_grad.reshape(N_FSDP, GROUP, D))
    grad_sums, rows_out = lax.scan(group_pass, start_sums, group_items)
    chan_grad, conv_grad = pack_chan_grads(grad_sums[4], grad_sums[5], grad_sums[6], MH)
    return (rows_out[0].reshape(TOKENS, D), rows_out[1].reshape(TOKENS, D), grad_sums[0], grad_sums[1].reshape(D, 2, chan_x), grad_sums[2], grad_sums[3], chan_grad, conv_grad, grad_sums[7], grad_sums[8], grad_sums[9].reshape(D, 2, KVH * HDIM), grad_sums[10], grad_sums[11], grad_sums[12].reshape(D, 2, FF), grad_sums[13])
```

```python
import jax
import jax.numpy as jnp
from jax import lax
from jax.sharding import PartitionSpec as P

HDIM = 64
NSTATE = 128
KCONV = 4
NORM_EPS = 1e-05
ROPE_BASE = 100000000000.0
EXACT = lax.Precision.HIGHEST
BF = jnp.bfloat16
F32 = jnp.float32


def swap_pair(block):
    return lax.ppermute(block, "tensor", [(0, 1), (1, 0)])


def join_pair(own, other, place, axis):
    low = jnp.where(place == 0, own, other)
    high = jnp.where(place == 0, other, own)
    return jnp.stack([low, high], axis=axis)


def exchange(blocks, axis):
    return lax.all_to_all(blocks, axis, 0, 0, tiled=True)


def spread(block, axis):
    return exchange(jnp.broadcast_to(block[None], (lax.axis_size(axis),) + block.shape), axis)


def hops(axis):
    count = lax.axis_size(axis)
    place = lax.axis_index(axis)
    for step in range(1, count):
        route = [(i, (i + step) % count) for i in range(count)]
        yield route, (place + step) % count, (place - step) % count


def spread_async(block, axis):
    count = lax.axis_size(axis)
    whole = jnp.zeros((count,) + block.shape, block.dtype)
    whole = lax.dynamic_update_index_in_dim(whole, block, lax.axis_index(axis), 0)
    for route, _, source in hops(axis):
        whole = lax.dynamic_update_index_in_dim(whole, lax.ppermute(block, axis, route), source, 0)
    return whole


def reduce_async(blocks, axis):
    total = lax.dynamic_index_in_dim(blocks, lax.axis_index(axis), 0, False).astype(F32)
    for route, target, _ in hops(axis):
        sent = lax.dynamic_index_in_dim(blocks, target, 0, False)
        total = total + lax.ppermute(sent, axis, route).astype(F32)
    return total


def sigmoid(values):
    return 1.0 / (1.0 + jnp.exp(-values))


def silu_grad(values, sigma):
    return sigma * (1.0 + values * (1.0 - sigma))


def rms_forward(values):
    inv_rms = lax.rsqrt(jnp.mean(values * values, axis=-1, keepdims=True) + NORM_EPS)
    return values * inv_rms, inv_rms


def rms_backward(grad_out, normed, inv_rms, gain_vec):
    grad_normed = grad_out * gain_vec[None, :]
    return inv_rms * (grad_normed - normed * jnp.mean(grad_normed * normed, axis=-1, keepdims=True))


def rotate_half(values):
    width = values.shape[-1] // 2
    return jnp.concatenate([-values[..., width:], values[..., :width]], axis=-1)


def dot(left, right, exact=None):
    return lax.dot_general(
        left, right, (((1,), (0,)), ((), ())), precision=exact, preferred_element_type=F32
    )


def dot_nt(left, right, exact=None):
    return lax.dot_general(
        left, right, (((1,), (1,)), ((), ())), precision=exact, preferred_element_type=F32
    )


def dot_tn(left, right, exact=None):
    return lax.dot_general(
        left, right, (((0,), (0,)), ((), ())), precision=exact, preferred_element_type=F32
    )


def pad_to(array, axis, size):
    if array.shape[axis] == size:
        return array
    widths = [(0, 0)] * array.ndim
    widths[axis] = (0, size - array.shape[axis])
    return jnp.pad(array, widths)


def ceil_to(value, unit):
    return -(-value // unit) * unit


def per_device(
    inputs,
    seq_lengths,
    norm_gains,
    mamba_in,
    dt_proj,
    bc_proj,
    mamba_chan,
    bc_conv,
    head_params,
    query_proj,
    kv_proj,
    attn_out,
    mamba_out,
    mlp_in,
    mlp_out,
    out_grad,
):
    n_f = lax.axis_size("fsdp")
    n_c = lax.axis_size("context")
    c_id = lax.axis_index("context")
    t_id = lax.axis_index("tensor")
    shards = n_f * n_c
    rows = inputs.shape[0]
    group = rows * n_c
    half = rows // 2
    d_loc = mamba_in.shape[0]
    width = d_loc * shards
    heads_t = head_params.shape[1]
    heads = -(-heads_t // n_c)
    heads_pad = heads * n_c
    q_t = query_proj.shape[1] // HDIM
    qh = -(-q_t // n_c)
    q_pad = qh * n_c
    kv_w = kv_proj.shape[2]
    ff = mlp_in.shape[2]
    chan = heads * HDIM
    chan_total = heads_t * HDIM * 2
    q_w = qh * HDIM
    bc_w = 2 * NSTATE
    conv_w = chan + bc_w
    o_x = chan
    o_q = chan + conv_w
    o_k = o_q + q_w
    o_v = o_k + kv_w
    o_dt = o_v + kv_w
    a_w = ceil_to(o_dt + heads, 128)
    cc = bc_conv.shape[1]
    mc = mamba_chan.shape[1]

    chan_ctx = pad_to(mamba_chan, 0, heads_pad).reshape(n_c, heads * mc)
    common = jnp.concatenate([norm_gains.reshape(-1), bc_conv.reshape(-1)])
    small = jnp.concatenate(
        [jnp.broadcast_to(common[None], (n_c,) + common.shape), chan_ctx], axis=1
    )
    s_len = small.shape[1]
    small = pad_to(small, 1, ceil_to(s_len, 128))
    small = exchange(small, "context")
    small = spread(small, "fsdp").reshape(shards, -1).astype(F32)
    n_gain = 2 * d_loc
    n_conv = (KCONV + 1) * cc
    gains = jnp.transpose(small[:, :n_gain].reshape(shards, 2, d_loc), (1, 0, 2)).reshape(2, width)
    conv_bc = jnp.transpose(
        small[:, n_gain : n_gain + n_conv].reshape(shards, KCONV + 1, cc), (1, 0, 2)
    ).reshape(KCONV + 1, bc_w)
    chan_all = jnp.transpose(
        small[:, n_gain + n_conv : s_len].reshape(shards, heads, mc), (1, 0, 2)
    ).reshape(heads, KCONV + 2, HDIM)
    chan_all = jnp.transpose(chan_all, (1, 0, 2)).reshape(KCONV + 2, chan)
    gain_mix = gains[0]
    gain_mlp = gains[1]
    conv_all = jnp.concatenate([chan_all[: KCONV + 1], conv_bc], axis=1)
    norm_gain = chan_all[KCONV + 1]

    inner_ctx = pad_to(mamba_in.reshape(d_loc, 2, heads_t, HDIM), 2, heads_pad)
    inner_ctx = jnp.transpose(inner_ctx.reshape(d_loc, 2, n_c, chan), (2, 0, 1, 3))
    query_ctx = jnp.transpose(
        pad_to(query_proj, 1, q_pad * HDIM).reshape(d_loc, n_c, q_w), (1, 0, 2)
    )
    dt_ctx = jnp.transpose(pad_to(dt_proj, 1, heads_pad).reshape(d_loc, n_c, heads), (1, 0, 2))
    bc_ctx = jnp.broadcast_to(bc_proj[None], (n_c, d_loc, bc_w))
    kv_ctx = jnp.broadcast_to(kv_proj.reshape(1, d_loc, 2 * kv_w), (n_c, d_loc, 2 * kv_w))
    pack_a = pad_to(
        jnp.concatenate(
            [inner_ctx.reshape(n_c, d_loc, 2 * chan), bc_ctx, query_ctx, kv_ctx, dt_ctx], axis=2
        ),
        2,
        a_w,
    )
    mo_ctx = jnp.swapaxes(pad_to(mamba_out, 0, heads_pad * HDIM).reshape(n_c, chan, d_loc), 1, 2)
    ao_ctx = jnp.swapaxes(pad_to(attn_out, 0, q_pad * HDIM).reshape(n_c, q_w, d_loc), 1, 2)
    pack_b = jnp.concatenate([mo_ctx, ao_ctx], axis=2)
    b_w = chan + q_w

    mine = lax.dynamic_slice_in_dim(inputs, t_id * half, half, 0)

    part_a = exchange(pack_a, "context").reshape(n_c * d_loc, a_w)
    w_a = spread(part_a, "fsdp").reshape(width, a_w)
    got_in = exchange(jnp.broadcast_to(mine[None], (n_c,) + mine.shape), "context")
    rows_in = join_pair(got_in, swap_pair(got_in), t_id, 1).reshape(group, width)
    part_b = exchange(pack_b, "context").reshape(n_c * d_loc, b_w)
    w_b = spread(part_b, "fsdp").reshape(width, b_w)

    mlp_in_flat = mlp_in.reshape(d_loc, 2 * ff)
    mlp_out_t = mlp_out.T
    mlp_in_flat, mlp_out_t, _ = lax.optimization_barrier((mlp_in_flat, mlp_out_t, part_b))
    mlp_in_part = spread_async(mlp_in_flat, "context").reshape(n_c * d_loc, 2 * ff)
    mlp_out_part = spread_async(mlp_out_t, "context").reshape(n_c * d_loc, ff)
    w_mi = spread_async(mlp_in_part, "fsdp").reshape(width, 2 * ff)
    w_mo = spread_async(mlp_out_part, "fsdp").reshape(width, ff)

    lengths_row = seq_lengths[0]
    starts = jnp.cumsum(lengths_row) - lengths_row
    row_ids = jnp.arange(group, dtype=jnp.int32)
    inside = row_ids[:, None] >= starts[None, :]
    seq_ids = jnp.sum(inside.astype(jnp.int32), axis=1) - 1
    positions = row_ids - jnp.max(jnp.where(inside, starts[None, :], 0), axis=1)
    linked = (seq_ids[:, None] == seq_ids[None, :]) & (row_ids[:, None] >= row_ids[None, :])

    head_vec = lax.dynamic_slice_in_dim(
        pad_to(head_params, 1, heads_pad), c_id * heads, heads, 1
    )

    normed_one = rms_forward(rows_in.astype(F32))[0]
    norm_one = (normed_one * gain_mix[None, :]).astype(BF)
    proj = dot(norm_one, w_a)
    z_gate = proj[:, :chan].astype(BF).astype(F32)
    conv_in = proj[:, o_x:o_q].astype(BF).astype(F32)
    dt_raw = proj[:, o_dt : o_dt + heads]

    def behind(values, step):
        moved = jnp.pad(values, ((step, 0), (0, 0)))[:group]
        return jnp.where((positions >= step)[:, None], moved, 0.0)

    def ahead(values, step):
        kept = jnp.where((positions >= step)[:, None], values, 0.0)
        return jnp.pad(kept, ((0, step), (0, 0)))[step:]

    pre_act = conv_all[KCONV][None, :]
    for k in range(KCONV):
        pre_act = pre_act + conv_all[k][None, :] * behind(conv_in, KCONV - 1 - k)
    pre_sig = sigmoid(pre_act)
    activated = pre_act * pre_sig
    ssm_x = activated[:, :chan]
    state_b = activated[:, chan : chan + NSTATE].astype(BF)
    state_c = activated[:, chan + NSTATE :].astype(BF)
    dt_step = jax.nn.softplus(dt_raw + head_vec[0][None, :])
    rate = jnp.exp(head_vec[1])[None, :]
    decay_log = -dt_step * rate
    lower = (row_ids[:, None] >= row_ids[None, :]).astype(F32)
    log_cum = dot(lower, decay_log, EXACT)
    cum_t = log_cum.T
    dt_t = dt_step.T
    c_dot_b = dot_nt(state_c, state_b)
    ssm_list = []
    for j in range(heads):
        gaps = jnp.where(linked, log_cum[:, j : j + 1] - cum_t[j : j + 1], -1e30)
        mixing = jnp.exp(gaps) * c_dot_b * dt_t[j : j + 1]
        x_head = ssm_x[:, j * HDIM : (j + 1) * HDIM]
        core = dot(mixing.astype(BF), x_head.astype(BF))
        ssm_list.append(core + head_vec[2, j] * x_head)
    ssm_out = jnp.concatenate(ssm_list, axis=1)
    z_sig = sigmoid(z_gate)
    silu_z = z_gate * z_sig
    gated = ssm_out * silu_z
    squares = jnp.sum(gated * gated, axis=1).reshape(n_c, rows)
    norm_in = (gated * norm_gain[None, :]).astype(BF)
    mamba_part = dot_nt(norm_in, w_b[:, :chan])

    freqs = jnp.power(ROPE_BASE, -jnp.arange(HDIM // 2).astype(F32) * (2.0 / HDIM))
    angles = positions.astype(F32)[:, None] * freqs[None, :]
    angles = jnp.concatenate([angles, angles], axis=1)
    cosine = jnp.cos(angles)
    sine = jnp.sin(angles)
    scale = HDIM ** (-0.5)
    k_raw = proj[:, o_k : o_k + HDIM]
    k_rot = (k_raw * cosine + rotate_half(k_raw) * sine).astype(BF)
    v_rows = proj[:, o_v : o_v + HDIM].astype(BF)
    q_list = []
    val_list = []
    prob_list = []
    for j in range(qh):
        q_raw = proj[:, o_q + j * HDIM : o_q + (j + 1) * HDIM]
        q_rot = (q_raw * cosine + rotate_half(q_raw) * sine).astype(BF)
        scores = jnp.where(linked, dot_nt(q_rot, k_rot) * scale, -1e30)
        exps = jnp.exp(scores - jnp.max(scores, axis=1, keepdims=True))
        probs = exps / jnp.sum(exps, axis=1, keepdims=True)
        probs_round = probs.astype(BF)
        q_list.append(q_rot)
        prob_list.append(probs_round)
        val_list.append(dot(probs_round, v_rows).astype(BF))
    attn_flat = jnp.concatenate(val_list, axis=1)
    attn_part = dot_nt(attn_flat, w_b[:, chan:])

    def pair_sum(values, lead):
        parts = values.reshape(lead + (2, half) + values.shape[1:])
        axis = len(lead)
        keep = lax.dynamic_index_in_dim(parts, t_id, axis, False)
        give = lax.dynamic_index_in_dim(parts, 1 - t_id, axis, False).astype(BF)
        return keep + swap_pair(give).astype(F32)

    both = jnp.concatenate([mamba_part, attn_part], axis=1)
    both = pair_sum(both, (n_c,)).astype(BF)
    both = jnp.sum(exchange(both, "context").astype(F32), axis=0)
    squares = squares + swap_pair(squares)
    squares = jnp.sum(spread(squares, "context"), axis=0)
    scale_rows = lax.rsqrt(squares / chan_total + NORM_EPS)
    scale_own = lax.dynamic_slice(scale_rows, (c_id, t_id * half), (1, half)).reshape(half, 1)
    scale_all = scale_rows.reshape(group, 1)
    mamba_own = both[:, :width]
    in_own = mine.astype(F32)
    residual = in_own + scale_own * mamba_own + both[:, width:]

    normed_two, inv_two = rms_forward(residual)
    norm_two_own = (normed_two * gain_mlp[None, :]).astype(BF)
    norm_two = join_pair(norm_two_own, swap_pair(norm_two_own), t_id, 0).reshape(rows, width)
    up_gate = dot(norm_two, w_mi)
    gate_val = up_gate[:, :ff]
    up_val = up_gate[:, ff:]
    gate_sig = sigmoid(gate_val)
    gate_act = gate_val * gate_sig
    mlp_act = (gate_act * up_val).astype(BF)
    grad_act = dot(out_grad, w_mo)
    grad_gate = (grad_act * up_val * silu_grad(gate_val, gate_sig)).astype(BF)
    grad_up = (grad_act * gate_act).astype(BF)
    grad_upgate = jnp.concatenate([grad_gate, grad_up], axis=1)
    grad_two = pair_sum(dot_nt(grad_upgate, w_mi), ())
    down_own = pair_sum(dot_nt(mlp_act, w_mo), ())
    out_own = (residual + down_own).astype(BF)
    output = join_pair(out_own, swap_pair(out_own), t_id, 0).reshape(rows, width)
    g_mi = dot_tn(norm_two, grad_upgate).astype(BF)
    g_mo = dot_tn(out_grad, mlp_act).astype(BF)

    top_own = lax.dynamic_slice_in_dim(out_grad, t_id * half, half, 0).astype(F32)
    g_gain_mlp = jnp.sum(grad_two * normed_two, axis=0)
    grad_res = top_own + rms_backward(grad_two, normed_two, inv_two, gain_mlp)
    grad_rs_own = jnp.sum(grad_res * mamba_own, axis=1)
    got_rs = spread(grad_rs_own.reshape(1, half), "context")
    grad_rs = join_pair(got_rs, swap_pair(got_rs), t_id, 1).reshape(group, 1)
    got_res = exchange(
        jnp.broadcast_to(grad_res.astype(BF)[None], (n_c, half, width)), "context"
    )
    grad_round = join_pair(got_res, swap_pair(got_res), t_id, 1).reshape(group, width)
    grad_scaled = (grad_round.astype(F32) * scale_all).astype(BF)

    def reduce_weight(grad, use):
        cols = grad.shape[1]
        blocks = grad.reshape(n_f, n_c * d_loc, cols)
        return use(blocks, "fsdp").astype(BF).reshape(n_c, d_loc, cols)

    def sum_exchange(blocks, axis):
        return jnp.sum(exchange(blocks, axis).astype(F32), axis=0)

    g_mi, g_mo, grad_round = lax.optimization_barrier((g_mi, g_mo, grad_round))
    out_mi = reduce_async(reduce_weight(g_mi, reduce_async), "context").reshape(d_loc, 2, ff)
    out_mo = reduce_async(reduce_weight(g_mo, reduce_async), "context").T

    g_b = jnp.concatenate([dot_tn(grad_scaled, norm_in), dot_tn(grad_round, attn_flat)], axis=1)
    g_b = reduce_weight(g_b.astype(BF), sum_exchange)
    g_b = exchange(g_b, "context").astype(F32)
    out_mout = jnp.swapaxes(g_b[:, :, :chan], 1, 2).reshape(heads_pad * HDIM, d_loc)
    out_mout = out_mout[: heads_t * HDIM]
    out_aout = jnp.swapaxes(g_b[:, :, chan:], 1, 2).reshape(q_pad * HDIM, d_loc)
    out_aout = out_aout[: q_t * HDIM]

    grad_attn = dot(grad_round, w_b[:, chan:])
    grad_k = jnp.zeros((group, HDIM), F32)
    grad_v = jnp.zeros((group, HDIM), F32)
    grad_q_list = []
    for j in range(qh):
        part = slice(j * HDIM, (j + 1) * HDIM)
        g_attn = grad_attn[:, part]
        delta = jnp.sum(g_attn * val_list[j].astype(F32), axis=1, keepdims=True)
        g_attn = g_attn.astype(BF)
        grad_prob = dot_nt(g_attn, v_rows)
        g_scores = (prob_list[j].astype(F32) * (grad_prob - delta)).astype(BF)
        g_q = dot(g_scores, k_rot) * scale
        grad_k = grad_k + dot_tn(g_scores, q_list[j]) * scale
        grad_v = grad_v + dot_tn(prob_list[j], g_attn)
        grad_q_list.append((g_q * cosine - rotate_half(g_q) * sine).astype(BF))
    grad_k = (grad_k * cosine - rotate_half(grad_k) * sine).astype(BF)
    grad_v = grad_v.astype(BF)

    grad_norm_in = dot(grad_scaled, w_b[:, :chan])
    g_norm_gain = jnp.sum(grad_norm_in * gated, axis=0)
    grad_gated = grad_norm_in * norm_gain[None, :] - gated * (
        grad_rs * scale_all * scale_all * scale_all / chan_total
    )
    grad_ssm = grad_gated * silu_z
    grad_z = (grad_gated * ssm_out * silu_grad(z_gate, z_sig)).astype(BF)

    grad_cb = jnp.zeros((group, group), F32)
    grad_x_list = []
    row_list = []
    col_list = []
    skip_list = []
    for j in range(heads):
        part = slice(j * HDIM, (j + 1) * HDIM)
        gaps = jnp.where(linked, log_cum[:, j : j + 1] - cum_t[j : j + 1], -1e30)
        decays = jnp.exp(gaps)
        weights = decays * c_dot_b
        x_head = ssm_x[:, part]
        g_head = grad_ssm[:, part]
        g_round = g_head.astype(BF)
        grad_mix = dot_nt(g_round, x_head.astype(BF))
        grad_x_list.append(
            dot_tn((weights * dt_t[j : j + 1]).astype(BF), g_round) + head_vec[2, j] * g_head
        )
        grad_cb = grad_cb + grad_mix * decays * dt_t[j : j + 1]
        flow = grad_mix * weights
        col_list.append(jnp.sum(flow, axis=0))
        row_list.append(jnp.sum(flow * dt_t[j : j + 1], axis=1))
        skip_list.append(jnp.sum(g_head * x_head))
    grad_cb = grad_cb.astype(BF)
    grad_c = dot(grad_cb, state_b)
    grad_b = dot_tn(grad_cb, state_c)
    col_sum = jnp.stack(col_list, axis=1)
    grad_cum = jnp.stack(row_list, axis=1) - dt_step * col_sum
    grad_decay = dot_tn(lower, grad_cum, EXACT)
    grad_dt = col_sum - rate * grad_decay
    grad_dt_raw = grad_dt * sigmoid(dt_raw + head_vec[0][None, :])
    g_head_params = jnp.stack(
        [
            jnp.sum(grad_dt_raw, axis=0),
            jnp.sum(grad_decay * decay_log, axis=0),
            jnp.stack(skip_list),
        ]
    )

    grad_act_mix = jnp.concatenate(grad_x_list + [grad_b, grad_c], axis=1)
    grad_pre = grad_act_mix * silu_grad(pre_act, pre_sig)
    grad_conv = jnp.zeros_like(grad_pre)
    g_taps = []
    for k in range(KCONV):
        step = KCONV - 1 - k
        g_taps.append(jnp.sum(grad_pre * behind(conv_in, step), axis=0))
        grad_conv = grad_conv + conv_all[k][None, :] * ahead(grad_pre, step)
    g_taps.append(jnp.sum(grad_pre, axis=0))
    g_taps = jnp.stack(g_taps)

    grad_a = pad_to(
        jnp.concatenate(
            [grad_z, grad_conv.astype(BF)]
            + grad_q_list
            + [pad_to(grad_k, 1, kv_w), pad_to(grad_v, 1, kv_w), grad_dt_raw.astype(BF)],
            axis=1,
        ),
        1,
        a_w,
    )
    partial = dot_nt(grad_a, w_a)
    g_gain_mix = jnp.sum(partial * normed_one, axis=0)
    partial = pair_sum(partial, (n_c,)).astype(BF)
    grad_one = jnp.sum(exchange(partial, "context").astype(F32), axis=0)
    normed_own, inv_own = rms_forward(in_own)
    grad_in_own = grad_res + rms_backward(grad_one, normed_own, inv_own, gain_mix)
    input_grad = join_pair(grad_in_own, swap_pair(grad_in_own), t_id, 0).reshape(rows, width)

    g_a = reduce_weight(dot_tn(norm_one, grad_a).astype(BF), sum_exchange)
    g_a = exchange(g_a, "context").astype(F32)
    out_inner = jnp.transpose(g_a[:, :, : 2 * chan].reshape(n_c, d_loc, 2, chan), (1, 2, 0, 3))
    out_inner = out_inner.reshape(d_loc, 2, heads_pad * HDIM)[:, :, : heads_t * HDIM]
    out_query = jnp.swapaxes(g_a[:, :, o_q:o_k], 0, 1).reshape(d_loc, q_pad * HDIM)
    out_query = out_query[:, : q_t * HDIM]
    out_dt = jnp.swapaxes(g_a[:, :, o_dt : o_dt + heads], 0, 1).reshape(d_loc, heads_pad)
    out_dt = out_dt[:, :heads_t]
    out_kv = jnp.sum(g_a[:, :, o_k:o_dt], axis=0).reshape(d_loc, 2, kv_w)
    sum_bc = jnp.sum(g_a[:, :, o_x + chan : o_q], axis=0)

    g_gains = jnp.stack([g_gain_mix, g_gain_mlp]).reshape(2, shards, d_loc)
    g_gains = jnp.transpose(g_gains, (1, 0, 2)).reshape(shards, n_gain)
    g_convbc = jnp.transpose(
        g_taps[:, chan:].reshape(KCONV + 1, shards, cc), (1, 0, 2)
    ).reshape(shards, n_conv)
    g_chan = jnp.concatenate([g_taps[:, :chan], g_norm_gain[None]], axis=0)
    g_chan = jnp.transpose(g_chan.reshape(KCONV + 2, heads, HDIM), (1, 0, 2))
    g_chan = jnp.transpose(g_chan.reshape(heads, shards, mc), (1, 0, 2)).reshape(shards, heads * mc)
    g_heads = jnp.broadcast_to(g_head_params.reshape(1, -1), (shards, 3 * heads))
    g_small = jnp.concatenate([g_gains, g_convbc, g_chan, g_heads], axis=1)
    g_len = g_small.shape[1]
    g_small = pad_to(g_small, 1, ceil_to(g_len, 128)).reshape(n_f, n_c, -1)
    g_small = jnp.sum(exchange(g_small, "fsdp"), axis=0)
    g_small = exchange(g_small, "context")
    g_common = jnp.sum(g_small[:, : n_gain + n_conv], axis=0)
    tail = jnp.concatenate([sum_bc.reshape(-1), g_common])
    tail = tail + swap_pair(tail)
    out_bc = tail[: d_loc * bc_w].reshape(d_loc, bc_w)
    g_common = tail[d_loc * bc_w :]
    out_gains = g_common[:n_gain].reshape(2, d_loc)
    out_convbc = g_common[n_gain:].reshape(KCONV + 1, cc)
    out_chan = g_small[:, n_gain + n_conv : n_gain + n_conv + heads * mc]
    out_chan = out_chan.reshape(heads_pad, mc)[:heads_t]
    out_heads = g_small[:, n_gain + n_conv + heads * mc : g_len].reshape(n_c, 3, heads)
    out_heads = jnp.swapaxes(out_heads, 0, 1).reshape(3, heads_pad)[:, :heads_t]

    return (
        output,
        input_grad,
        out_gains,
        out_inner,
        out_dt,
        out_bc,
        out_chan,
        out_convbc,
        out_heads,
        out_query,
        out_kv,
        out_aout,
        out_mout,
        out_mi,
        out_mo,
    )


def solution(mesh):
    both = ("fsdp", "context")
    rows = P(both, None)
    return jax.shard_map(
        per_device,
        mesh=mesh,
        in_specs=(
            rows,
            P("fsdp", None),
            P(None, both),
            P(both, None, "tensor"),
            P(both, "tensor"),
            rows,
            P("tensor", both),
            P(None, both),
            P(None, "tensor"),
            P(both, "tensor"),
            P(both, None, "tensor"),
            P("tensor", both),
            P("tensor", both),
            P(both, None, "tensor"),
            P("tensor", both),
            rows,
        ),
        out_specs=(
            rows,
            rows,
            P(None, both),
            P(both, None, "tensor"),
            P(both, "tensor"),
            rows,
            P("tensor", both),
            P(None, both),
            P(None, "tensor"),
            P(both, "tensor"),
            P(both, None, "tensor"),
            P("tensor", both),
            P("tensor", both),
            P(both, None, "tensor"),
            P("tensor", both),
        ),
        check_vma=False,
    )
```

```python
import jax
import jax.numpy as jnp
from jax import lax
from jax.experimental import pallas as pl
from jax.experimental.pallas import tpu as pltpu
from jax.sharding import PartitionSpec as P


HDIM = 64
NSTATE = 128
KCONV = 4
NORM_EPS = 1e-05
ROPE_BASE = 100000000000.0
EXACT = lax.Precision.HIGHEST
BF = jnp.bfloat16
F32 = jnp.float32


def swap_pair(block):
    return lax.ppermute(block, "tensor", [(0, 1), (1, 0)])


def join_pair(own, other, place, axis):
    low = jnp.where(place == 0, own, other)
    high = jnp.where(place == 0, other, own)
    return jnp.stack([low, high], axis=axis)


def exchange(blocks, axis):
    return lax.all_to_all(blocks, axis, 0, 0, tiled=True)


def spread(block, axis):
    return exchange(jnp.broadcast_to(block[None], (lax.axis_size(axis),) + block.shape), axis)


def hops(axis):
    count = lax.axis_size(axis)
    place = lax.axis_index(axis)
    for step in range(1, count):
        route = [(i, (i + step) % count) for i in range(count)]
        yield route, (place + step) % count, (place - step) % count


def spread_async(block, axis):
    count = lax.axis_size(axis)
    got = [(lax.ppermute(block, axis, route), source) for route, _, source in hops(axis)]
    whole = jnp.zeros((count,) + block.shape, block.dtype)
    whole = lax.dynamic_update_index_in_dim(whole, block, lax.axis_index(axis), 0)
    for piece, source in got:
        whole = lax.dynamic_update_index_in_dim(whole, piece, source, 0)
    return whole


def reduce_async(blocks, axis):
    got = [
        lax.ppermute(lax.dynamic_index_in_dim(blocks, target, 0, False), axis, route)
        for route, target, _ in hops(axis)
    ]
    total = lax.dynamic_index_in_dim(blocks, lax.axis_index(axis), 0, False).astype(F32)
    for piece in got:
        total = total + piece.astype(F32)
    return total


def beside(step):
    return [(i, i ^ step) for i in range(4)]


def plane_gather(block):
    if lax.axis_size("fsdp") != 4:
        return spread_async(block, "fsdp")
    half = block.shape[0] // 2
    place = lax.axis_index("fsdp")
    near = lax.ppermute(block, "fsdp", beside(1))
    side = lax.ppermute(block, "fsdp", beside(2))
    far_top = lax.ppermute(side[:half], "fsdp", beside(1))
    far_low = lax.ppermute(near[half:], "fsdp", beside(2))
    whole = jnp.zeros((4, 2, half) + block.shape[1:], block.dtype)
    parts = ((block, place), (near, place ^ 1), (side, place ^ 2))
    for piece, index in parts:
        piece = piece.reshape((1, 2, half) + block.shape[1:])
        whole = lax.dynamic_update_slice(whole, piece, (index, 0, 0, 0))
    for row, piece in enumerate((far_top, far_low)):
        whole = lax.dynamic_update_slice(whole, piece[None, None], (place ^ 3, row, 0, 0))
    return whole


def plane_reduce(make):
    if lax.axis_size("fsdp") != 4:
        sent = [(route, make(target).astype(BF)) for route, target, _ in hops("fsdp")]
        own = make(lax.axis_index("fsdp"))
        for route, piece in sent:
            own = own + lax.ppermute(piece, "fsdp", route).astype(F32)
        return own
    place = lax.axis_index("fsdp")
    far = make(place ^ 3).astype(BF)
    half = far.shape[0] // 2
    got_side = lax.ppermute(far[:half], "fsdp", beside(1))
    got_near = lax.ppermute(far[half:], "fsdp", beside(2))
    near = make(place ^ 1)
    side = make(place ^ 2)
    near_top = lax.ppermute(near[:half].astype(BF), "fsdp", beside(1))
    side_low = lax.ppermute(side[half:].astype(BF), "fsdp", beside(2))
    own = make(place)
    near_low = (near[half:] + got_near.astype(F32)).astype(BF)
    side_top = (side[:half] + got_side.astype(F32)).astype(BF)
    near_low = lax.ppermute(near_low, "fsdp", beside(1))
    side_top = lax.ppermute(side_top, "fsdp", beside(2))
    top = own[:half] + near_top.astype(F32) + side_top.astype(F32)
    low = own[half:] + near_low.astype(F32) + side_low.astype(F32)
    return jnp.concatenate([top, low], axis=0).astype(BF)


def sigmoid(values):
    return 1.0 / (1.0 + jnp.exp(-values))


def silu_grad(values, sigma):
    return sigma * (1.0 + values * (1.0 - sigma))


def rms_forward(values):
    inv_rms = lax.rsqrt(jnp.mean(values * values, axis=-1, keepdims=True) + NORM_EPS)
    return values * inv_rms, inv_rms


def rms_backward(grad_out, normed, inv_rms, gain_vec):
    grad_normed = grad_out * gain_vec[None, :]
    return inv_rms * (grad_normed - normed * jnp.mean(grad_normed * normed, axis=-1, keepdims=True))


def dot(left, right, exact=None):
    return lax.dot_general(
        left, right, (((1,), (0,)), ((), ())), precision=exact, preferred_element_type=F32
    )


def dot_nt(left, right, exact=None):
    return lax.dot_general(
        left, right, (((1,), (1,)), ((), ())), precision=exact, preferred_element_type=F32
    )


def dot_tn(left, right, exact=None):
    return lax.dot_general(
        left, right, (((0,), (0,)), ((), ())), precision=exact, preferred_element_type=F32
    )


def pad_to(array, axis, size):
    if array.shape[axis] == size:
        return array
    widths = [(0, 0)] * array.ndim
    widths[axis] = (0, size - array.shape[axis])
    return jnp.pad(array, widths)


def ceil_to(value, unit):
    return -(-value // unit) * unit


def split(values, pieces, wide=True):
    parts = []
    for _ in range(pieces):
        high = lax.reduce_precision(values, 8, 7)
        parts.append(high.astype(BF))
        values = values - high
    joined = jnp.concatenate(parts, axis=-1)
    return pad_to(joined, joined.ndim - 1, 128) if wide else joined


def fuse(values, pieces, count):
    values = values.astype(F32)
    total = values[..., :count]
    for i in range(1, pieces):
        total = total + values[..., i * count : (i + 1) * count]
    return total


class Plan:
    def __init__(self, group, rows, width, d_loc, heads, total, cc, mc):
        self.group, self.rows, self.width, self.d_loc = group, rows, width, d_loc
        self.heads, self.total, self.cc, self.mc = heads, total, cc, mc
        self.half = rows // 2
        self.chan = heads * HDIM
        self.wide = ceil_to(self.chan, 128)
        self.off = self.chan % 128
        self.conv = 2 * NSTATE + self.wide
        self.o_x = 2 * NSTATE
        self.o_v = self.o_x + self.chan
        self.o_z = ceil_to(self.o_v + HDIM, 128)
        self.o_dt = self.o_z + self.chan
        self.o_s = self.o_dt + heads
        self.n_small = KCONV + 4 + heads
        self.o_end = self.o_s + 2 * self.n_small
        self.o_q = ceil_to(self.o_end, 128)
        self.o_k = self.o_q + HDIM
        self.a_w = self.o_q + 2 * HDIM
        self.o_mo = self.a_w
        self.o_ao = self.a_w + self.chan
        self.p_w = ceil_to(self.o_ao + HDIM, 128)
        self.s_v = self.o_v - self.off
        self.s_dt = self.o_dt - self.off
        self.s_ao = self.o_ao - self.off
        self.row = self.off + heads


def lanes(count):
    return lax.broadcasted_iota(jnp.int32, (1, count), 1)


def first_rows(lengths_ref, index):
    start = jnp.zeros_like(index)
    edge = jnp.int32(0)
    for i in range(lengths_ref.shape[1] - 1):
        edge = edge + lengths_ref[0, i]
        start = jnp.where(index >= edge, edge, start)
    return start


def head_row(plan, head_ref, which):
    lane = lanes(128)
    row = jnp.zeros((1, 128), F32)
    for j in range(plan.heads):
        row = jnp.where(lane == plan.off + j, head_ref[which, j], row)
    return row


def head_wide(plan, values):
    lane = lanes(plan.wide)
    row = jnp.zeros((1, plan.wide), F32)
    for j in range(plan.heads):
        row = jnp.where(lane // HDIM == j, values[j], row)
    return row


def steps_of(plan, head_ref, slab):
    lane = lanes(128)
    live = (lane >= plan.off) & (lane < plan.row)
    shifted = jnp.where(live, slab + head_row(plan, head_ref, 0), 0.0)
    soft = jnp.maximum(shifted, 0.0) + jnp.log1p(jnp.exp(-jnp.abs(shifted)))
    dt_step = jnp.where(live, soft, 0.0)
    rate = jnp.where(live, jnp.exp(head_row(plan, head_ref, 1)), 0.0)
    return dt_step, rate, shifted, live


def small_rows(plan, w_ref, sel_ref):
    slab = w_ref[:, plan.s_dt : plan.s_dt + 128]
    turned = slab.astype(F32).T
    picked = dot_tn(slab, sel_ref[...])
    row = plan.row
    lane = lanes(plan.wide)
    taps = []
    for k in range(KCONV + 2):
        low = 2 * NSTATE + k * plan.wide
        piece = jnp.zeros((1, plan.wide), F32)
        for j in range(plan.heads):
            at = row + KCONV + 3 + j
            piece = jnp.where(lane // HDIM == j, picked[at : at + 1, low : low + plan.wide], piece)
        if k <= KCONV:
            piece = jnp.concatenate(
                [picked[row + 2 + k : row + 3 + k, : 2 * NSTATE], piece], axis=1
            )
        taps.append(piece)
    return turned[row : row + 1], turned[row + 1 : row + 2], taps


def lower_tri(group):
    return (
        lax.broadcasted_iota(jnp.int32, (group, group), 0)
        >= lax.broadcasted_iota(jnp.int32, (group, group), 1)
    ).astype(F32)


def linked_rows(plan, lengths_ref, low):
    index = lax.broadcasted_iota(jnp.int32, (plan.rows, 1), 0) + low
    start = first_rows(lengths_ref, index)
    cols = lanes(plan.group)
    return (cols <= index) & (cols >= start), index - start


def turn(values, cosine, sine):
    lane = lanes(2 * HDIM)
    moved = jnp.where(
        lane % HDIM < HDIM // 2, -pltpu.roll(values, 2 * HDIM - HDIM // 2, 1),
        pltpu.roll(values, HDIM // 2, 1),
    )
    return values * cosine + moved * sine


def split_rows(plan, values, t_id):
    low = values[: plan.half]
    high = values[plan.half :]
    return jnp.where(t_id == 0, low, high), jnp.where(t_id == 0, high, low)


def forward_kernel(
    plan, lengths_ref, head_ref, t_ref, x_ref, w_ref, sel_ref, cos_ref, sin_ref,
    keep_ref, give_ref, gain2_ref, norm_ref, proj_ref, pre_ref, cum_ref, ssm_ref, attn_ref, lse_ref, qk_ref,
    kq_ref, act_ref, ext_ref,
):
    rows, group, wide = plan.rows, plan.group, plan.wide
    gain, gain_two, taps = small_rows(plan, w_ref, sel_ref)
    gain2_ref[...] = gain_two
    blocks = group // rows
    t_id = t_ref[0]
    ext_ref[0:8, :] = jnp.zeros((8, plan.conv), F32)

    def project(b, _):
        at = pl.ds(pl.multiple_of(b * rows, rows), rows)
        values = x_ref[at, :].astype(F32)
        normed = rms_forward(values)[0]
        norm = (normed * gain).astype(BF)
        norm_ref[at, :] = norm
        proj = dot(norm, w_ref[:, : plan.a_w])
        proj_ref[at, :] = proj
        ext_ref[pl.ds(pl.multiple_of(b * rows + 8, 8), rows), :] = (
            proj[:, : plan.conv].astype(BF).astype(F32)
        )
        rot = turn(proj[:, plan.o_q :], cos_ref[at, :], sin_ref[at, :])
        qk_ref[at, :] = rot.astype(BF)
        kq_ref[at, :] = pltpu.roll(rot, HDIM, 1).astype(BF)
        return 0

    lax.fori_loop(0, blocks, project, 0)

    dt_step, rate, _, _ = steps_of(plan, head_ref, proj_ref[:, plan.s_dt : plan.s_dt + 128])
    cum = dot(lower_tri(group), -dt_step * rate, EXACT)
    cum_ref[...] = cum
    cum_t = cum.T
    dt_t = dt_step.T

    def convolve(b, _):
        low = pl.multiple_of(b * rows, rows)
        at = pl.ds(low, rows)
        pos = linked_rows(plan, lengths_ref, low)[1]
        ext = ext_ref[pl.ds(low, rows + 8), :]
        total = jnp.broadcast_to(taps[KCONV], (rows, plan.conv))
        for k in range(KCONV):
            step = KCONV - 1 - k
            total = total + taps[k] * (ext[8 - step : 8 - step + rows] * (pos >= step).astype(F32))
        pre_ref[at, :] = total
        act_ref[at, :] = (total * sigmoid(total)).astype(BF)
        return 0

    lax.fori_loop(0, blocks, convolve, 0)

    lane_w = lanes(wide)
    lane = lanes(128)
    in_v = (lane >= plan.off) & (lane < plan.off + HDIM)
    b_all = act_ref[:, :NSTATE]
    x_all = act_ref[:, plan.o_x : plan.o_x + wide]
    v_all = jnp.where(in_v, proj_ref[:, plan.s_v : plan.s_v + 128], 0.0).astype(BF)
    k_all = kq_ref[...]
    skip = head_wide(plan, [head_ref[2, j] for j in range(plan.heads)])
    w_m = w_ref[:, plan.o_mo : plan.o_mo + wide]
    w_o = w_ref[:, plan.s_ao : plan.s_ao + 128]

    def mix(b, _):
        low = pl.multiple_of(b * rows, rows)
        at = pl.ds(low, rows)
        linked = linked_rows(plan, lengths_ref, low)[0]
        cross = dot_nt(act_ref[at, NSTATE : 2 * NSTATE], b_all)
        cum_b = cum_ref[at, :]
        core = jnp.zeros((rows, wide), F32)
        for j in range(plan.heads):
            col = cum_b[:, plan.off + j : plan.off + j + 1]
            gaps = jnp.where(linked, col - cum_t[plan.off + j : plan.off + j + 1], -1e30)
            mixing = jnp.exp(gaps) * cross * dt_t[plan.off + j : plan.off + j + 1]
            core = jnp.where(lane_w // HDIM == j, dot(mixing.astype(BF), x_all), core)
        pre = pre_ref[at, plan.o_x : plan.o_x + wide]
        ssm = core + skip * (pre * sigmoid(pre))
        ssm_ref[at, :] = ssm
        z_gate = proj_ref[at, plan.o_z : plan.o_z + wide].astype(BF).astype(F32)
        gated = jnp.where(lane_w < plan.chan, ssm * (z_gate * sigmoid(z_gate)), 0.0)
        norm_in = (gated * taps[KCONV + 1]).astype(BF)
        square = jnp.sum(gated * gated, axis=1, keepdims=True)
        high = square.astype(BF).astype(F32)
        square = jnp.where(
            lane == 2 * t_id, high, jnp.where(lane == 2 * t_id + 1, square - high, 0.0)
        )

        query = jnp.where(lane < HDIM, qk_ref[at, :].astype(F32), 0.0).astype(BF)
        scores = jnp.where(linked, dot_nt(query, k_all) * HDIM ** (-0.5), -1e30)
        top = jnp.max(scores, axis=1, keepdims=True)
        exps = jnp.exp(scores - top)
        total = jnp.sum(exps, axis=1, keepdims=True)
        values = dot((exps / total).astype(BF), v_all).astype(BF)
        attn_ref[at, :] = values
        lse_ref[at, :] = jnp.broadcast_to(top + jnp.log(total), (rows, 128))

        out = pl.ds(pl.multiple_of(b * plan.half, plan.half), plan.half)
        width = plan.width
        for start, piece in (
            (0, dot_nt(norm_in, w_m)),
            (width, dot_nt(values, w_o)),
            (2 * width, square),
        ):
            keep, give = split_rows(plan, piece, t_id)
            keep_ref[out, start : start + piece.shape[1]] = keep.astype(BF)
            give_ref[out, start : start + piece.shape[1]] = give.astype(BF)
        return 0

    lax.fori_loop(0, blocks, mix, 0)


def backward_kernel(
    plan, lengths_ref, head_ref, t_ref, x_ref, w_ref, sel_ref, cos_ref, sin_ref,
    norm_ref, proj_ref, pre_ref, cum_ref, ssm_ref, attn_ref, lse_ref, qk_ref, kq_ref, got_ref,
    gain2_ref,
    keep_ref, give_ref, pack_ref,
    act_ref, ext_ref, gs_ref, ni_ref, gy_ref, ga_ref, gact_ref, gext_ref, gv_ref, gk_ref, gat_ref,
    row_ref, col_ref, dtt_ref, cumt_ref,
):
    rows, group, wide, width = plan.rows, plan.group, plan.wide, plan.width
    heads, off, row = plan.heads, plan.off, plan.row
    _, _, taps = small_rows(plan, w_ref, sel_ref)
    blocks = group // rows
    t_id = t_ref[0]
    lane_w = lanes(wide)
    lane = lanes(128)
    in_v = (lane >= off) & (lane < off + HDIM)
    norm_gain = taps[KCONV + 1]
    w_m = w_ref[:, plan.o_mo : plan.o_mo + wide]
    w_o = w_ref[:, plan.s_ao : plan.s_ao + 128]
    ext_ref[0:8, :] = jnp.zeros((8, plan.conv), F32)
    gext_ref[group : group + 8, :] = jnp.zeros((8, plan.conv), F32)
    skip = head_wide(plan, [head_ref[2, j] for j in range(heads)])
    scale = HDIM ** (-0.5)

    dt_step, rate, shifted, live = steps_of(
        plan, head_ref, proj_ref[:, plan.s_dt : plan.s_dt + 128]
    )
    dtt_ref[...] = dt_step.T
    cumt_ref[...] = cum_ref[...].T

    def gate(b, sums):
        at = pl.ds(pl.multiple_of(b * rows, rows), rows)
        grad_round = got_ref[at, :width]
        factor = got_ref[at, width : width + 128].astype(F32)
        grad_rs = factor[:, 0:1] + factor[:, 2:3]
        row_scale = factor[:, 1:2] + factor[:, 3:4]
        grad_scaled = (grad_round.astype(F32) * row_scale).astype(BF)
        gs_ref[at, :] = grad_scaled
        grad_in = jnp.where(lane_w < plan.chan, dot(grad_scaled, w_m), 0.0)
        gat_ref[at, :] = jnp.where(in_v, dot(grad_round, w_o), 0.0)
        z_gate = proj_ref[at, plan.o_z : plan.o_z + wide].astype(BF).astype(F32)
        z_gate = jnp.where(lane_w < plan.chan, z_gate, 0.0)
        z_sig = sigmoid(z_gate)
        silu_z = z_gate * z_sig
        ssm = ssm_ref[at, :]
        gated = ssm * silu_z
        ni_ref[at, :] = (gated * norm_gain).astype(BF)
        grad_gated = grad_in * norm_gain - gated * (
            grad_rs * row_scale * row_scale * row_scale / plan.total
        )
        grad_y = grad_gated * silu_z
        gy_ref[at, :] = grad_y
        grad_z = grad_gated * ssm * silu_grad(z_gate, z_sig)
        ga_ref[at, plan.o_z : plan.o_z + wide] = grad_z.astype(BF)
        pre = pre_ref[at, :]
        active = pre * sigmoid(pre)
        act_ref[at, :] = active.astype(BF)
        ext_ref[pl.ds(pl.multiple_of(b * rows + 8, 8), rows), :] = (
            proj_ref[at, : plan.conv].astype(BF).astype(F32)
        )
        gact_ref[at, plan.o_x : plan.o_x + wide] = jnp.zeros((rows, wide), F32)
        gact_ref[at, :NSTATE] = jnp.zeros((rows, NSTATE), F32)
        gv_ref[at, :] = jnp.zeros((rows, 128), F32)
        gk_ref[at, :] = jnp.zeros((rows, 128), F32)
        return (
            sums[0] + jnp.sum(grad_in * gated, axis=0, keepdims=True),
            sums[1]
            + jnp.sum(grad_y * active[:, plan.o_x : plan.o_x + wide], axis=0, keepdims=True),
        )

    blank = jnp.zeros((1, wide), F32)
    g_norm_gain, skip_sum = lax.fori_loop(0, blocks, gate, (blank, blank))
    col_ref[...] = jnp.zeros((128, group), F32)

    b_all = act_ref[:, :NSTATE]
    x_all = act_ref[:, plan.o_x : plan.o_x + wide]
    v_all = jnp.where(in_v, proj_ref[:, plan.s_v : plan.s_v + 128], 0.0).astype(BF)
    k_all = kq_ref[...]

    def mix(b, _):
        low = pl.multiple_of(b * rows, rows)
        at = pl.ds(low, rows)
        linked = linked_rows(plan, lengths_ref, low)[0]
        c_blk = act_ref[at, NSTATE : 2 * NSTATE]
        cross = dot_nt(c_blk, b_all)
        cum_b = cum_ref[at, :]
        grad_y = gy_ref[at, :]
        grad_cross = jnp.zeros((rows, group), F32)
        grad_x = jnp.zeros((group, wide), F32)
        row_slab = jnp.zeros((rows, 128), F32)
        y_round = grad_y.astype(BF)
        for j in range(heads):
            col = cum_b[:, off + j : off + j + 1]
            dt_row = dtt_ref[off + j : off + j + 1, :]
            gaps = jnp.where(linked, col - cumt_ref[off + j : off + j + 1, :], -1e30)
            decays = jnp.exp(gaps)
            weights = decays * cross
            mine = lane_w // HDIM == j
            grad_mix = dot_nt(jnp.where(mine, grad_y, 0.0).astype(BF), x_all)
            flow = grad_mix * weights
            col_ref[off + j : off + j + 1, :] += jnp.sum(flow, axis=0, keepdims=True)
            row_slab = jnp.where(
                lane == off + j, jnp.sum(flow * dt_row, axis=1, keepdims=True), row_slab
            )
            grad_cross = grad_cross + grad_mix * (decays * dt_row)
            grad_x = jnp.where(mine, dot_tn((weights * dt_row).astype(BF), y_round), grad_x)
        row_ref[at, :] = row_slab
        grad_cross = grad_cross.astype(BF)
        gact_ref[:, plan.o_x : plan.o_x + wide] += grad_x
        gact_ref[at, NSTATE : 2 * NSTATE] = dot(grad_cross, b_all)
        gact_ref[:, :NSTATE] += dot_tn(grad_cross, c_blk)

        query = jnp.where(lane < HDIM, qk_ref[at, :].astype(F32), 0.0).astype(BF)
        scores = jnp.where(linked, dot_nt(query, k_all) * scale, -1e30)
        probs = jnp.exp(scores - lse_ref[at, 0:1])
        grad_attn = gat_ref[at, :]
        delta = jnp.sum(grad_attn * attn_ref[at, :].astype(F32), axis=1, keepdims=True)
        attn_round = grad_attn.astype(BF)
        grad_prob = dot_nt(attn_round, v_all)
        grad_scores = (probs * (grad_prob - delta)).astype(BF)
        grad_q = dot(grad_scores, k_all) * scale
        gk_ref[...] += dot_tn(grad_scores, kq_ref[at, :]) * scale
        gv_ref[...] += dot_tn(probs.astype(BF), attn_round)
        gat_ref[at, :] = grad_q
        return 0

    lax.fori_loop(0, blocks, mix, 0)

    col_slab = col_ref[...].T
    grad_cum = row_ref[...] - dt_step * col_slab
    grad_decay = dot_tn(lower_tri(group), grad_cum, EXACT)
    grad_dt = col_slab - rate * grad_decay
    grad_dt = jnp.where(live, grad_dt * sigmoid(shifted), 0.0)
    bias_sum = jnp.sum(grad_dt, axis=0, keepdims=True)
    rate_sum = jnp.sum(grad_decay * (-dt_step * rate), axis=0, keepdims=True)
    z_part = ga_ref[:, plan.s_dt : plan.s_dt + 128].astype(F32)
    ga_ref[:, plan.s_dt : plan.s_dt + 128] = (
        jnp.where(lane < off, z_part, 0.0) + grad_dt
    ).astype(BF)

    def finish(b, sums):
        low = pl.multiple_of(b * rows, rows)
        at = pl.ds(low, rows)
        pre = pre_ref[at, :]
        grad_act = gact_ref[at, :]
        grad_x = grad_act[:, plan.o_x :] + skip * gy_ref[at, :]
        grad_act = jnp.concatenate([grad_act[:, : plan.o_x], grad_x], axis=1)
        grad_pre = grad_act * silu_grad(pre, sigmoid(pre))
        gext_ref[at, :] = grad_pre
        pos = linked_rows(plan, lengths_ref, low)[1]
        ext = ext_ref[pl.ds(low, rows + 8), :]
        new = []
        for k in range(KCONV):
            step = KCONV - 1 - k
            moved = ext[8 - step : 8 - step + rows] * (pos >= step).astype(F32)
            new.append(sums[k] + jnp.sum(grad_pre * moved, axis=0, keepdims=True))
        new.append(sums[KCONV] + jnp.sum(grad_pre, axis=0, keepdims=True))
        grad_q = gat_ref[at, :]
        grad_k = gk_ref[at, :]
        both = turn(jnp.where(lane < HDIM, grad_q, grad_k), cos_ref[at, :], -sin_ref[at, :])
        ga_ref[at, plan.o_q :] = both.astype(BF)
        return tuple(new)

    blank = jnp.zeros((1, plan.conv), F32)
    g_taps = lax.fori_loop(0, blocks, finish, (blank,) * (KCONV + 1))

    def close(b, total):
        low = pl.multiple_of(b * rows, rows)
        at = pl.ds(low, rows)
        ext = gext_ref[pl.ds(low, rows + 8), :]
        index = lax.broadcasted_iota(jnp.int32, (rows, 1), 0) + low
        grad_conv = jnp.zeros((rows, plan.conv), F32)
        for k in range(KCONV):
            step = KCONV - 1 - k
            later = index + step
            fits = (later - first_rows(lengths_ref, later) >= step).astype(F32)
            grad_conv = grad_conv + taps[k] * (ext[step : step + rows] * fits)
        ga_ref[at, : plan.conv] = grad_conv.astype(BF)
        v_part = jnp.where(in_v, gv_ref[at, :], 0.0)
        if plan.s_v < plan.conv:
            v_part = v_part + jnp.where(in_v, 0.0, grad_conv[:, plan.s_v : plan.s_v + 128])
        ga_ref[at, plan.s_v : plan.s_v + 128] = v_part.astype(BF)
        partial = dot_nt(ga_ref[at, :], w_ref[:, : plan.a_w])
        normed = rms_forward(x_ref[at, :].astype(F32))[0]
        keep, give = split_rows(plan, partial, t_id)
        out = pl.ds(pl.multiple_of(b * plan.half, plan.half), plan.half)
        keep_ref[out, :] = keep.astype(BF)
        give_ref[out, :] = give.astype(BF)
        return total + jnp.sum(partial * normed, axis=0, keepdims=True)

    g_gain = lax.fori_loop(0, blocks, close, jnp.zeros((1, width), F32))

    def rows_at(entries, count):
        index = lax.broadcasted_iota(jnp.int32, (128, 1), 0)
        total = jnp.zeros((128, count), F32)
        for i, value in entries:
            high = value.astype(BF).astype(F32)
            total = jnp.where(index == row + i, high, total)
            total = jnp.where(index == row + plan.n_small + i, value - high, total)
        return total

    lane_d = lanes(width) % plan.d_loc
    head_vals = jnp.zeros((1, width), F32)
    for j in range(heads):
        picks = (
            jnp.sum(jnp.where(lane == off + j, bias_sum, 0.0), axis=1, keepdims=True),
            jnp.sum(jnp.where(lane == off + j, rate_sum, 0.0), axis=1, keepdims=True),
            jnp.sum(jnp.where(lane_w // HDIM == j, skip_sum, 0.0), axis=1, keepdims=True),
        )
        for i in range(3):
            head_vals = jnp.where(lane_d == i * heads + j, picks[i], head_vals)
    direct = rows_at([(0, g_gain), (1, gain2_ref[...]), (plan.n_small - 1, head_vals)], width)
    selected = [
        rows_at([(2 + k, g_taps[k][:, : 2 * NSTATE]) for k in range(KCONV + 1)], 2 * NSTATE)
    ]
    for k in range(KCONV + 2):
        source = g_taps[k][:, plan.o_x :] if k <= KCONV else g_norm_gain
        selected.append(
            rows_at(
                [
                    (KCONV + 3 + j, jnp.where(lane_w // HDIM == j, source, 0.0))
                    for j in range(heads)
                ],
                wide,
            )
        )
    selected = jnp.concatenate(selected, axis=1).astype(BF)
    small = direct.T + dot_nt(sel_ref[...], selected)
    chunk = min(256, width)
    for start in range(0, width, chunk):
        part = slice(start, start + chunk)
        pack_ref[part, : plan.a_w] = dot_tn(norm_ref[:, part], ga_ref[...]).astype(BF)
        slab = slice(plan.s_dt, plan.s_dt + 128)
        pack_ref[part, slab] = jnp.where(
            lane < row, pack_ref[part, slab].astype(F32), small[part]
        ).astype(BF)
        pack_ref[part, plan.o_mo : plan.o_mo + wide] = dot_tn(gs_ref[:, part], ni_ref[...]).astype(BF)
        slab = slice(plan.s_ao, plan.s_ao + 128)
        attn = dot_tn(got_ref[:, part], attn_ref[...])
        if plan.off:
            attn = jnp.where(in_v, attn, pack_ref[part, slab].astype(F32))
        pack_ref[part, slab] = attn.astype(BF)


def call(kernel, plan, outs, scratch, scalars, arrays):
    smem = pl.BlockSpec(memory_space=pltpu.SMEM)
    vmem = pl.BlockSpec(memory_space=pltpu.VMEM)
    return pl.pallas_call(
        lambda *refs: kernel(plan, *refs),
        out_shape=[jax.ShapeDtypeStruct(shape, kind) for shape, kind in outs],
        in_specs=[smem] * len(scalars) + [vmem] * len(arrays),
        out_specs=[vmem] * len(outs),
        scratch_shapes=[pltpu.VMEM(shape, kind) for shape, kind in scratch],
        compiler_params=pltpu.CompilerParams(vmem_limit_bytes=48 << 20),
    )(*scalars, *arrays)


def per_device(
    inputs,
    seq_lengths,
    norm_gains,
    mamba_in,
    dt_proj,
    bc_proj,
    mamba_chan,
    bc_conv,
    head_params,
    query_proj,
    kv_proj,
    attn_out,
    mamba_out,
    mlp_in,
    mlp_out,
    out_grad,
):
    n_f = lax.axis_size("fsdp")
    n_c = lax.axis_size("context")
    c_id = lax.axis_index("context")
    t_id = lax.axis_index("tensor")
    shards = n_f * n_c
    rows = inputs.shape[0]
    group = rows * n_c
    half = rows // 2
    d_loc = mamba_in.shape[0]
    width = d_loc * shards
    heads_t = head_params.shape[1]
    heads = -(-heads_t // n_c)
    heads_pad = heads * n_c
    q_t = query_proj.shape[1] // HDIM
    ff = mlp_in.shape[2]
    cc = bc_conv.shape[1]
    mc = mamba_chan.shape[1]
    plan = Plan(group, rows, width, d_loc, heads, 2 * heads_t * HDIM, cc, mc)
    chan = plan.chan
    bc_w = 2 * NSTATE
    o_s, o_end, n_small, p_w = plan.o_s, plan.o_end, plan.n_small, plan.p_w

    def by_context(array, axis, count, size):
        padded = pad_to(array, axis, count * n_c * size)
        shape = padded.shape[:axis] + (n_c, count * size) + padded.shape[axis + 1 :]
        return jnp.moveaxis(padded.reshape(shape), axis, 0)

    inner_ctx = by_context(mamba_in, 2, heads, HDIM)
    query_ctx = by_context(query_proj, 1, 1, HDIM)
    dt_ctx = by_context(dt_proj, 1, heads, 1)
    chan_ctx = pad_to(jnp.swapaxes(by_context(mamba_chan, 0, heads, 1), 1, 2), 1, d_loc)
    mo_ctx = jnp.swapaxes(by_context(mamba_out, 0, heads, HDIM), 1, 2)
    ao_ctx = jnp.swapaxes(by_context(attn_out, 0, 1, HDIM), 1, 2)

    def everywhere(array):
        return jnp.broadcast_to(array[None], (n_c,) + array.shape)

    pieces = [
        (0, everywhere(bc_proj)),
        (plan.o_x, inner_ctx[:, :, 1]),
        (plan.o_v, everywhere(kv_proj[:, 1])),
        (plan.o_z, inner_ctx[:, :, 0]),
        (plan.o_dt, dt_ctx),
        (
            plan.o_s,
            everywhere(jnp.concatenate([norm_gains.T, pad_to(bc_conv.T, 0, d_loc)], axis=1)),
        ),
        (plan.o_s + KCONV + 3, chan_ctx),
        (plan.o_q, query_ctx),
        (plan.o_k, everywhere(kv_proj[:, 0])),
        (plan.o_mo, mo_ctx),
        (plan.o_ao, ao_ctx),
        (plan.p_w, None),
    ]
    columns = []
    filled = 0
    for start, piece in pieces:
        if start > filled:
            columns.append(jnp.zeros((n_c, d_loc, start - filled), BF))
        if piece is not None:
            columns.append(piece)
            filled = start + piece.shape[2]
    pack = jnp.concatenate(columns, axis=2)

    mine = lax.dynamic_slice_in_dim(inputs, t_id * half, half, 0)
    part = exchange(pack, "context").reshape(n_c * d_loc, p_w)
    got_in = spread_async(mine, "context")
    w_all = spread(part, "fsdp").reshape(width, p_w)
    rows_in = join_pair(got_in, swap_pair(got_in), t_id, 1).reshape(group, width)
    part_mi = spread_async(mlp_in.reshape(d_loc, 2 * ff), "context")
    part_mo = spread_async(mlp_out.T, "context")
    w_mi = plane_gather(part_mi.reshape(n_c * d_loc, 2 * ff)).reshape(width, 2 * ff)
    w_mo = plane_gather(part_mo.reshape(n_c * d_loc, ff)).reshape(width, ff)

    starts = jnp.cumsum(seq_lengths[0]) - seq_lengths[0]
    row_ids = jnp.arange(group, dtype=jnp.int32)
    inside = row_ids[:, None] >= starts[None, :]
    positions = row_ids - jnp.max(jnp.where(inside, starts[None, :], 0), axis=1)
    freqs = jnp.power(ROPE_BASE, -jnp.arange(HDIM // 2).astype(F32) * (2.0 / HDIM))
    angles = positions.astype(F32)[:, None] * jnp.concatenate([freqs] * 4)[None, :]
    cosine = jnp.cos(angles)
    sine = jnp.sin(angles)
    head_vec = lax.dynamic_slice_in_dim(
        pad_to(head_params, 1, heads_pad), c_id * heads, heads, 1
    )
    feature = jnp.arange(width, dtype=jnp.int32)[:, None]
    place = feature % d_loc
    shard = feature // d_loc
    lane = jnp.arange(plan.wide, dtype=jnp.int32)[None, :] % HDIM
    sel = [(place < cc) & (shard * cc + place == jnp.arange(bc_w, dtype=jnp.int32)[None, :])]
    for k in range(KCONV + 2):
        sel.append((place < mc) & (shard * mc + place == k * HDIM + lane))
    sel = jnp.concatenate(sel, axis=1).astype(BF)
    scalars = (seq_lengths, head_vec, t_id.reshape(1))
    slab_w = 2 * width + 128
    part_rows = n_c * half
    keep, give, gain_two, norm, proj, pre, cum, ssm, attn, lse, qk, kq = call(
        forward_kernel,
        plan,
        [
            ((part_rows, slab_w), BF),
            ((part_rows, slab_w), BF),
            ((1, width), F32),
            ((group, width), BF),
            ((group, plan.a_w), F32),
            ((group, plan.conv), F32),
            ((group, 128), F32),
            ((group, plan.wide), F32),
            ((group, 128), BF),
            ((group, 128), F32),
            ((group, 128), BF),
            ((group, 128), BF),
        ],
        [((group, plan.conv), BF), ((group + 8, plan.conv), F32)],
        scalars,
        (rows_in, w_all, sel, cosine, sine),
    )
    gain_mlp = gain_two[0]

    def pair_parts(values, lead):
        parts = values.reshape(lead + (2, half) + values.shape[1:])
        keep = lax.dynamic_index_in_dim(parts, t_id, len(lead), False)
        return keep, lax.dynamic_index_in_dim(parts, 1 - t_id, len(lead), False)

    def pair_sum(values, lead):
        keep, give = pair_parts(values, lead)
        return keep + swap_pair(give.astype(BF)).astype(F32)

    def pair_add(keep, give):
        return (keep.astype(F32) + swap_pair(give).astype(F32)).astype(BF)

    summed = pair_add(keep, give).reshape(n_c, half, slab_w)
    both = jnp.sum(exchange(summed, "context").astype(F32), axis=0)
    squares = jnp.sum(both[:, 2 * width : 2 * width + 4], axis=1, keepdims=True)
    scale_own = lax.rsqrt(squares / plan.total + NORM_EPS)
    mamba_own = both[:, :width]
    in_own = mine.astype(F32)
    residual = in_own + scale_own * mamba_own + both[:, width : 2 * width]

    normed_two, inv_two = rms_forward(residual)
    norm_two_own = (normed_two * gain_mlp[None, :]).astype(BF)
    norm_two = join_pair(norm_two_own, swap_pair(norm_two_own), t_id, 0).reshape(rows, width)
    stacked = jnp.concatenate([norm_two, out_grad], axis=0)
    first = dot(norm_two, w_mi)
    gate_val = first[:, :ff]
    up_val = first[:, ff:]
    grad_act = dot(out_grad, w_mo)
    gate_sig = sigmoid(gate_val)
    gate_act = gate_val * gate_sig
    mlp_act = (gate_act * up_val).astype(BF)
    grad_gate = (grad_act * up_val * silu_grad(gate_val, gate_sig)).astype(BF)
    grad_up = (grad_act * gate_act).astype(BF)
    blank = jnp.zeros((rows, ff), BF)
    mixed = jnp.concatenate(
        [
            jnp.concatenate([grad_gate, grad_up, blank], axis=1),
            jnp.concatenate([blank, blank, mlp_act], axis=1),
        ],
        axis=0,
    )
    grad_two = pair_sum(dot_nt(mixed[:rows, : 2 * ff], w_mi), ())
    out_own = (residual + pair_sum(dot_nt(mlp_act, w_mo), ())).astype(BF)

    top_own = lax.dynamic_slice_in_dim(out_grad, t_id * half, half, 0).astype(F32)
    g_gain_mlp = jnp.sum(grad_two * normed_two, axis=0)
    grad_res = top_own + rms_backward(grad_two, normed_two, inv_two, gain_mlp)
    grad_rs_own = jnp.sum(grad_res * mamba_own, axis=1, keepdims=True)
    factor = split(jnp.concatenate([grad_rs_own, scale_own], axis=1), 2)
    got = spread(jnp.concatenate([grad_res.astype(BF), factor], axis=1), "context")
    got = join_pair(got, swap_pair(got), t_id, 1).reshape(group, -1)
    block = n_c * d_loc

    def mlp_block(target):
        cols = lax.dynamic_slice_in_dim(stacked, target * block, block, 1)
        return dot_tn(cols, mixed)

    own = plane_reduce(mlp_block)
    own = reduce_async(own.astype(BF).reshape(n_c, d_loc, 3 * ff), "context")
    out_mi = own[:, : 2 * ff].reshape(d_loc, 2, ff)
    out_mo = own[:, 2 * ff :].T

    keep, give, g_pack = call(
        backward_kernel,
        plan,
        [((part_rows, width), BF), ((part_rows, width), BF), ((width, p_w), BF)],
        [
            ((group, plan.conv), BF),
            ((group + 8, plan.conv), F32),
            ((group, width), BF),
            ((group, plan.wide), BF),
            ((group, plan.wide), F32),
            ((group, plan.a_w), BF),
            ((group, plan.conv), F32),
            ((group + 8, plan.conv), F32),
            ((group, 128), F32),
            ((group, 128), F32),
            ((group, 128), F32),
            ((group, 128), F32),
            ((128, group), F32),
            ((128, group), F32),
            ((128, group), F32),
        ],
        scalars,
        (
            rows_in, w_all, sel, cosine, sine, norm, proj, pre, cum, ssm, attn, lse, qk, kq, got,
            g_gain_mlp[None],
        ),
    )
    partial = pair_add(keep, give).reshape(n_c, half, width)
    grad_one = reduce_async(partial, "context")
    gain_mix = w_all[:, o_s].astype(F32)
    normed_own, inv_own = rms_forward(in_own)
    grad_in_own = grad_res + rms_backward(grad_one, normed_own, inv_own, gain_mix)
    output = join_pair(out_own, swap_pair(out_own), t_id, 0).reshape(rows, width)
    input_grad = join_pair(grad_in_own, swap_pair(grad_in_own), t_id, 0).reshape(rows, width)

    got = exchange(g_pack.reshape(n_f, block, p_w), "fsdp")
    got = jnp.sum(got.astype(F32), axis=0)
    g_small = fuse(got[:, o_s:o_end], 2, n_small)
    g_pack = jnp.concatenate(
        [got[:, :o_s].astype(BF), split(g_small, 2, False), got[:, o_end:].astype(BF)], axis=1
    )
    g_a = exchange(g_pack.reshape(n_c, d_loc, p_w), "context").astype(F32)

    def joined(low, size, count):
        moved = jnp.moveaxis(g_a[:, :, low : low + size], 0, 1).reshape(d_loc, n_c * size)
        return moved[:, : count]

    out_inner = jnp.stack(
        [
            joined(plan.o_z, chan, heads_t * HDIM),
            joined(plan.o_x, chan, heads_t * HDIM),
        ],
        axis=1,
    )
    out_query = joined(plan.o_q, HDIM, q_t * HDIM)
    out_dt = joined(plan.o_dt, heads, heads_t)
    out_kv = jnp.stack(
        [
            jnp.sum(g_a[:, :, plan.o_k : plan.o_k + HDIM], axis=0),
            jnp.sum(g_a[:, :, plan.o_v : plan.o_v + HDIM], axis=0),
        ],
        axis=1,
    )
    out_mout = joined(plan.o_mo, chan, heads_t * HDIM).T
    out_aout = joined(plan.o_ao, HDIM, q_t * HDIM).T
    g_small = fuse(g_a[:, :, o_s:o_end], 2, n_small)
    tail = jnp.concatenate([g_a[:, :, :bc_w], g_small[:, :, : KCONV + 3]], axis=2)
    tail = jnp.sum(tail, axis=0)
    tail = tail + swap_pair(tail)
    out_bc = tail[:, :bc_w]
    out_gains = tail[:, bc_w : bc_w + 2].T
    out_convbc = tail[:cc, bc_w + 2 :].T
    out_chan = jnp.swapaxes(g_small[:, :mc, KCONV + 3 : KCONV + 3 + heads], 1, 2)
    out_chan = out_chan.reshape(heads_pad, mc)[:heads_t]
    out_heads = g_small[:, : 3 * heads, n_small - 1].reshape(n_c, 3, heads)
    out_heads = jnp.swapaxes(out_heads, 0, 1).reshape(3, heads_pad)[:, :heads_t]

    return (
        output,
        input_grad,
        out_gains,
        out_inner,
        out_dt,
        out_bc,
        out_chan,
        out_convbc,
        out_heads,
        out_query,
        out_kv,
        out_aout,
        out_mout,
        out_mi,
        out_mo,
    )


def solution(mesh):
    both = ("fsdp", "context")
    rows = P(both, None)

    return jax.shard_map(
        per_device,
        mesh=mesh,
        in_specs=(
            rows,
            P("fsdp", None),
            P(None, both),
            P(both, None, "tensor"),
            P(both, "tensor"),
            rows,
            P("tensor", both),
            P(None, both),
            P(None, "tensor"),
            P(both, "tensor"),
            P(both, None, "tensor"),
            P("tensor", both),
            P("tensor", both),
            P(both, None, "tensor"),
            P("tensor", both),
            rows,
        ),
        out_specs=(
            rows,
            rows,
            P(None, both),
            P(both, None, "tensor"),
            P(both, "tensor"),
            rows,
            P("tensor", both),
            P(None, both),
            P(None, "tensor"),
            P(both, "tensor"),
            P(both, None, "tensor"),
            P("tensor", both),
            P("tensor", both),
            P(both, None, "tensor"),
            P("tensor", both),
        ),
        check_vma=False,
    )
```

```python
import jax
import jax.numpy as jnp
from jax import lax
from jax.experimental import pallas as pl
from jax.experimental.pallas import tpu as pltpu
from jax.sharding import PartitionSpec as P


HDIM = 64
NSTATE = 128
KCONV = 4
NORM_EPS = 1e-05
ROPE_BASE = 100000000000.0
EXACT = lax.Precision.HIGHEST
BF = jnp.bfloat16
F32 = jnp.float32


def swap_pair(block):
    return lax.ppermute(block, "tensor", [(0, 1), (1, 0)])


def join_pair(own, other, place, axis):
    low = jnp.where(place == 0, own, other)
    high = jnp.where(place == 0, other, own)
    return jnp.stack([low, high], axis=axis)


def exchange(blocks, axis):
    return lax.all_to_all(blocks, axis, 0, 0, tiled=True)


def spread(block, axis):
    return exchange(jnp.broadcast_to(block[None], (lax.axis_size(axis),) + block.shape), axis)


def hops(axis):
    count = lax.axis_size(axis)
    place = lax.axis_index(axis)
    for step in range(1, count):
        route = [(i, (i + step) % count) for i in range(count)]
        yield route, (place + step) % count, (place - step) % count


def spread_async(block, axis):
    count = lax.axis_size(axis)
    got = [(lax.ppermute(block, axis, route), source) for route, _, source in hops(axis)]
    if block.size > 1 << 18:
        whole = jnp.zeros((count,) + block.shape, block.dtype)
        whole = lax.dynamic_update_index_in_dim(whole, block, lax.axis_index(axis), 0)
        for piece, source in got:
            whole = lax.dynamic_update_index_in_dim(whole, piece, source, 0)
        return whole
    place = lax.axis_index(axis)
    pieces = [block] + [piece for piece, _ in got]
    return jnp.stack(
        [lax.select_n((place - i) % count, *pieces) for i in range(count)], axis=0
    )


def reduce_async(blocks, axis):
    got = [
        lax.ppermute(lax.dynamic_index_in_dim(blocks, target, 0, False), axis, route)
        for route, target, _ in hops(axis)
    ]
    total = lax.dynamic_index_in_dim(blocks, lax.axis_index(axis), 0, False).astype(F32)
    for piece in got:
        total = total + piece.astype(F32)
    return total


def beside(step):
    return [(i, i ^ step) for i in range(4)]


def plane_gather(block):
    if lax.axis_size("fsdp") != 4:
        return spread_async(block, "fsdp")
    half = block.shape[0] // 2
    place = lax.axis_index("fsdp")
    near = lax.ppermute(block, "fsdp", beside(1))
    side = lax.ppermute(block, "fsdp", beside(2))
    far_top = lax.ppermute(side[:half], "fsdp", beside(1))
    far_low = lax.ppermute(near[half:], "fsdp", beside(2))
    whole = jnp.zeros((4, 2, half) + block.shape[1:], block.dtype)
    parts = ((block, place), (near, place ^ 1), (side, place ^ 2))
    for piece, index in parts:
        piece = piece.reshape((1, 2, half) + block.shape[1:])
        whole = lax.dynamic_update_slice(whole, piece, (index, 0, 0, 0))
    for row, piece in enumerate((far_top, far_low)):
        whole = lax.dynamic_update_slice(whole, piece[None, None], (place ^ 3, row, 0, 0))
    return whole


def plane_reduce(make):
    def whole(target):
        return jnp.concatenate([make(target, 0), make(target, 1)], axis=0)

    if lax.axis_size("fsdp") != 4:
        sent = [(route, whole(target).astype(BF)) for route, target, _ in hops("fsdp")]
        own = whole(lax.axis_index("fsdp"))
        for route, piece in sent:
            own = own + lax.ppermute(piece, "fsdp", route).astype(F32)
        return own.astype(BF)
    place = lax.axis_index("fsdp")
    got_side = lax.ppermute(make(place ^ 3, 0).astype(BF), "fsdp", beside(1))
    got_near = lax.ppermute(make(place ^ 3, 1).astype(BF), "fsdp", beside(2))
    near_top = lax.ppermute(make(place ^ 1, 0).astype(BF), "fsdp", beside(1))
    side_low = lax.ppermute(make(place ^ 2, 1).astype(BF), "fsdp", beside(2))
    own_top = make(place, 0).astype(BF)
    own_low = make(place, 1).astype(BF)
    side_top = make(place ^ 2, 0).astype(BF)
    near_low = make(place ^ 1, 1).astype(BF)
    side_top = (side_top.astype(F32) + got_side.astype(F32)).astype(BF)
    near_low = (near_low.astype(F32) + got_near.astype(F32)).astype(BF)
    side_top = lax.ppermute(side_top, "fsdp", beside(2))
    near_low = lax.ppermute(near_low, "fsdp", beside(1))
    top = own_top.astype(F32) + near_top.astype(F32) + side_top.astype(F32)
    low = own_low.astype(F32) + near_low.astype(F32) + side_low.astype(F32)
    return jnp.concatenate([top, low], axis=0).astype(BF)


def sigmoid(values):
    return 1.0 / (1.0 + jnp.exp(-values))


def silu_grad(values, sigma):
    return sigma * (1.0 + values * (1.0 - sigma))


def rms_forward(values):
    inv_rms = lax.rsqrt(jnp.mean(values * values, axis=-1, keepdims=True) + NORM_EPS)
    return values * inv_rms, inv_rms


def rms_backward(grad_out, normed, inv_rms, gain_vec):
    grad_normed = grad_out * gain_vec[None, :]
    return inv_rms * (grad_normed - normed * jnp.mean(grad_normed * normed, axis=-1, keepdims=True))


def dot(left, right, exact=None):
    return lax.dot_general(
        left, right, (((1,), (0,)), ((), ())), precision=exact, preferred_element_type=F32
    )


def dot_nt(left, right, exact=None):
    return lax.dot_general(
        left, right, (((1,), (1,)), ((), ())), precision=exact, preferred_element_type=F32
    )


def dot_tn(left, right, exact=None):
    return lax.dot_general(
        left, right, (((0,), (0,)), ((), ())), precision=exact, preferred_element_type=F32
    )


def pad_to(array, axis, size):
    if array.shape[axis] == size:
        return array
    widths = [(0, 0)] * array.ndim
    widths[axis] = (0, size - array.shape[axis])
    return jnp.pad(array, widths)


def ceil_to(value, unit):
    return -(-value // unit) * unit


def split(values, pieces, wide=True):
    parts = []
    for _ in range(pieces):
        high = lax.reduce_precision(values, 8, 7)
        parts.append(high.astype(BF))
        values = values - high
    joined = jnp.concatenate(parts, axis=-1)
    return pad_to(joined, joined.ndim - 1, 128) if wide else joined


def fuse(values, pieces, count):
    values = values.astype(F32)
    total = values[..., :count]
    for i in range(1, pieces):
        total = total + values[..., i * count : (i + 1) * count]
    return total


class Plan:
    def __init__(self, group, rows, width, d_loc, heads, total, cc, mc):
        self.group, self.rows, self.width, self.d_loc = group, rows, width, d_loc
        self.heads, self.total, self.cc, self.mc = heads, total, cc, mc
        self.half = rows // 2
        self.chan = heads * HDIM
        self.wide = ceil_to(self.chan, 128)
        self.off = self.chan % 128
        self.conv = 2 * NSTATE + self.wide
        self.o_x = 2 * NSTATE
        self.o_v = self.o_x + self.chan
        self.o_z = ceil_to(self.o_v + HDIM, 128)
        self.o_dt = self.o_z + self.chan
        self.o_s = self.o_dt + heads
        self.n_small = KCONV + 4 + heads
        self.o_end = self.o_s + 2 * self.n_small
        self.o_q = ceil_to(self.o_end, 128)
        self.o_k = self.o_q + HDIM
        self.a_w = self.o_q + 2 * HDIM
        self.o_mo = self.a_w
        self.o_ao = self.a_w + self.chan
        self.p_w = ceil_to(self.o_ao + HDIM, 128)
        self.s_v = self.o_v - self.off
        self.s_dt = self.o_dt - self.off
        self.s_ao = self.o_ao - self.off
        self.row = self.off + heads


def lanes(count):
    return lax.broadcasted_iota(jnp.int32, (1, count), 1)


def first_rows(lengths_ref, index):
    start = jnp.zeros_like(index)
    edge = jnp.int32(0)
    for i in range(lengths_ref.shape[1] - 1):
        edge = edge + lengths_ref[0, i]
        start = jnp.where(index >= edge, edge, start)
    return start


def head_row(plan, head_ref, which):
    lane = lanes(128)
    row = jnp.zeros((1, 128), F32)
    for j in range(plan.heads):
        row = jnp.where(lane == plan.off + j, head_ref[which, j], row)
    return row


def head_wide(plan, values):
    lane = lanes(plan.wide)
    row = jnp.zeros((1, plan.wide), F32)
    for j in range(plan.heads):
        row = jnp.where(lane // HDIM == j, values[j], row)
    return row


def steps_of(plan, head_ref, slab):
    lane = lanes(128)
    live = (lane >= plan.off) & (lane < plan.row)
    shifted = jnp.where(live, slab + head_row(plan, head_ref, 0), 0.0)
    soft = jnp.maximum(shifted, 0.0) + jnp.log1p(jnp.exp(-jnp.abs(shifted)))
    dt_step = jnp.where(live, soft, 0.0)
    rate = jnp.where(live, jnp.exp(head_row(plan, head_ref, 1)), 0.0)
    return dt_step, rate, shifted, live


def small_rows(plan, w_ref, sel_ref):
    slab = w_ref[:, plan.s_dt : plan.s_dt + 128]
    turned = slab.astype(F32).T
    picked = dot_tn(slab, sel_ref[...])
    row = plan.row
    lane = lanes(plan.wide)
    taps = []
    for k in range(KCONV + 2):
        low = 2 * NSTATE + k * plan.wide
        piece = jnp.zeros((1, plan.wide), F32)
        for j in range(plan.heads):
            at = row + KCONV + 3 + j
            piece = jnp.where(lane // HDIM == j, picked[at : at + 1, low : low + plan.wide], piece)
        if k <= KCONV:
            piece = jnp.concatenate(
                [picked[row + 2 + k : row + 3 + k, : 2 * NSTATE], piece], axis=1
            )
        taps.append(piece)
    return turned[row : row + 1], turned[row + 1 : row + 2], taps


def lower_tri(group):
    return (
        lax.broadcasted_iota(jnp.int32, (group, group), 0)
        >= lax.broadcasted_iota(jnp.int32, (group, group), 1)
    ).astype(F32)


def linked_rows(plan, lengths_ref, low):
    index = lax.broadcasted_iota(jnp.int32, (plan.rows, 1), 0) + low
    start = first_rows(lengths_ref, index)
    cols = lanes(plan.group)
    return (cols <= index) & (cols >= start), index - start


def turn(values, cosine, sine):
    lane = lanes(2 * HDIM)
    moved = jnp.where(
        lane % HDIM < HDIM // 2, -pltpu.roll(values, 2 * HDIM - HDIM // 2, 1),
        pltpu.roll(values, HDIM // 2, 1),
    )
    return values * cosine + moved * sine


def split_rows(plan, values, t_id):
    low = values[: plan.half]
    high = values[plan.half :]
    return jnp.where(t_id == 0, low, high), jnp.where(t_id == 0, high, low)


def forward_kernel(
    plan, lengths_ref, head_ref, t_ref, x_ref, w_ref, sel_ref, cos_ref, sin_ref,
    keep_ref, give_ref, gain2_ref, taps_ref, norm_ref, proj_ref, pre_ref, cum_ref, ssm_ref, attn_ref, lse_ref, qk_ref,
    kq_ref, act_ref, ext_ref, dt_ref,
):
    rows, group, wide = plan.rows, plan.group, plan.wide
    gain, gain_two, taps = small_rows(plan, w_ref, sel_ref)
    gain2_ref[...] = gain_two
    for k in range(KCONV + 1):
        taps_ref[k : k + 1, :] = taps[k]
    taps_ref[KCONV + 1 : KCONV + 2, plan.o_x :] = taps[KCONV + 1]
    blocks = group // rows
    t_id = t_ref[0]
    ext_ref[0:8, :] = jnp.zeros((8, plan.conv), F32)

    lower = lower_tri(rows)

    def project(b, before):
        at = pl.ds(pl.multiple_of(b * rows, rows), rows)
        values = x_ref[at, :].astype(F32)
        normed = rms_forward(values)[0]
        norm = (normed * gain).astype(BF)
        norm_ref[at, :] = norm
        proj = dot(norm, w_ref[:, : plan.a_w])
        proj_ref[at, :] = proj
        ext_ref[pl.ds(pl.multiple_of(b * rows + 8, 8), rows), :] = (
            proj[:, : plan.conv].astype(BF).astype(F32)
        )
        rot = turn(proj[:, plan.o_q :], cos_ref[at, :], sin_ref[at, :])
        qk_ref[at, :] = rot.astype(BF)
        kq_ref[at, :] = pltpu.roll(rot, HDIM, 1).astype(BF)
        dt_step, rate, _, _ = steps_of(plan, head_ref, proj[:, plan.s_dt : plan.s_dt + 128])
        dt_ref[at, :] = dt_step
        cum = dot(lower, -dt_step * rate, EXACT) + before
        cum_ref[at, :] = cum
        return cum[rows - 1 : rows]

    lax.fori_loop(0, blocks, project, jnp.zeros((1, 128), F32))
    cum_t = cum_ref[...].T
    dt_t = dt_ref[...].T

    def convolve(b, _):
        low = pl.multiple_of(b * rows, rows)
        at = pl.ds(low, rows)
        pos = linked_rows(plan, lengths_ref, low)[1]
        ext = ext_ref[pl.ds(low, rows + 8), :]
        total = jnp.broadcast_to(taps[KCONV], (rows, plan.conv))
        for k in range(KCONV):
            step = KCONV - 1 - k
            total = total + taps[k] * (ext[8 - step : 8 - step + rows] * (pos >= step).astype(F32))
        pre_ref[at, :] = total
        act_ref[at, :] = (total * sigmoid(total)).astype(BF)
        return 0

    lax.fori_loop(0, blocks, convolve, 0)

    lane_w = lanes(wide)
    lane = lanes(128)
    in_v = (lane >= plan.off) & (lane < plan.off + HDIM)
    b_all = act_ref[:, :NSTATE]
    x_all = act_ref[:, plan.o_x : plan.o_x + wide]
    v_all = jnp.where(in_v, proj_ref[:, plan.s_v : plan.s_v + 128], 0.0).astype(BF)
    k_all = kq_ref[...]
    skip = head_wide(plan, [head_ref[2, j] for j in range(plan.heads)])
    w_m = w_ref[:, plan.o_mo : plan.o_mo + wide]
    w_o = w_ref[:, plan.s_ao : plan.s_ao + 128]

    def mix(b, _):
        low = pl.multiple_of(b * rows, rows)
        at = pl.ds(low, rows)
        linked = linked_rows(plan, lengths_ref, low)[0]
        cross = dot_nt(act_ref[at, NSTATE : 2 * NSTATE], b_all)
        cum_b = cum_ref[at, :]
        core = jnp.zeros((rows, wide), F32)
        for j in range(plan.heads):
            col = cum_b[:, plan.off + j : plan.off + j + 1]
            gaps = jnp.where(linked, col - cum_t[plan.off + j : plan.off + j + 1], -1e30)
            mixing = jnp.exp(gaps) * cross * dt_t[plan.off + j : plan.off + j + 1]
            core = jnp.where(lane_w // HDIM == j, dot(mixing.astype(BF), x_all), core)
        pre = pre_ref[at, plan.o_x : plan.o_x + wide]
        ssm = core + skip * (pre * sigmoid(pre))
        ssm_ref[at, :] = ssm
        z_gate = proj_ref[at, plan.o_z : plan.o_z + wide].astype(BF).astype(F32)
        gated = jnp.where(lane_w < plan.chan, ssm * (z_gate * sigmoid(z_gate)), 0.0)
        norm_in = (gated * taps[KCONV + 1]).astype(BF)
        square = jnp.sum(gated * gated, axis=1, keepdims=True)
        high = square.astype(BF).astype(F32)
        square = jnp.where(
            lane == 2 * t_id, high, jnp.where(lane == 2 * t_id + 1, square - high, 0.0)
        )

        query = jnp.where(lane < HDIM, qk_ref[at, :].astype(F32), 0.0).astype(BF)
        scores = jnp.where(linked, dot_nt(query, k_all) * HDIM ** (-0.5), -1e30)
        top = jnp.max(scores, axis=1, keepdims=True)
        exps = jnp.exp(scores - top)
        total = jnp.sum(exps, axis=1, keepdims=True)
        values = dot((exps / total).astype(BF), v_all).astype(BF)
        attn_ref[at, :] = values
        lse_ref[at, :] = jnp.broadcast_to(top + jnp.log(total), (rows, 128))

        out = pl.ds(pl.multiple_of(b * plan.half, plan.half), plan.half)
        width = plan.width
        for start, piece in (
            (0, dot_nt(norm_in, w_m)),
            (width, dot_nt(values, w_o)),
            (2 * width, square),
        ):
            keep, give = split_rows(plan, piece, t_id)
            keep_ref[out, start : start + piece.shape[1]] = keep.astype(BF)
            give_ref[out, start : start + piece.shape[1]] = give.astype(BF)
        return 0

    lax.fori_loop(0, blocks, mix, 0)


def backward_kernel(
    plan, lengths_ref, head_ref, t_ref, x_ref, w_ref, sel_ref, cos_ref, sin_ref,
    taps_ref, norm_ref, proj_ref, pre_ref, cum_ref, ssm_ref, attn_ref, lse_ref, qk_ref, kq_ref, got_ref,
    gain2_ref,
    keep_ref, give_ref, pack_ref,
    act_ref, ext_ref, gs_ref, ni_ref, gy_ref, ga_ref, gact_ref, gext_ref, gv_ref, gk_ref, gat_ref,
    row_ref, col_ref, dtt_ref, cumt_ref, small_ref, dt_ref,
):
    rows, group, wide, width = plan.rows, plan.group, plan.wide, plan.width
    heads, off, row = plan.heads, plan.off, plan.row
    taps = [taps_ref[k : k + 1, :] for k in range(KCONV + 1)]
    blocks = group // rows
    t_id = t_ref[0]
    lane_w = lanes(wide)
    lane = lanes(128)
    in_v = (lane >= off) & (lane < off + HDIM)
    norm_gain = taps_ref[KCONV + 1 : KCONV + 2, plan.o_x :]
    w_m = w_ref[:, plan.o_mo : plan.o_mo + wide]
    w_o = w_ref[:, plan.s_ao : plan.s_ao + 128]
    ext_ref[0:8, :] = jnp.zeros((8, plan.conv), F32)
    gext_ref[group : group + 8, :] = jnp.zeros((8, plan.conv), F32)
    skip = head_wide(plan, [head_ref[2, j] for j in range(heads)])
    scale = HDIM ** (-0.5)

    cumt_ref[...] = cum_ref[...].T

    def gate(b, sums):
        at = pl.ds(pl.multiple_of(b * rows, rows), rows)
        grad_round = got_ref[at, :width]
        factor = got_ref[at, width : width + 128].astype(F32)
        grad_rs = factor[:, 0:1] + factor[:, 2:3]
        row_scale = factor[:, 1:2] + factor[:, 3:4]
        grad_scaled = (grad_round.astype(F32) * row_scale).astype(BF)
        gs_ref[at, :] = grad_scaled
        grad_in = jnp.where(lane_w < plan.chan, dot(grad_scaled, w_m), 0.0)
        gat_ref[at, :] = jnp.where(in_v, dot(grad_round, w_o), 0.0)
        z_gate = proj_ref[at, plan.o_z : plan.o_z + wide].astype(BF).astype(F32)
        z_gate = jnp.where(lane_w < plan.chan, z_gate, 0.0)
        z_sig = sigmoid(z_gate)
        silu_z = z_gate * z_sig
        ssm = ssm_ref[at, :]
        gated = ssm * silu_z
        ni_ref[at, :] = (gated * norm_gain).astype(BF)
        grad_gated = grad_in * norm_gain - gated * (
            grad_rs * row_scale * row_scale * row_scale / plan.total
        )
        grad_y = grad_gated * silu_z
        gy_ref[at, :] = grad_y
        grad_z = grad_gated * ssm * silu_grad(z_gate, z_sig)
        ga_ref[at, plan.o_z : plan.o_z + wide] = grad_z.astype(BF)
        pre = pre_ref[at, :]
        active = pre * sigmoid(pre)
        act_ref[at, :] = active.astype(BF)
        ext_ref[pl.ds(pl.multiple_of(b * rows + 8, 8), rows), :] = (
            proj_ref[at, : plan.conv].astype(BF).astype(F32)
        )
        gact_ref[at, plan.o_x : plan.o_x + wide] = jnp.zeros((rows, wide), F32)
        gact_ref[at, :NSTATE] = jnp.zeros((rows, NSTATE), F32)
        gv_ref[at, :] = jnp.zeros((rows, 128), F32)
        gk_ref[at, :] = jnp.zeros((rows, 128), F32)
        dt_ref[at, :] = steps_of(plan, head_ref, proj_ref[at, plan.s_dt : plan.s_dt + 128])[0]
        return (
            sums[0] + jnp.sum(grad_in * gated, axis=0, keepdims=True),
            sums[1]
            + jnp.sum(grad_y * active[:, plan.o_x : plan.o_x + wide], axis=0, keepdims=True),
        )

    blank = jnp.zeros((1, wide), F32)
    g_norm_gain, skip_sum = lax.fori_loop(0, blocks, gate, (blank, blank))
    col_ref[...] = jnp.zeros((128, group), F32)
    dtt_ref[...] = dt_ref[...].T

    b_all = act_ref[:, :NSTATE]
    x_all = act_ref[:, plan.o_x : plan.o_x + wide]
    v_all = jnp.where(in_v, proj_ref[:, plan.s_v : plan.s_v + 128], 0.0).astype(BF)
    k_all = kq_ref[...]

    def mix(b, _):
        low = pl.multiple_of(b * rows, rows)
        at = pl.ds(low, rows)
        linked = linked_rows(plan, lengths_ref, low)[0]
        c_blk = act_ref[at, NSTATE : 2 * NSTATE]
        cross = dot_nt(c_blk, b_all)
        cum_b = cum_ref[at, :]
        grad_y = gy_ref[at, :]
        grad_cross = jnp.zeros((rows, group), F32)
        grad_x = jnp.zeros((group, wide), F32)
        row_slab = jnp.zeros((rows, 128), F32)
        y_round = grad_y.astype(BF)
        for j in range(heads):
            col = cum_b[:, off + j : off + j + 1]
            dt_row = dtt_ref[off + j : off + j + 1, :]
            gaps = jnp.where(linked, col - cumt_ref[off + j : off + j + 1, :], -1e30)
            decays = jnp.exp(gaps)
            weights = decays * cross
            mine = lane_w // HDIM == j
            grad_mix = dot_nt(jnp.where(mine, grad_y, 0.0).astype(BF), x_all)
            flow = grad_mix * weights
            col_ref[off + j : off + j + 1, :] += jnp.sum(flow, axis=0, keepdims=True)
            row_slab = jnp.where(
                lane == off + j, jnp.sum(flow * dt_row, axis=1, keepdims=True), row_slab
            )
            grad_cross = grad_cross + grad_mix * (decays * dt_row)
            grad_x = jnp.where(mine, dot_tn((weights * dt_row).astype(BF), y_round), grad_x)
        row_ref[at, :] = row_slab
        grad_cross = grad_cross.astype(BF)
        gact_ref[:, plan.o_x : plan.o_x + wide] += grad_x
        gact_ref[at, NSTATE : 2 * NSTATE] = dot(grad_cross, b_all)
        gact_ref[:, :NSTATE] += dot_tn(grad_cross, c_blk)

        query = jnp.where(lane < HDIM, qk_ref[at, :].astype(F32), 0.0).astype(BF)
        scores = jnp.where(linked, dot_nt(query, k_all) * scale, -1e30)
        probs = jnp.exp(scores - lse_ref[at, 0:1])
        grad_attn = gat_ref[at, :]
        delta = jnp.sum(grad_attn * attn_ref[at, :].astype(F32), axis=1, keepdims=True)
        attn_round = grad_attn.astype(BF)
        grad_prob = dot_nt(attn_round, v_all)
        grad_scores = (probs * (grad_prob - delta)).astype(BF)
        grad_q = dot(grad_scores, k_all) * scale
        gk_ref[...] += dot_tn(grad_scores, kq_ref[at, :]) * scale
        gv_ref[...] += dot_tn(probs.astype(BF), attn_round)
        gat_ref[at, :] = grad_q
        return 0

    lax.fori_loop(0, blocks, mix, 0)

    dt_ref[...] = col_ref[...].T
    lower = lower_tri(rows)

    def unwind(i, sums):
        at = pl.ds(pl.multiple_of((blocks - 1 - i) * rows, rows), rows)
        after, bias_sum, rate_sum = sums
        slab = slice(plan.s_dt, plan.s_dt + 128)
        dt_step, rate, shifted, live = steps_of(plan, head_ref, proj_ref[at, slab])
        col_slab = dt_ref[at, :]
        grad_cum = row_ref[at, :] - dt_step * col_slab
        grad_decay = dot_tn(lower, grad_cum, EXACT) + after
        grad_dt = jnp.where(live, (col_slab - rate * grad_decay) * sigmoid(shifted), 0.0)
        z_part = ga_ref[at, slab].astype(F32)
        ga_ref[at, slab] = (jnp.where(lane < off, z_part, 0.0) + grad_dt).astype(BF)
        return (
            after + jnp.sum(grad_cum, axis=0, keepdims=True),
            bias_sum + jnp.sum(grad_dt, axis=0, keepdims=True),
            rate_sum + jnp.sum(grad_decay * (-dt_step * rate), axis=0, keepdims=True),
        )

    blank = jnp.zeros((1, 128), F32)
    _, bias_sum, rate_sum = lax.fori_loop(0, blocks, unwind, (blank, blank, blank))

    def finish(b, sums):
        low = pl.multiple_of(b * rows, rows)
        at = pl.ds(low, rows)
        pre = pre_ref[at, :]
        grad_act = gact_ref[at, :]
        grad_x = grad_act[:, plan.o_x :] + skip * gy_ref[at, :]
        grad_act = jnp.concatenate([grad_act[:, : plan.o_x], grad_x], axis=1)
        grad_pre = grad_act * silu_grad(pre, sigmoid(pre))
        gext_ref[at, :] = grad_pre
        pos = linked_rows(plan, lengths_ref, low)[1]
        ext = ext_ref[pl.ds(low, rows + 8), :]
        new = []
        for k in range(KCONV):
            step = KCONV - 1 - k
            moved = ext[8 - step : 8 - step + rows] * (pos >= step).astype(F32)
            new.append(sums[k] + jnp.sum(grad_pre * moved, axis=0, keepdims=True))
        new.append(sums[KCONV] + jnp.sum(grad_pre, axis=0, keepdims=True))
        grad_q = gat_ref[at, :]
        grad_k = gk_ref[at, :]
        both = turn(jnp.where(lane < HDIM, grad_q, grad_k), cos_ref[at, :], -sin_ref[at, :])
        ga_ref[at, plan.o_q :] = both.astype(BF)
        return tuple(new)

    blank = jnp.zeros((1, plan.conv), F32)
    g_taps = lax.fori_loop(0, blocks, finish, (blank,) * (KCONV + 1))

    def close(b, total):
        low = pl.multiple_of(b * rows, rows)
        at = pl.ds(low, rows)
        ext = gext_ref[pl.ds(low, rows + 8), :]
        index = lax.broadcasted_iota(jnp.int32, (rows, 1), 0) + low
        grad_conv = jnp.zeros((rows, plan.conv), F32)
        for k in range(KCONV):
            step = KCONV - 1 - k
            later = index + step
            fits = (later - first_rows(lengths_ref, later) >= step).astype(F32)
            grad_conv = grad_conv + taps[k] * (ext[step : step + rows] * fits)
        ga_ref[at, : plan.conv] = grad_conv.astype(BF)
        v_part = jnp.where(in_v, gv_ref[at, :], 0.0)
        if plan.s_v < plan.conv:
            v_part = v_part + jnp.where(in_v, 0.0, grad_conv[:, plan.s_v : plan.s_v + 128])
        ga_ref[at, plan.s_v : plan.s_v + 128] = v_part.astype(BF)
        partial = dot_nt(ga_ref[at, :], w_ref[:, : plan.a_w])
        normed = rms_forward(x_ref[at, :].astype(F32))[0]
        keep, give = split_rows(plan, partial, t_id)
        out = pl.ds(pl.multiple_of(b * plan.half, plan.half), plan.half)
        keep_ref[out, :] = keep.astype(BF)
        give_ref[out, :] = give.astype(BF)
        return total + jnp.sum(partial * normed, axis=0, keepdims=True)

    g_gain = lax.fori_loop(0, blocks, close, jnp.zeros((1, width), F32))

    def rows_at(entries, count):
        index = lax.broadcasted_iota(jnp.int32, (128, 1), 0)
        total = jnp.zeros((128, count), F32)
        for i, value in entries:
            high = value.astype(BF).astype(F32)
            total = jnp.where(index == row + i, high, total)
            total = jnp.where(index == row + plan.n_small + i, value - high, total)
        return total

    lane_d = lanes(width) % plan.d_loc
    head_vals = jnp.zeros((1, width), F32)
    for j in range(heads):
        picks = (
            jnp.sum(jnp.where(lane == off + j, bias_sum, 0.0), axis=1, keepdims=True),
            jnp.sum(jnp.where(lane == off + j, rate_sum, 0.0), axis=1, keepdims=True),
            jnp.sum(jnp.where(lane_w // HDIM == j, skip_sum, 0.0), axis=1, keepdims=True),
        )
        for i in range(3):
            head_vals = jnp.where(lane_d == i * heads + j, picks[i], head_vals)
    direct = rows_at([(0, g_gain), (1, gain2_ref[...]), (plan.n_small - 1, head_vals)], width)
    selected = [
        rows_at([(2 + k, g_taps[k][:, : 2 * NSTATE]) for k in range(KCONV + 1)], 2 * NSTATE)
    ]
    for k in range(KCONV + 2):
        source = g_taps[k][:, plan.o_x :] if k <= KCONV else g_norm_gain
        selected.append(
            rows_at(
                [
                    (KCONV + 3 + j, jnp.where(lane_w // HDIM == j, source, 0.0))
                    for j in range(heads)
                ],
                wide,
            )
        )
    selected = jnp.concatenate(selected, axis=1).astype(BF)
    small = direct.T + dot_nt(sel_ref[...], selected)
    small_ref[...] = small
    chunk = 256

    def weigh(i, _):
        part = pl.ds(pl.multiple_of(i * chunk, chunk), chunk)
        pack_ref[part, : plan.a_w] = dot_tn(norm_ref[:, part], ga_ref[...]).astype(BF)
        slab = slice(plan.s_dt, plan.s_dt + 128)
        pack_ref[part, slab] = jnp.where(
            lane < row, pack_ref[part, slab].astype(F32), small_ref[part, :]
        ).astype(BF)
        pack_ref[part, plan.o_mo : plan.o_mo + wide] = dot_tn(
            gs_ref[:, part], ni_ref[...]
        ).astype(BF)
        slab = slice(plan.s_ao, plan.s_ao + 128)
        attn = dot_tn(got_ref[:, part], attn_ref[...])
        if plan.off:
            attn = jnp.where(in_v, attn, pack_ref[part, slab].astype(F32))
        pack_ref[part, slab] = attn.astype(BF)
        return 0

    lax.fori_loop(0, width // chunk, weigh, 0)


def call(kernel, plan, outs, scratch, scalars, arrays):
    smem = pl.BlockSpec(memory_space=pltpu.SMEM)
    vmem = pl.BlockSpec(memory_space=pltpu.VMEM)
    return pl.pallas_call(
        lambda *refs: kernel(plan, *refs),
        out_shape=[jax.ShapeDtypeStruct(shape, kind) for shape, kind in outs],
        in_specs=[smem] * len(scalars) + [vmem] * len(arrays),
        out_specs=[vmem] * len(outs),
        scratch_shapes=[pltpu.VMEM(shape, kind) for shape, kind in scratch],
        compiler_params=pltpu.CompilerParams(vmem_limit_bytes=48 << 20),
    )(*scalars, *arrays)


def per_device(
    inputs,
    seq_lengths,
    norm_gains,
    mamba_in,
    dt_proj,
    bc_proj,
    mamba_chan,
    bc_conv,
    head_params,
    query_proj,
    kv_proj,
    attn_out,
    mamba_out,
    mlp_in,
    mlp_out,
    out_grad,
):
    n_f = lax.axis_size("fsdp")
    n_c = lax.axis_size("context")
    c_id = lax.axis_index("context")
    t_id = lax.axis_index("tensor")
    shards = n_f * n_c
    rows = inputs.shape[0]
    group = rows * n_c
    half = rows // 2
    d_loc = mamba_in.shape[0]
    width = d_loc * shards
    heads_t = head_params.shape[1]
    heads = -(-heads_t // n_c)
    heads_pad = heads * n_c
    q_t = query_proj.shape[1] // HDIM
    ff = mlp_in.shape[2]
    cc = bc_conv.shape[1]
    mc = mamba_chan.shape[1]
    plan = Plan(group, rows, width, d_loc, heads, 2 * heads_t * HDIM, cc, mc)
    chan = plan.chan
    bc_w = 2 * NSTATE
    o_s, o_end, n_small, p_w = plan.o_s, plan.o_end, plan.n_small, plan.p_w

    def by_context(array, axis, count, size):
        padded = pad_to(array, axis, count * n_c * size)
        shape = padded.shape[:axis] + (n_c, count * size) + padded.shape[axis + 1 :]
        return jnp.moveaxis(padded.reshape(shape), axis, 0)

    inner_ctx = by_context(mamba_in, 2, heads, HDIM)
    query_ctx = by_context(query_proj, 1, 1, HDIM)
    dt_ctx = by_context(dt_proj, 1, heads, 1)
    chan_ctx = pad_to(jnp.swapaxes(by_context(mamba_chan, 0, heads, 1), 1, 2), 1, d_loc)
    mo_ctx = jnp.swapaxes(by_context(mamba_out, 0, heads, HDIM), 1, 2)
    ao_ctx = jnp.swapaxes(by_context(attn_out, 0, 1, HDIM), 1, 2)

    def everywhere(array):
        return jnp.broadcast_to(array[None], (n_c,) + array.shape)

    pieces = [
        (0, everywhere(bc_proj)),
        (plan.o_x, inner_ctx[:, :, 1]),
        (plan.o_v, everywhere(kv_proj[:, 1])),
        (plan.o_z, inner_ctx[:, :, 0]),
        (plan.o_dt, dt_ctx),
        (
            plan.o_s,
            everywhere(jnp.concatenate([norm_gains.T, pad_to(bc_conv.T, 0, d_loc)], axis=1)),
        ),
        (plan.o_s + KCONV + 3, chan_ctx),
        (plan.o_q, query_ctx),
        (plan.o_k, everywhere(kv_proj[:, 0])),
        (plan.o_mo, mo_ctx),
        (plan.o_ao, ao_ctx),
        (plan.p_w, None),
    ]
    columns = []
    filled = 0
    for start, piece in pieces:
        if start > filled:
            columns.append(jnp.zeros((n_c, d_loc, start - filled), BF))
        if piece is not None:
            columns.append(piece)
            filled = start + piece.shape[2]
    pack = jnp.concatenate(columns, axis=2)

    mine = lax.dynamic_slice_in_dim(inputs, t_id * half, half, 0)
    part = exchange(pack, "context").reshape(n_c * d_loc, p_w)
    got_in = spread_async(mine, "context")
    w_all = spread(part, "fsdp").reshape(width, p_w)
    rows_in = join_pair(got_in, swap_pair(got_in), t_id, 1).reshape(group, width)
    part_mi = spread_async(mlp_in.reshape(d_loc, 2 * ff), "context")
    part_mo = spread_async(mlp_out.T, "context")
    w_mi = plane_gather(part_mi.reshape(n_c * d_loc, 2 * ff)).reshape(width, 2 * ff)
    w_mo = plane_gather(part_mo.reshape(n_c * d_loc, ff)).reshape(width, ff)

    starts = jnp.cumsum(seq_lengths[0]) - seq_lengths[0]
    row_ids = jnp.arange(group, dtype=jnp.int32)
    inside = row_ids[:, None] >= starts[None, :]
    positions = row_ids - jnp.max(jnp.where(inside, starts[None, :], 0), axis=1)
    freqs = jnp.power(ROPE_BASE, -jnp.arange(HDIM // 2).astype(F32) * (2.0 / HDIM))
    angles = positions.astype(F32)[:, None] * jnp.concatenate([freqs] * 4)[None, :]
    cosine = jnp.cos(angles)
    sine = jnp.sin(angles)
    head_vec = lax.dynamic_slice_in_dim(
        pad_to(head_params, 1, heads_pad), c_id * heads, heads, 1
    )
    feature = jnp.arange(width, dtype=jnp.int32)[:, None]
    place = feature % d_loc
    shard = feature // d_loc
    lane = jnp.arange(plan.wide, dtype=jnp.int32)[None, :] % HDIM
    sel = [(place < cc) & (shard * cc + place == jnp.arange(bc_w, dtype=jnp.int32)[None, :])]
    for k in range(KCONV + 2):
        sel.append((place < mc) & (shard * mc + place == k * HDIM + lane))
    sel = jnp.concatenate(sel, axis=1).astype(BF)
    scalars = (seq_lengths, head_vec, t_id.reshape(1))
    slab_w = 2 * width + 128
    part_rows = n_c * half
    keep, give, gain_two, taps, norm, proj, pre, cum, ssm, attn, lse, qk, kq = call(
        forward_kernel,
        plan,
        [
            ((part_rows, slab_w), BF),
            ((part_rows, slab_w), BF),
            ((1, width), F32),
            ((8, plan.conv), F32),
            ((group, width), BF),
            ((group, plan.a_w), F32),
            ((group, plan.conv), F32),
            ((group, 128), F32),
            ((group, plan.wide), F32),
            ((group, 128), BF),
            ((group, 128), F32),
            ((group, 128), BF),
            ((group, 128), BF),
        ],
        [((group, plan.conv), BF), ((group + 8, plan.conv), F32), ((group, 128), F32)],
        scalars,
        (rows_in, w_all, sel, cosine, sine),
    )
    gain_mlp = gain_two[0]

    def pair_parts(values, lead):
        parts = values.reshape(lead + (2, half) + values.shape[1:])
        keep = lax.dynamic_index_in_dim(parts, t_id, len(lead), False)
        return keep, lax.dynamic_index_in_dim(parts, 1 - t_id, len(lead), False)

    def pair_sum(values, lead):
        keep, give = pair_parts(values, lead)
        return keep + swap_pair(give.astype(BF)).astype(F32)

    def pair_add(keep, give):
        return (keep.astype(F32) + swap_pair(give).astype(F32)).astype(BF)

    summed = pair_add(keep, give).reshape(n_c, half, slab_w)
    both = jnp.sum(exchange(summed, "context").astype(F32), axis=0)
    squares = jnp.sum(both[:, 2 * width : 2 * width + 4], axis=1, keepdims=True)
    scale_own = lax.rsqrt(squares / plan.total + NORM_EPS)
    mamba_own = both[:, :width]
    in_own = mine.astype(F32)
    residual = in_own + scale_own * mamba_own + both[:, width : 2 * width]

    normed_two, inv_two = rms_forward(residual)
    norm_two_own = (normed_two * gain_mlp[None, :]).astype(BF)
    norm_two = join_pair(norm_two_own, swap_pair(norm_two_own), t_id, 0).reshape(rows, width)
    stacked = jnp.concatenate([norm_two, out_grad], axis=0)
    first = dot(norm_two, w_mi)
    gate_val = first[:, :ff]
    up_val = first[:, ff:]
    grad_act = dot(out_grad, w_mo)
    gate_sig = sigmoid(gate_val)
    gate_act = gate_val * gate_sig
    mlp_act = (gate_act * up_val).astype(BF)
    grad_gate = (grad_act * up_val * silu_grad(gate_val, gate_sig)).astype(BF)
    grad_up = (grad_act * gate_act).astype(BF)
    blank = jnp.zeros((rows, ff), BF)
    mixed = jnp.concatenate(
        [
            jnp.concatenate([grad_gate, grad_up, blank], axis=1),
            jnp.concatenate([blank, blank, mlp_act], axis=1),
        ],
        axis=0,
    )
    grad_two = pair_sum(dot_nt(mixed[:rows, : 2 * ff], w_mi), ())
    top_own = lax.dynamic_slice_in_dim(out_grad, t_id * half, half, 0).astype(F32)
    g_gain_mlp = jnp.sum(grad_two * normed_two, axis=0)
    grad_res = top_own + rms_backward(grad_two, normed_two, inv_two, gain_mlp)
    grad_rs_own = jnp.sum(grad_res * mamba_own, axis=1, keepdims=True)
    factor = split(jnp.concatenate([grad_rs_own, scale_own], axis=1), 2)
    got = spread(jnp.concatenate([grad_res.astype(BF), factor], axis=1), "context")
    got = join_pair(got, swap_pair(got), t_id, 1).reshape(group, -1)
    block = n_c * d_loc

    def mlp_block(target, part):
        low = target * block + part * (block // 2)
        cols = lax.dynamic_slice_in_dim(stacked, low, block // 2, 1)
        return dot_tn(cols, mixed)

    own = plane_reduce(mlp_block)
    own = reduce_async(own.reshape(n_c, d_loc, 3 * ff), "context")
    out_mi = own[:, : 2 * ff].reshape(d_loc, 2, ff)
    out_mo = own[:, 2 * ff :].T

    keep, give, g_pack = call(
        backward_kernel,
        plan,
        [((part_rows, width), BF), ((part_rows, width), BF), ((width, p_w), BF)],
        [
            ((group, plan.conv), BF),
            ((group + 8, plan.conv), F32),
            ((group, width), BF),
            ((group, plan.wide), BF),
            ((group, plan.wide), F32),
            ((group, plan.a_w), BF),
            ((group, plan.conv), F32),
            ((group + 8, plan.conv), F32),
            ((group, 128), F32),
            ((group, 128), F32),
            ((group, 128), F32),
            ((group, 128), F32),
            ((128, group), F32),
            ((128, group), F32),
            ((128, group), F32),
            ((width, 128), F32),
            ((group, 128), F32),
        ],
        scalars,
        (
            rows_in, w_all, sel, cosine, sine, taps, norm, proj, pre, cum, ssm, attn, lse, qk, kq, got,
            g_gain_mlp[None],
        ),
    )
    mlp_act, residual, keep = lax.optimization_barrier((mlp_act, residual, keep))
    out_own = (residual + pair_sum(dot_nt(mlp_act, w_mo), ())).astype(BF)
    partial = pair_add(keep, give).reshape(n_c, half, width)
    grad_one = reduce_async(partial, "context")
    gain_mix = w_all[:, o_s].astype(F32)
    normed_own, inv_own = rms_forward(in_own)
    grad_in_own = grad_res + rms_backward(grad_one, normed_own, inv_own, gain_mix)
    output = join_pair(out_own, swap_pair(out_own), t_id, 0).reshape(rows, width)
    input_grad = join_pair(grad_in_own, swap_pair(grad_in_own), t_id, 0).reshape(rows, width)

    got = exchange(g_pack.reshape(n_f, block, p_w), "fsdp")
    got = jnp.sum(got.astype(F32), axis=0)
    g_small = fuse(got[:, o_s:o_end], 2, n_small)
    g_pack = jnp.concatenate(
        [got[:, :o_s].astype(BF), split(g_small, 2, False), got[:, o_end:].astype(BF)], axis=1
    )
    g_a = exchange(g_pack.reshape(n_c, d_loc, p_w), "context").astype(F32)

    def joined(low, size, count):
        moved = jnp.moveaxis(g_a[:, :, low : low + size], 0, 1).reshape(d_loc, n_c * size)
        return moved[:, : count]

    out_inner = jnp.stack(
        [
            joined(plan.o_z, chan, heads_t * HDIM),
            joined(plan.o_x, chan, heads_t * HDIM),
        ],
        axis=1,
    )
    out_query = joined(plan.o_q, HDIM, q_t * HDIM)
    out_dt = joined(plan.o_dt, heads, heads_t)
    out_kv = jnp.stack(
        [
            jnp.sum(g_a[:, :, plan.o_k : plan.o_k + HDIM], axis=0),
            jnp.sum(g_a[:, :, plan.o_v : plan.o_v + HDIM], axis=0),
        ],
        axis=1,
    )
    out_mout = joined(plan.o_mo, chan, heads_t * HDIM).T
    out_aout = joined(plan.o_ao, HDIM, q_t * HDIM).T
    g_small = fuse(g_a[:, :, o_s:o_end], 2, n_small)
    tail = jnp.concatenate([g_a[:, :, :bc_w], g_small[:, :, : KCONV + 3]], axis=2)
    tail = jnp.sum(tail, axis=0)
    tail = tail + swap_pair(tail)
    out_bc = tail[:, :bc_w]
    out_gains = tail[:, bc_w : bc_w + 2].T
    out_convbc = tail[:cc, bc_w + 2 :].T
    out_chan = jnp.swapaxes(g_small[:, :mc, KCONV + 3 : KCONV + 3 + heads], 1, 2)
    out_chan = out_chan.reshape(heads_pad, mc)[:heads_t]
    out_heads = g_small[:, : 3 * heads, n_small - 1].reshape(n_c, 3, heads)
    out_heads = jnp.swapaxes(out_heads, 0, 1).reshape(3, heads_pad)[:, :heads_t]

    return (
        output,
        input_grad,
        out_gains,
        out_inner,
        out_dt,
        out_bc,
        out_chan,
        out_convbc,
        out_heads,
        out_query,
        out_kv,
        out_aout,
        out_mout,
        out_mi,
        out_mo,
    )


def solution(mesh):
    both = ("fsdp", "context")
    rows = P(both, None)

    return jax.shard_map(
        per_device,
        mesh=mesh,
        in_specs=(
            rows,
            P("fsdp", None),
            P(None, both),
            P(both, None, "tensor"),
            P(both, "tensor"),
            rows,
            P("tensor", both),
            P(None, both),
            P(None, "tensor"),
            P(both, "tensor"),
            P(both, None, "tensor"),
            P("tensor", both),
            P("tensor", both),
            P(both, None, "tensor"),
            P("tensor", both),
            rows,
        ),
        out_specs=(
            rows,
            rows,
            P(None, both),
            P(both, None, "tensor"),
            P(both, "tensor"),
            rows,
            P("tensor", both),
            P(None, both),
            P(None, "tensor"),
            P(both, "tensor"),
            P(both, None, "tensor"),
            P("tensor", both),
            P("tensor", both),
            P(both, None, "tensor"),
            P("tensor", both),
        ),
        check_vma=False,
    )
```

```python
import jax
import jax.numpy as jnp
from jax import lax
from jax.experimental import pallas as pl
from jax.experimental.pallas import tpu as pltpu
from jax.sharding import PartitionSpec as P


HDIM = 64
NSTATE = 128
KCONV = 4
NORM_EPS = 1e-05
ROPE_BASE = 100000000000.0
EXACT = lax.Precision.HIGHEST
BF = jnp.bfloat16
F32 = jnp.float32


def swap_pair(block):
    return lax.ppermute(block, "tensor", [(0, 1), (1, 0)])


def join_pair(own, other, place, axis):
    low = jnp.where(place == 0, own, other)
    high = jnp.where(place == 0, other, own)
    return jnp.stack([low, high], axis=axis)


def exchange(blocks, axis):
    return lax.all_to_all(blocks, axis, 0, 0, tiled=True)


def spread(block, axis):
    return exchange(jnp.broadcast_to(block[None], (lax.axis_size(axis),) + block.shape), axis)


def hops(axis):
    count = lax.axis_size(axis)
    place = lax.axis_index(axis)
    for step in range(1, count):
        route = [(i, (i + step) % count) for i in range(count)]
        yield route, (place + step) % count, (place - step) % count


def spread_async(block, axis):
    count = lax.axis_size(axis)
    got = [(lax.ppermute(block, axis, route), source) for route, _, source in hops(axis)]
    if block.size > 1 << 18:
        whole = jnp.zeros((count,) + block.shape, block.dtype)
        whole = lax.dynamic_update_index_in_dim(whole, block, lax.axis_index(axis), 0)
        for piece, source in got:
            whole = lax.dynamic_update_index_in_dim(whole, piece, source, 0)
        return whole
    place = lax.axis_index(axis)
    pieces = [block] + [piece for piece, _ in got]
    return jnp.stack(
        [lax.select_n((place - i) % count, *pieces) for i in range(count)], axis=0
    )


def reduce_async(blocks, axis):
    got = [
        lax.ppermute(lax.dynamic_index_in_dim(blocks, target, 0, False), axis, route)
        for route, target, _ in hops(axis)
    ]
    total = lax.dynamic_index_in_dim(blocks, lax.axis_index(axis), 0, False).astype(F32)
    for piece in got:
        total = total + piece.astype(F32)
    return total


def beside(step):
    return [(i, i ^ step) for i in range(4)]


def plane_gather(block):
    if lax.axis_size("fsdp") != 4:
        return spread_async(block, "fsdp")
    half = block.shape[0] // 2
    place = lax.axis_index("fsdp")
    near = lax.ppermute(block, "fsdp", beside(1))
    side = lax.ppermute(block, "fsdp", beside(2))
    far_top = lax.ppermute(side[:half], "fsdp", beside(1))
    far_low = lax.ppermute(near[half:], "fsdp", beside(2))
    whole = jnp.zeros((4, 2, half) + block.shape[1:], block.dtype)
    parts = ((block, place), (near, place ^ 1), (side, place ^ 2))
    for piece, index in parts:
        piece = piece.reshape((1, 2, half) + block.shape[1:])
        whole = lax.dynamic_update_slice(whole, piece, (index, 0, 0, 0))
    for row, piece in enumerate((far_top, far_low)):
        whole = lax.dynamic_update_slice(whole, piece[None, None], (place ^ 3, row, 0, 0))
    return whole


def plane_reduce(make):
    def whole(target):
        return jnp.concatenate([make(target, 0), make(target, 1)], axis=0)

    if lax.axis_size("fsdp") != 4:
        sent = [(route, whole(target).astype(BF)) for route, target, _ in hops("fsdp")]
        own = whole(lax.axis_index("fsdp"))
        for route, piece in sent:
            own = own + lax.ppermute(piece, "fsdp", route).astype(F32)
        return own.astype(BF)
    place = lax.axis_index("fsdp")
    got_side = lax.ppermute(make(place ^ 3, 0).astype(BF), "fsdp", beside(1))
    got_near = lax.ppermute(make(place ^ 3, 1).astype(BF), "fsdp", beside(2))
    near_top = lax.ppermute(make(place ^ 1, 0).astype(BF), "fsdp", beside(1))
    side_low = lax.ppermute(make(place ^ 2, 1).astype(BF), "fsdp", beside(2))
    own_top = make(place, 0).astype(BF)
    own_low = make(place, 1).astype(BF)
    side_top = make(place ^ 2, 0).astype(BF)
    near_low = make(place ^ 1, 1).astype(BF)
    side_top = (side_top.astype(F32) + got_side.astype(F32)).astype(BF)
    near_low = (near_low.astype(F32) + got_near.astype(F32)).astype(BF)
    side_top = lax.ppermute(side_top, "fsdp", beside(2))
    near_low = lax.ppermute(near_low, "fsdp", beside(1))
    top = own_top.astype(F32) + near_top.astype(F32) + side_top.astype(F32)
    low = own_low.astype(F32) + near_low.astype(F32) + side_low.astype(F32)
    return jnp.concatenate([top, low], axis=0).astype(BF)


def sigmoid(values):
    return 1.0 / (1.0 + jnp.exp(-values))


def silu_grad(values, sigma):
    return sigma * (1.0 + values * (1.0 - sigma))


def rms_forward(values):
    inv_rms = lax.rsqrt(jnp.mean(values * values, axis=-1, keepdims=True) + NORM_EPS)
    return values * inv_rms, inv_rms


def rms_backward(grad_out, normed, inv_rms, gain_vec):
    grad_normed = grad_out * gain_vec[None, :]
    return inv_rms * (grad_normed - normed * jnp.mean(grad_normed * normed, axis=-1, keepdims=True))


def dot(left, right, exact=None):
    return lax.dot_general(
        left, right, (((1,), (0,)), ((), ())), precision=exact, preferred_element_type=F32
    )


def dot_nt(left, right, exact=None):
    return lax.dot_general(
        left, right, (((1,), (1,)), ((), ())), precision=exact, preferred_element_type=F32
    )


def dot_tn(left, right, exact=None):
    return lax.dot_general(
        left, right, (((0,), (0,)), ((), ())), precision=exact, preferred_element_type=F32
    )


def pad_to(array, axis, size):
    if array.shape[axis] == size:
        return array
    widths = [(0, 0)] * array.ndim
    widths[axis] = (0, size - array.shape[axis])
    return jnp.pad(array, widths)


def ceil_to(value, unit):
    return -(-value // unit) * unit


def split(values, pieces, wide=True):
    parts = []
    for _ in range(pieces):
        high = lax.reduce_precision(values, 8, 7)
        parts.append(high.astype(BF))
        values = values - high
    joined = jnp.concatenate(parts, axis=-1)
    return pad_to(joined, joined.ndim - 1, 128) if wide else joined


class Plan:
    def __init__(self, group, rows, width, d_loc, heads, total, cc, mc):
        self.group, self.rows, self.width, self.d_loc = group, rows, width, d_loc
        self.heads, self.total, self.cc, self.mc = heads, total, cc, mc
        self.half = rows // 2
        self.chan = heads * HDIM
        self.wide = ceil_to(self.chan, 128)
        self.off = self.chan % 128
        self.conv = 2 * NSTATE + self.wide
        self.o_x = 2 * NSTATE
        self.o_v = self.o_x + self.chan
        self.o_z = ceil_to(self.o_v + HDIM, 128)
        self.o_dt = self.o_z + self.chan
        self.o_s = self.o_dt + heads
        self.n_small = KCONV + 4 + heads
        self.o_end = self.o_s + 2 * self.n_small
        self.o_q = ceil_to(self.o_end, 128)
        self.o_k = self.o_q + HDIM
        self.a_w = self.o_q + 2 * HDIM
        self.o_mo = self.a_w
        self.o_ao = self.a_w + self.chan
        self.p_w = ceil_to(self.o_ao + HDIM, 128)
        self.s_v = self.o_v - self.off
        self.s_dt = self.o_dt - self.off
        self.s_ao = self.o_ao - self.off
        self.row = self.off + heads


def lanes(count):
    return lax.broadcasted_iota(jnp.int32, (1, count), 1)


def first_rows(lengths_ref, index):
    start = jnp.zeros_like(index)
    edge = jnp.int32(0)
    for i in range(lengths_ref.shape[1] - 1):
        edge = edge + lengths_ref[0, i]
        start = jnp.where(index >= edge, edge, start)
    return start


def head_row(plan, head_ref, which):
    lane = lanes(128)
    row = jnp.zeros((1, 128), F32)
    for j in range(plan.heads):
        row = jnp.where(lane == plan.off + j, head_ref[which, j], row)
    return row


def head_wide(plan, values):
    lane = lanes(plan.wide)
    row = jnp.zeros((1, plan.wide), F32)
    for j in range(plan.heads):
        row = jnp.where(lane // HDIM == j, values[j], row)
    return row


def steps_of(plan, head_ref, slab):
    lane = lanes(128)
    live = (lane >= plan.off) & (lane < plan.row)
    shifted = jnp.where(live, slab + head_row(plan, head_ref, 0), 0.0)
    soft = jnp.maximum(shifted, 0.0) + jnp.log1p(jnp.exp(-jnp.abs(shifted)))
    dt_step = jnp.where(live, soft, 0.0)
    rate = jnp.where(live, jnp.exp(head_row(plan, head_ref, 1)), 0.0)
    return dt_step, rate, shifted, live


def small_rows(plan, w_ref, sel_ref):
    slab = w_ref[:, plan.s_dt : plan.s_dt + 128]
    turned = slab.astype(F32).T
    picked = dot_tn(slab, sel_ref[...])
    row = plan.row
    lane = lanes(plan.wide)
    taps = []
    for k in range(KCONV + 2):
        low = 2 * NSTATE + k * plan.wide
        piece = jnp.zeros((1, plan.wide), F32)
        for j in range(plan.heads):
            at = row + KCONV + 3 + j
            piece = jnp.where(lane // HDIM == j, picked[at : at + 1, low : low + plan.wide], piece)
        if k <= KCONV:
            piece = jnp.concatenate(
                [picked[row + 2 + k : row + 3 + k, : 2 * NSTATE], piece], axis=1
            )
        taps.append(piece)
    return turned[row : row + 1], turned[row + 1 : row + 2], taps


def lower_tri(group):
    return (
        lax.broadcasted_iota(jnp.int32, (group, group), 0)
        >= lax.broadcasted_iota(jnp.int32, (group, group), 1)
    ).astype(F32)


def linked_rows(plan, lengths_ref, low):
    index = lax.broadcasted_iota(jnp.int32, (plan.rows, 1), 0) + low
    start = first_rows(lengths_ref, index)
    cols = lanes(plan.group)
    return (cols <= index) & (cols >= start), index - start


def turn(values, cosine, sine):
    lane = lanes(2 * HDIM)
    moved = jnp.where(
        lane % HDIM < HDIM // 2, -pltpu.roll(values, 2 * HDIM - HDIM // 2, 1),
        pltpu.roll(values, HDIM // 2, 1),
    )
    return values * cosine + moved * sine


def split_rows(plan, values, t_id):
    low = values[: plan.half]
    high = values[plan.half :]
    return jnp.where(t_id == 0, low, high), jnp.where(t_id == 0, high, low)


def views(plan, trig_ref, wide_ref, thin_ref):
    def part(ref, low, size):
        return ref.at[:, low : low + size]

    wide = plan.wide
    return (
        part(trig_ref, 0, 128),
        part(trig_ref, 128, 128),
        part(wide_ref, 0, wide),
        part(wide_ref, wide, 128),
        part(wide_ref, wide + 128, 128),
        part(thin_ref, 0, 128),
        part(thin_ref, 128, 128),
        part(thin_ref, 256, 128),
    )


def forward_kernel(
    plan, lengths_ref, head_ref, t_ref, x_ref, w_ref, sel_ref, trig_ref,
    keep_ref, give_ref, gain1_ref, gain2_ref, taps_ref, norm_ref, proj_ref, pre_ref, wide_ref, thin_ref,
    act_ref, ext_ref, dt_ref,
):
    cos_ref, sin_ref, ssm_ref, cum_ref, lse_ref, attn_ref, qk_ref, kq_ref = views(
        plan, trig_ref, wide_ref, thin_ref
    )
    rows, group, wide = plan.rows, plan.group, plan.wide
    gain, gain_two, taps = small_rows(plan, w_ref, sel_ref)
    gain1_ref[...] = gain
    gain2_ref[...] = gain_two
    for k in range(KCONV + 1):
        taps_ref[k : k + 1, :] = taps[k]
    taps_ref[KCONV + 1 : KCONV + 2, plan.o_x :] = taps[KCONV + 1]
    blocks = group // rows
    t_id = t_ref[0]
    ext_ref[0:8, :] = jnp.zeros((8, plan.conv), F32)

    lower = lower_tri(rows)

    def project(b, before):
        at = pl.ds(pl.multiple_of(b * rows, rows), rows)
        values = x_ref[at, :].astype(F32)
        normed = rms_forward(values)[0]
        norm = (normed * gain).astype(BF)
        norm_ref[at, :] = norm
        proj = dot(norm, w_ref[:, : plan.a_w])
        proj_ref[at, :] = proj
        ext_ref[pl.ds(pl.multiple_of(b * rows + 8, 8), rows), :] = (
            proj[:, : plan.conv].astype(BF).astype(F32)
        )
        rot = turn(proj[:, plan.o_q :], cos_ref[at, :], sin_ref[at, :])
        qk_ref[at, :] = rot.astype(BF)
        kq_ref[at, :] = pltpu.roll(rot, HDIM, 1).astype(BF)
        dt_step, rate, _, _ = steps_of(plan, head_ref, proj[:, plan.s_dt : plan.s_dt + 128])
        dt_ref[at, :] = dt_step
        cum = dot(lower, -dt_step * rate, EXACT) + before
        cum_ref[at, :] = cum
        return cum[rows - 1 : rows]

    lax.fori_loop(0, blocks, project, jnp.zeros((1, 128), F32))
    cum_t = cum_ref[...].T
    dt_t = dt_ref[...].T

    def convolve(b, _):
        low = pl.multiple_of(b * rows, rows)
        at = pl.ds(low, rows)
        pos = linked_rows(plan, lengths_ref, low)[1]
        ext = ext_ref[pl.ds(low, rows + 8), :]
        total = jnp.broadcast_to(taps[KCONV], (rows, plan.conv))
        for k in range(KCONV):
            step = KCONV - 1 - k
            total = total + taps[k] * (ext[8 - step : 8 - step + rows] * (pos >= step).astype(F32))
        pre_ref[at, :] = total
        act_ref[at, :] = (total * sigmoid(total)).astype(BF)
        return 0

    lax.fori_loop(0, blocks, convolve, 0)

    lane_w = lanes(wide)
    lane = lanes(128)
    in_v = (lane >= plan.off) & (lane < plan.off + HDIM)
    b_all = act_ref[:, :NSTATE]
    x_all = act_ref[:, plan.o_x : plan.o_x + wide]
    v_all = jnp.where(in_v, proj_ref[:, plan.s_v : plan.s_v + 128], 0.0).astype(BF)
    k_all = kq_ref[...]
    skip = head_wide(plan, [head_ref[2, j] for j in range(plan.heads)])
    w_m = w_ref[:, plan.o_mo : plan.o_mo + wide]
    w_o = w_ref[:, plan.s_ao : plan.s_ao + 128]

    def mix(b, _):
        low = pl.multiple_of(b * rows, rows)
        at = pl.ds(low, rows)
        linked = linked_rows(plan, lengths_ref, low)[0]
        cross = dot_nt(act_ref[at, NSTATE : 2 * NSTATE], b_all)
        cum_b = cum_ref[at, :]
        core = jnp.zeros((rows, wide), F32)
        for j in range(plan.heads):
            col = cum_b[:, plan.off + j : plan.off + j + 1]
            gaps = jnp.where(linked, col - cum_t[plan.off + j : plan.off + j + 1], -1e30)
            mixing = jnp.exp(gaps) * cross * dt_t[plan.off + j : plan.off + j + 1]
            core = jnp.where(lane_w // HDIM == j, dot(mixing.astype(BF), x_all), core)
        pre = pre_ref[at, plan.o_x : plan.o_x + wide]
        ssm = core + skip * (pre * sigmoid(pre))
        ssm_ref[at, :] = ssm
        z_gate = proj_ref[at, plan.o_z : plan.o_z + wide].astype(BF).astype(F32)
        gated = jnp.where(lane_w < plan.chan, ssm * (z_gate * sigmoid(z_gate)), 0.0)
        norm_in = (gated * taps[KCONV + 1]).astype(BF)
        square = jnp.sum(gated * gated, axis=1, keepdims=True)
        high = square.astype(BF).astype(F32)
        square = jnp.where(
            lane == 2 * t_id, high, jnp.where(lane == 2 * t_id + 1, square - high, 0.0)
        )

        query = jnp.where(lane < HDIM, qk_ref[at, :].astype(F32), 0.0).astype(BF)
        scores = jnp.where(linked, dot_nt(query, k_all) * HDIM ** (-0.5), -1e30)
        top = jnp.max(scores, axis=1, keepdims=True)
        exps = jnp.exp(scores - top)
        total = jnp.sum(exps, axis=1, keepdims=True)
        values = dot((exps / total).astype(BF), v_all).astype(BF)
        attn_ref[at, :] = values
        lse_ref[at, :] = jnp.broadcast_to(top + jnp.log(total), (rows, 128))

        out = pl.ds(pl.multiple_of(b * plan.half, plan.half), plan.half)
        width = plan.width
        for start, piece in (
            (0, dot_nt(norm_in, w_m)),
            (width, dot_nt(values, w_o)),
            (2 * width, square),
        ):
            keep, give = split_rows(plan, piece, t_id)
            keep_ref[out, start : start + piece.shape[1]] = keep.astype(BF)
            give_ref[out, start : start + piece.shape[1]] = give.astype(BF)
        return 0

    lax.fori_loop(0, blocks, mix, 0)


def backward_kernel(
    plan, lengths_ref, head_ref, t_ref, x_ref, w_ref, sel_ref, trig_ref,
    taps_ref, norm_ref, proj_ref, pre_ref, wide_ref, thin_ref, mine_ref,
    other_ref, gain2_ref,
    keep_ref, give_ref, pack_ref,
    act_ref, ext_ref, gs_ref, ni_ref, gy_ref, ga_ref, gact_ref, gext_ref, gv_ref, gk_ref, gat_ref,
    row_ref, col_ref, dtt_ref, cumt_ref, small_ref, dt_ref, got_ref,
):
    cos_ref, sin_ref, ssm_ref, cum_ref, lse_ref, attn_ref, qk_ref, kq_ref = views(
        plan, trig_ref, wide_ref, thin_ref
    )
    rows, group, wide, width = plan.rows, plan.group, plan.wide, plan.width
    heads, off, row = plan.heads, plan.off, plan.row
    taps = [taps_ref[k : k + 1, :] for k in range(KCONV + 1)]
    blocks = group // rows
    t_id = t_ref[0]
    lane_w = lanes(wide)
    lane = lanes(128)
    in_v = (lane >= off) & (lane < off + HDIM)
    norm_gain = taps_ref[KCONV + 1 : KCONV + 2, plan.o_x :]
    w_m = w_ref[:, plan.o_mo : plan.o_mo + wide]
    w_o = w_ref[:, plan.s_ao : plan.s_ao + 128]
    ext_ref[0:8, :] = jnp.zeros((8, plan.conv), F32)
    gext_ref[group : group + 8, :] = jnp.zeros((8, plan.conv), F32)
    skip = head_wide(plan, [head_ref[2, j] for j in range(heads)])
    scale = HDIM ** (-0.5)

    cumt_ref[...] = cum_ref[...].T

    def gate(b, sums):
        at = pl.ds(pl.multiple_of(b * rows, rows), rows)
        for low, t_low in ((b * rows, 0), (b * rows + plan.half, 1)):
            half_at = pl.ds(pl.multiple_of(low, plan.half), plan.half)
            got_ref[half_at, :] = jnp.where(t_id == t_low, mine_ref[b], other_ref[b])
        grad_round = got_ref[at, :width]
        factor = got_ref[at, width : width + 128].astype(F32)
        grad_rs = factor[:, 0:1] + factor[:, 2:3]
        row_scale = factor[:, 1:2] + factor[:, 3:4]
        grad_scaled = (grad_round.astype(F32) * row_scale).astype(BF)
        gs_ref[at, :] = grad_scaled
        grad_in = jnp.where(lane_w < plan.chan, dot(grad_scaled, w_m), 0.0)
        gat_ref[at, :] = jnp.where(in_v, dot(grad_round, w_o), 0.0)
        z_gate = proj_ref[at, plan.o_z : plan.o_z + wide].astype(BF).astype(F32)
        z_gate = jnp.where(lane_w < plan.chan, z_gate, 0.0)
        z_sig = sigmoid(z_gate)
        silu_z = z_gate * z_sig
        ssm = ssm_ref[at, :]
        gated = ssm * silu_z
        ni_ref[at, :] = (gated * norm_gain).astype(BF)
        grad_gated = grad_in * norm_gain - gated * (
            grad_rs * row_scale * row_scale * row_scale / plan.total
        )
        grad_y = grad_gated * silu_z
        gy_ref[at, :] = grad_y
        grad_z = grad_gated * ssm * silu_grad(z_gate, z_sig)
        ga_ref[at, plan.o_z : plan.o_z + wide] = grad_z.astype(BF)
        pre = pre_ref[at, :]
        active = pre * sigmoid(pre)
        act_ref[at, :] = active.astype(BF)
        ext_ref[pl.ds(pl.multiple_of(b * rows + 8, 8), rows), :] = (
            proj_ref[at, : plan.conv].astype(BF).astype(F32)
        )
        gact_ref[at, plan.o_x : plan.o_x + wide] = jnp.zeros((rows, wide), F32)
        gact_ref[at, :NSTATE] = jnp.zeros((rows, NSTATE), F32)
        gv_ref[at, :] = jnp.zeros((rows, 128), F32)
        gk_ref[at, :] = jnp.zeros((rows, 128), F32)
        dt_ref[at, :] = steps_of(plan, head_ref, proj_ref[at, plan.s_dt : plan.s_dt + 128])[0]
        return (
            sums[0] + jnp.sum(grad_in * gated, axis=0, keepdims=True),
            sums[1]
            + jnp.sum(grad_y * active[:, plan.o_x : plan.o_x + wide], axis=0, keepdims=True),
        )

    blank = jnp.zeros((1, wide), F32)
    g_norm_gain, skip_sum = lax.fori_loop(0, blocks, gate, (blank, blank))
    col_ref[...] = jnp.zeros((128, group), F32)
    dtt_ref[...] = dt_ref[...].T

    b_all = act_ref[:, :NSTATE]
    x_all = act_ref[:, plan.o_x : plan.o_x + wide]
    v_all = jnp.where(in_v, proj_ref[:, plan.s_v : plan.s_v + 128], 0.0).astype(BF)
    k_all = kq_ref[...]

    def mix(b, _):
        low = pl.multiple_of(b * rows, rows)
        at = pl.ds(low, rows)
        linked = linked_rows(plan, lengths_ref, low)[0]
        c_blk = act_ref[at, NSTATE : 2 * NSTATE]
        cross = dot_nt(c_blk, b_all)
        cum_b = cum_ref[at, :]
        grad_y = gy_ref[at, :]
        grad_cross = jnp.zeros((rows, group), F32)
        grad_x = jnp.zeros((group, wide), F32)
        row_slab = jnp.zeros((rows, 128), F32)
        y_round = grad_y.astype(BF)
        for j in range(heads):
            col = cum_b[:, off + j : off + j + 1]
            dt_row = dtt_ref[off + j : off + j + 1, :]
            gaps = jnp.where(linked, col - cumt_ref[off + j : off + j + 1, :], -1e30)
            decays = jnp.exp(gaps)
            weights = decays * cross
            mine = lane_w // HDIM == j
            grad_mix = dot_nt(jnp.where(mine, grad_y, 0.0).astype(BF), x_all)
            flow = grad_mix * weights
            col_ref[off + j : off + j + 1, :] += jnp.sum(flow, axis=0, keepdims=True)
            row_slab = jnp.where(
                lane == off + j, jnp.sum(flow * dt_row, axis=1, keepdims=True), row_slab
            )
            grad_cross = grad_cross + grad_mix * (decays * dt_row)
            grad_x = jnp.where(mine, dot_tn((weights * dt_row).astype(BF), y_round), grad_x)
        row_ref[at, :] = row_slab
        grad_cross = grad_cross.astype(BF)
        gact_ref[:, plan.o_x : plan.o_x + wide] += grad_x
        gact_ref[at, NSTATE : 2 * NSTATE] = dot(grad_cross, b_all)
        gact_ref[:, :NSTATE] += dot_tn(grad_cross, c_blk)

        query = jnp.where(lane < HDIM, qk_ref[at, :].astype(F32), 0.0).astype(BF)
        scores = jnp.where(linked, dot_nt(query, k_all) * scale, -1e30)
        probs = jnp.exp(scores - lse_ref[at, 0:1])
        grad_attn = gat_ref[at, :]
        delta = jnp.sum(grad_attn * attn_ref[at, :].astype(F32), axis=1, keepdims=True)
        attn_round = grad_attn.astype(BF)
        grad_prob = dot_nt(attn_round, v_all)
        grad_scores = (probs * (grad_prob - delta)).astype(BF)
        grad_q = dot(grad_scores, k_all) * scale
        gk_ref[...] += dot_tn(grad_scores, kq_ref[at, :]) * scale
        gv_ref[...] += dot_tn(probs.astype(BF), attn_round)
        gat_ref[at, :] = grad_q
        return 0

    lax.fori_loop(0, blocks, mix, 0)

    dt_ref[...] = col_ref[...].T
    lower = lower_tri(rows)

    def unwind(i, sums):
        at = pl.ds(pl.multiple_of((blocks - 1 - i) * rows, rows), rows)
        after, bias_sum, rate_sum = sums
        slab = slice(plan.s_dt, plan.s_dt + 128)
        dt_step, rate, shifted, live = steps_of(plan, head_ref, proj_ref[at, slab])
        col_slab = dt_ref[at, :]
        grad_cum = row_ref[at, :] - dt_step * col_slab
        grad_decay = dot_tn(lower, grad_cum, EXACT) + after
        grad_dt = jnp.where(live, (col_slab - rate * grad_decay) * sigmoid(shifted), 0.0)
        z_part = ga_ref[at, slab].astype(F32)
        ga_ref[at, slab] = (jnp.where(lane < off, z_part, 0.0) + grad_dt).astype(BF)
        return (
            after + jnp.sum(grad_cum, axis=0, keepdims=True),
            bias_sum + jnp.sum(grad_dt, axis=0, keepdims=True),
            rate_sum + jnp.sum(grad_decay * (-dt_step * rate), axis=0, keepdims=True),
        )

    blank = jnp.zeros((1, 128), F32)
    _, bias_sum, rate_sum = lax.fori_loop(0, blocks, unwind, (blank, blank, blank))

    def finish(b, sums):
        low = pl.multiple_of(b * rows, rows)
        at = pl.ds(low, rows)
        pre = pre_ref[at, :]
        grad_act = gact_ref[at, :]
        grad_x = grad_act[:, plan.o_x :] + skip * gy_ref[at, :]
        grad_act = jnp.concatenate([grad_act[:, : plan.o_x], grad_x], axis=1)
        grad_pre = grad_act * silu_grad(pre, sigmoid(pre))
        gext_ref[at, :] = grad_pre
        pos = linked_rows(plan, lengths_ref, low)[1]
        ext = ext_ref[pl.ds(low, rows + 8), :]
        new = []
        for k in range(KCONV):
            step = KCONV - 1 - k
            moved = ext[8 - step : 8 - step + rows] * (pos >= step).astype(F32)
            new.append(sums[k] + jnp.sum(grad_pre * moved, axis=0, keepdims=True))
        new.append(sums[KCONV] + jnp.sum(grad_pre, axis=0, keepdims=True))
        grad_q = gat_ref[at, :]
        grad_k = gk_ref[at, :]
        both = turn(jnp.where(lane < HDIM, grad_q, grad_k), cos_ref[at, :], -sin_ref[at, :])
        ga_ref[at, plan.o_q :] = both.astype(BF)
        return tuple(new)

    blank = jnp.zeros((1, plan.conv), F32)
    g_taps = lax.fori_loop(0, blocks, finish, (blank,) * (KCONV + 1))

    def close(b, total):
        low = pl.multiple_of(b * rows, rows)
        at = pl.ds(low, rows)
        ext = gext_ref[pl.ds(low, rows + 8), :]
        index = lax.broadcasted_iota(jnp.int32, (rows, 1), 0) + low
        grad_conv = jnp.zeros((rows, plan.conv), F32)
        for k in range(KCONV):
            step = KCONV - 1 - k
            later = index + step
            fits = (later - first_rows(lengths_ref, later) >= step).astype(F32)
            grad_conv = grad_conv + taps[k] * (ext[step : step + rows] * fits)
        ga_ref[at, : plan.conv] = grad_conv.astype(BF)
        v_part = jnp.where(in_v, gv_ref[at, :], 0.0)
        if plan.s_v < plan.conv:
            v_part = v_part + jnp.where(in_v, 0.0, grad_conv[:, plan.s_v : plan.s_v + 128])
        ga_ref[at, plan.s_v : plan.s_v + 128] = v_part.astype(BF)
        partial = dot_nt(ga_ref[at, :], w_ref[:, : plan.a_w])
        normed = rms_forward(x_ref[at, :].astype(F32))[0]
        keep, give = split_rows(plan, partial, t_id)
        out = pl.ds(pl.multiple_of(b * plan.half, plan.half), plan.half)
        keep_ref[out, :] = keep.astype(BF)
        give_ref[out, :] = give.astype(BF)
        return total + jnp.sum(partial * normed, axis=0, keepdims=True)

    g_gain = lax.fori_loop(0, blocks, close, jnp.zeros((1, width), F32))

    def rows_at(entries, count):
        index = lax.broadcasted_iota(jnp.int32, (128, 1), 0)
        total = jnp.zeros((128, count), F32)
        for i, value in entries:
            high = value.astype(BF).astype(F32)
            total = jnp.where(index == row + i, high, total)
            total = jnp.where(index == row + plan.n_small + i, value - high, total)
        return total

    lane_d = lanes(width) % plan.d_loc
    head_vals = jnp.zeros((1, width), F32)
    for j in range(heads):
        picks = (
            jnp.sum(jnp.where(lane == off + j, bias_sum, 0.0), axis=1, keepdims=True),
            jnp.sum(jnp.where(lane == off + j, rate_sum, 0.0), axis=1, keepdims=True),
            jnp.sum(jnp.where(lane_w // HDIM == j, skip_sum, 0.0), axis=1, keepdims=True),
        )
        for i in range(3):
            head_vals = jnp.where(lane_d == i * heads + j, picks[i], head_vals)
    direct = rows_at([(0, g_gain), (1, gain2_ref[...]), (plan.n_small - 1, head_vals)], width)
    selected = [
        rows_at([(2 + k, g_taps[k][:, : 2 * NSTATE]) for k in range(KCONV + 1)], 2 * NSTATE)
    ]
    for k in range(KCONV + 2):
        source = g_taps[k][:, plan.o_x :] if k <= KCONV else g_norm_gain
        selected.append(
            rows_at(
                [
                    (KCONV + 3 + j, jnp.where(lane_w // HDIM == j, source, 0.0))
                    for j in range(heads)
                ],
                wide,
            )
        )
    selected = jnp.concatenate(selected, axis=1).astype(BF)
    small = direct.T + dot_nt(sel_ref[...], selected)
    small_ref[...] = small
    chunk = 256

    def weigh(i, _):
        part = pl.ds(pl.multiple_of(i * chunk, chunk), chunk)
        pack_ref[part, : plan.a_w] = dot_tn(norm_ref[:, part], ga_ref[...]).astype(BF)
        slab = slice(plan.s_dt, plan.s_dt + 128)
        pack_ref[part, slab] = jnp.where(
            lane < row, pack_ref[part, slab].astype(F32), small_ref[part, :]
        ).astype(BF)
        pack_ref[part, plan.o_mo : plan.o_mo + wide] = dot_tn(
            gs_ref[:, part], ni_ref[...]
        ).astype(BF)
        slab = slice(plan.s_ao, plan.s_ao + 128)
        attn = dot_tn(got_ref[:, part], attn_ref[...])
        if plan.off:
            attn = jnp.where(in_v, attn, pack_ref[part, slab].astype(F32))
        pack_ref[part, slab] = attn.astype(BF)
        return 0

    lax.fori_loop(0, width // chunk, weigh, 0)


def sum_kernel(plan, got_ref, out_ref):
    lane = lanes(128)
    row, count = plan.row, plan.n_small
    slab = slice(plan.s_dt, plan.s_dt + 128)

    def one(c, _):
        at = pl.ds(pl.multiple_of(c * plan.d_loc, plan.d_loc), plan.d_loc)
        total = got_ref[0, at, :].astype(F32)
        for f in range(1, got_ref.shape[0]):
            total = total + got_ref[f, at, :].astype(F32)
        out_ref[at, :] = total.astype(BF)
        part = total[:, slab]
        small = part + pltpu.roll(part, 128 - count, 1)
        high = small.astype(BF).astype(F32)
        low = pltpu.roll(small - high, count, 1)
        part = jnp.where(
            lane < row, part, jnp.where(lane < row + count, high, low)
        )
        out_ref[at, slab] = jnp.where(lane < row + 2 * count, part, 0.0).astype(BF)
        return 0

    lax.fori_loop(0, got_ref.shape[1] // plan.d_loc, one, 0)


def pack_kernel(plan, inner_ref, kv_ref, query_ref, dt_ref, bc_ref, gain_ref, conv_ref, chan_ref,
                mout_ref, aout_ref, out_ref, turn_ref):
    heads, chan, row = plan.heads, plan.chan, plan.row
    count = out_ref.shape[0]
    heads_t, q_t = mout_ref.shape[1] // HDIM, aout_ref.shape[1] // HDIM
    dts = dt_ref[...].astype(F32)
    chans = chan_ref[...].astype(F32)
    query = query_ref[...].astype(F32)
    turn_ref[...] = jnp.zeros(turn_ref.shape, F32)
    turn_ref[row : row + 2, : plan.d_loc] = gain_ref[...].astype(F32)
    turn_ref[row + 2 : row + KCONV + 3, : plan.cc] = conv_ref[...].astype(F32)
    for c in range(count):
        live = max(0, min(heads, heads_t - c * heads))
        wide = live * HDIM
        out_ref[c] = jnp.zeros(out_ref.shape[1:], BF)
        out_ref[c, :, : 2 * NSTATE] = bc_ref[...]
        low = row + KCONV + 3
        if live:
            at = c * heads
            turn_ref[low : low + live, : plan.mc] = chans[at : at + live]
            turn_ref[plan.off : plan.off + live, : plan.d_loc] = dts[at : at + live]
        else:
            turn_ref[low : low + heads, :] = jnp.zeros((heads, 128), F32)
            turn_ref[plan.off : plan.off + heads, :] = jnp.zeros((heads, 128), F32)
        slab = turn_ref[...].T[: plan.d_loc]
        out_ref[c, :, plan.s_dt : plan.s_dt + 128] = slab.astype(BF)
        if live:
            at = c * chan
            out_ref[c, :, plan.o_z : plan.o_z + wide] = inner_ref[:, at : at + wide]
            at = at + heads_t * HDIM
            out_ref[c, :, plan.o_x : plan.o_x + wide] = inner_ref[:, at : at + wide]
            at = c * chan
            out_ref[c, :, plan.o_mo : plan.o_mo + wide] = mout_ref[:, at : at + wide]
        if c < q_t:
            at = c * HDIM
            out_ref[c, :, plan.o_q : plan.o_q + HDIM] = query[:, at : at + HDIM].astype(BF)
            out_ref[c, :, plan.o_ao : plan.o_ao + HDIM] = aout_ref[:, at : at + HDIM]
        out_ref[c, :, plan.o_k : plan.o_k + HDIM] = kv_ref[:, :HDIM]
        out_ref[c, :, plan.o_v : plan.o_v + HDIM] = kv_ref[:, HDIM:]


def unpack_kernel(plan, heads_t, q_t, got_ref, inner_ref, query_ref, dt_ref, kv_ref, mout_ref,
                  aout_ref, chan_ref, head_ref, tail_ref):
    heads, chan, off, row = plan.heads, plan.chan, plan.off, plan.row
    count = got_ref.shape[0]
    kv_sum = jnp.zeros((plan.d_loc, 128), F32)
    bc_sum = jnp.zeros((plan.d_loc, 2 * NSTATE), F32)
    small_sum = jnp.zeros((plan.d_loc, 128), F32)
    lane = lanes(128)
    for c in range(count):
        live = max(0, min(heads, heads_t - c * heads))
        wide = live * HDIM
        query = got_ref[c, :, plan.o_q :].astype(F32)[:, :128]
        value = got_ref[c, :, plan.s_v : plan.s_v + 128].astype(F32)
        value = value if off == HDIM else pltpu.roll(value, HDIM, 1)
        kv_sum = kv_sum + jnp.where(lane < HDIM, pltpu.roll(query, HDIM, 1), value)
        bc_sum = bc_sum + got_ref[c, :, : 2 * NSTATE].astype(F32)
        slab = got_ref[c, :, plan.s_dt : plan.s_dt + 128].astype(F32)
        small = slab + pltpu.roll(slab, 128 - plan.n_small, 1)
        small_sum = small_sum + small
        if c < q_t:
            query_ref[:, c * HDIM : (c + 1) * HDIM] = query[:, :HDIM]
            out = got_ref[c, :, plan.s_ao : plan.s_ao + 128].astype(F32)
            aout_ref[:, c * HDIM : (c + 1) * HDIM] = out[:, off : off + HDIM]
        if live:
            low = c * chan
            for i, start in enumerate((plan.o_z, plan.o_x)):
                part = got_ref[c, :, start : start + plan.wide].astype(F32)
                at = i * heads_t * HDIM + low
                inner_ref[:, at : at + wide] = part[:, :wide]
            out = got_ref[c, :, plan.o_mo : plan.o_mo + plan.wide].astype(F32)
            mout_ref[:, low : low + wide] = out[:, :wide]
            turned = jnp.where(lane < row, slab, small).T
            at = c * heads
            dt_ref[at : at + live, :] = turned[off : off + live, : plan.d_loc]
            low = row + KCONV + 3
            chan_ref[at : at + live, :] = turned[low : low + live, : plan.mc]
            last = turned[row + plan.n_small - 1 : row + plan.n_small]
            for i in range(3):
                head_ref[i : i + 1, at : at + live] = last[:, i * heads : i * heads + live]
    kv_ref[...] = kv_sum
    tail_ref[:, : 2 * NSTATE] = bc_sum
    tail_ref[:, 2 * NSTATE :] = small_sum


def call(kernel, plan, outs, scratch, scalars, arrays):
    smem = pl.BlockSpec(memory_space=pltpu.SMEM)
    vmem = pl.BlockSpec(memory_space=pltpu.VMEM)
    return pl.pallas_call(
        lambda *refs: kernel(plan, *refs),
        out_shape=[jax.ShapeDtypeStruct(shape, kind) for shape, kind in outs],
        in_specs=[smem] * len(scalars) + [vmem] * len(arrays),
        out_specs=[vmem] * len(outs),
        scratch_shapes=[pltpu.VMEM(shape, kind) for shape, kind in scratch],
        compiler_params=pltpu.CompilerParams(vmem_limit_bytes=48 << 20),
    )(*scalars, *arrays)


def per_device(
    inputs,
    seq_lengths,
    norm_gains,
    mamba_in,
    dt_proj,
    bc_proj,
    mamba_chan,
    bc_conv,
    head_params,
    query_proj,
    kv_proj,
    attn_out,
    mamba_out,
    mlp_in,
    mlp_out,
    out_grad,
):
    n_f = lax.axis_size("fsdp")
    n_c = lax.axis_size("context")
    c_id = lax.axis_index("context")
    t_id = lax.axis_index("tensor")
    shards = n_f * n_c
    rows = inputs.shape[0]
    group = rows * n_c
    half = rows // 2
    d_loc = mamba_in.shape[0]
    width = d_loc * shards
    heads_t = head_params.shape[1]
    heads = -(-heads_t // n_c)
    heads_pad = heads * n_c
    q_t = query_proj.shape[1] // HDIM
    ff = mlp_in.shape[2]
    cc = bc_conv.shape[1]
    mc = mamba_chan.shape[1]
    plan = Plan(group, rows, width, d_loc, heads, 2 * heads_t * HDIM, cc, mc)
    bc_w = 2 * NSTATE
    p_w = plan.p_w

    (pack,) = call(
        pack_kernel,
        plan,
        [((n_c, d_loc, p_w), BF)],
        [((128, 128), F32)],
        (),
        (
            mamba_in.reshape(d_loc, 2 * heads_t * HDIM),
            kv_proj.reshape(d_loc, 2 * HDIM),
            query_proj,
            dt_proj.T,
            bc_proj,
            norm_gains,
            bc_conv,
            mamba_chan,
            mamba_out.T,
            attn_out.T,
        ),
    )

    mine = lax.dynamic_slice_in_dim(inputs, t_id * half, half, 0)
    part = exchange(pack, "context").reshape(n_c * d_loc, p_w)
    got_in = spread_async(mine, "context")
    w_all = spread(part, "fsdp").reshape(width, p_w)
    rows_in = join_pair(got_in, swap_pair(got_in), t_id, 1).reshape(group, width)
    part_mi = spread_async(mlp_in.reshape(d_loc, 2 * ff), "context")
    part_mo = spread_async(mlp_out.T, "context")
    w_mi = plane_gather(part_mi.reshape(n_c * d_loc, 2 * ff)).reshape(width, 2 * ff)
    w_mo = plane_gather(part_mo.reshape(n_c * d_loc, ff)).reshape(width, ff)

    starts = jnp.cumsum(seq_lengths[0]) - seq_lengths[0]
    row_ids = jnp.arange(group, dtype=jnp.int32)
    inside = row_ids[:, None] >= starts[None, :]
    positions = row_ids - jnp.max(jnp.where(inside, starts[None, :], 0), axis=1)
    freqs = jnp.power(ROPE_BASE, -jnp.arange(HDIM // 2).astype(F32) * (2.0 / HDIM))
    angles = positions.astype(F32)[:, None] * jnp.concatenate([freqs] * 4)[None, :]
    trig = jnp.concatenate([jnp.cos(angles), jnp.sin(angles)], axis=1)
    head_vec = lax.dynamic_slice_in_dim(
        pad_to(head_params, 1, heads_pad), c_id * heads, heads, 1
    )
    feature = jnp.arange(width, dtype=jnp.int32)[:, None]
    place = feature % d_loc
    shard = feature // d_loc
    lane = jnp.arange(plan.wide, dtype=jnp.int32)[None, :] % HDIM
    sel = [(place < cc) & (shard * cc + place == jnp.arange(bc_w, dtype=jnp.int32)[None, :])]
    for k in range(KCONV + 2):
        sel.append((place < mc) & (shard * mc + place == k * HDIM + lane))
    sel = jnp.concatenate(sel, axis=1).astype(BF)
    scalars = (seq_lengths, head_vec, t_id.reshape(1))
    slab_w = 2 * width + 128
    part_rows = n_c * half
    keep, give, gain_one, gain_two, taps, norm, proj, pre, wide, thin = call(
        forward_kernel,
        plan,
        [
            ((part_rows, slab_w), BF),
            ((part_rows, slab_w), BF),
            ((1, width), F32),
            ((1, width), F32),
            ((8, plan.conv), F32),
            ((group, width), BF),
            ((group, plan.a_w), F32),
            ((group, plan.conv), F32),
            ((group, plan.wide + 256), F32),
            ((group, 384), BF),
        ],
        [((group, plan.conv), BF), ((group + 8, plan.conv), F32), ((group, 128), F32)],
        scalars,
        (rows_in, w_all, sel, trig),
    )
    gain_mlp = gain_two[0]

    def pair_parts(values, lead):
        parts = values.reshape(lead + (2, half) + values.shape[1:])
        keep = lax.dynamic_index_in_dim(parts, t_id, len(lead), False)
        return keep, lax.dynamic_index_in_dim(parts, 1 - t_id, len(lead), False)

    def pair_sum(values, lead):
        keep, give = pair_parts(values, lead)
        return keep + swap_pair(give.astype(BF)).astype(F32)

    def pair_add(keep, give):
        return (keep.astype(F32) + swap_pair(give).astype(F32)).astype(BF)

    summed = pair_add(keep, give).reshape(n_c, half, slab_w)
    both = jnp.sum(exchange(summed, "context").astype(F32), axis=0)
    squares = jnp.sum(both[:, 2 * width : 2 * width + 4], axis=1, keepdims=True)
    scale_own = lax.rsqrt(squares / plan.total + NORM_EPS)
    mamba_own = both[:, :width]
    in_own = mine.astype(F32)
    residual = in_own + scale_own * mamba_own + both[:, width : 2 * width]

    normed_two, inv_two = rms_forward(residual)
    norm_two_own = (normed_two * gain_mlp[None, :]).astype(BF)
    norm_two = join_pair(norm_two_own, swap_pair(norm_two_own), t_id, 0).reshape(rows, width)
    stacked = jnp.concatenate([norm_two, out_grad], axis=0)
    first = dot(norm_two, w_mi)
    gate_val = first[:, :ff]
    up_val = first[:, ff:]
    grad_act = dot(out_grad, w_mo)
    gate_sig = sigmoid(gate_val)
    gate_act = gate_val * gate_sig
    mlp_act = (gate_act * up_val).astype(BF)
    grad_gate = (grad_act * up_val * silu_grad(gate_val, gate_sig)).astype(BF)
    grad_up = (grad_act * gate_act).astype(BF)
    blank = jnp.zeros((rows, ff), BF)
    mixed = jnp.concatenate(
        [
            jnp.concatenate([grad_gate, grad_up, blank], axis=1),
            jnp.concatenate([blank, blank, mlp_act], axis=1),
        ],
        axis=0,
    )
    grad_two = pair_sum(dot_nt(mixed[:rows, : 2 * ff], w_mi), ())
    top_own = lax.dynamic_slice_in_dim(out_grad, t_id * half, half, 0).astype(F32)
    g_gain_mlp = jnp.sum(grad_two * normed_two, axis=0)
    grad_res = top_own + rms_backward(grad_two, normed_two, inv_two, gain_mlp)
    grad_rs_own = jnp.sum(grad_res * mamba_own, axis=1, keepdims=True)
    factor = split(jnp.concatenate([grad_rs_own, scale_own], axis=1), 2)
    got = spread(jnp.concatenate([grad_res.astype(BF), factor], axis=1), "context")
    got_other = swap_pair(got)
    block = n_c * d_loc

    def mlp_block(target, part):
        low = target * block + part * (block // 2)
        cols = lax.dynamic_slice_in_dim(stacked, low, block // 2, 1)
        return dot_tn(cols, mixed)

    own = plane_reduce(mlp_block)
    own = reduce_async(own.reshape(n_c, d_loc, 3 * ff), "context")
    out_mi = own[:, : 2 * ff].reshape(d_loc, 2, ff)
    out_mo = own[:, 2 * ff :].T

    keep, give, g_pack = call(
        backward_kernel,
        plan,
        [((part_rows, width), BF), ((part_rows, width), BF), ((width, p_w), BF)],
        [
            ((group, plan.conv), BF),
            ((group + 8, plan.conv), F32),
            ((group, width), BF),
            ((group, plan.wide), BF),
            ((group, plan.wide), F32),
            ((group, plan.a_w), BF),
            ((group, plan.conv), F32),
            ((group + 8, plan.conv), F32),
            ((group, 128), F32),
            ((group, 128), F32),
            ((group, 128), F32),
            ((group, 128), F32),
            ((128, group), F32),
            ((128, group), F32),
            ((128, group), F32),
            ((width, 128), F32),
            ((group, 128), F32),
            ((group, width + 128), BF),
        ],
        scalars,
        (
            rows_in, w_all, sel, trig, taps, norm, proj, pre, wide, thin, got,
            got_other,
            g_gain_mlp[None],
        ),
    )
    mlp_act, residual, keep = lax.optimization_barrier((mlp_act, residual, keep))
    out_own = (residual + pair_sum(dot_nt(mlp_act, w_mo), ())).astype(BF)
    partial = pair_add(keep, give).reshape(n_c, half, width)
    grad_one = reduce_async(partial, "context")
    gain_mix = gain_one[0]
    normed_own, inv_own = rms_forward(in_own)
    grad_in_own = grad_res + rms_backward(grad_one, normed_own, inv_own, gain_mix)
    output = join_pair(out_own, swap_pair(out_own), t_id, 0).reshape(rows, width)
    input_grad = join_pair(grad_in_own, swap_pair(grad_in_own), t_id, 0).reshape(rows, width)

    got = exchange(g_pack.reshape(n_f, block, p_w), "fsdp")
    (g_pack,) = call(sum_kernel, plan, [((block, p_w), BF)], [], (), (got,))
    got = exchange(g_pack.reshape(n_c, d_loc, p_w), "context")
    out_inner, out_query, out_dt, out_kv, out_mout, out_aout, out_chan, out_heads, tail = call(
        lambda plan, *refs: unpack_kernel(plan, heads_t, q_t, *refs),
        plan,
        [
            ((d_loc, 2 * heads_t * HDIM), F32),
            ((d_loc, q_t * HDIM), F32),
            ((heads_t, d_loc), F32),
            ((d_loc, 2 * HDIM), F32),
            ((d_loc, heads_t * HDIM), F32),
            ((d_loc, q_t * HDIM), F32),
            ((heads_t, mc), F32),
            ((3, heads_t), F32),
            ((d_loc, bc_w + 128), F32),
        ],
        [],
        (),
        (got,),
    )
    tail = tail + swap_pair(tail)
    out_inner = out_inner.reshape(d_loc, 2, heads_t * HDIM)
    out_kv = out_kv.reshape(d_loc, 2, HDIM)
    out_dt, out_mout, out_aout = out_dt.T, out_mout.T, out_aout.T
    out_bc = tail[:, :bc_w]
    low = bc_w + plan.row
    out_gains = tail[:, low : low + 2].T
    out_convbc = tail[:cc, low + 2 : low + KCONV + 3].T

    return (
        output,
        input_grad,
        out_gains,
        out_inner,
        out_dt,
        out_bc,
        out_chan,
        out_convbc,
        out_heads,
        out_query,
        out_kv,
        out_aout,
        out_mout,
        out_mi,
        out_mo,
    )


def solution(mesh):
    both = ("fsdp", "context")
    rows = P(both, None)

    return jax.shard_map(
        per_device,
        mesh=mesh,
        in_specs=(
            rows,
            P("fsdp", None),
            P(None, both),
            P(both, None, "tensor"),
            P(both, "tensor"),
            rows,
            P("tensor", both),
            P(None, both),
            P(None, "tensor"),
            P(both, "tensor"),
            P(both, None, "tensor"),
            P("tensor", both),
            P("tensor", both),
            P(both, None, "tensor"),
            P("tensor", both),
            rows,
        ),
        out_specs=(
            rows,
            rows,
            P(None, both),
            P(both, None, "tensor"),
            P(both, "tensor"),
            rows,
            P("tensor", both),
            P(None, both),
            P(None, "tensor"),
            P(both, "tensor"),
            P(both, None, "tensor"),
            P("tensor", both),
            P("tensor", both),
            P(both, None, "tensor"),
            P("tensor", both),
        ),
        check_vma=False,
    )
```

```python
import jax
import jax.numpy as jnp
from jax import lax
from jax.experimental import pallas as pl
from jax.experimental.pallas import tpu as pltpu
from jax.sharding import PartitionSpec as P

S_TENSOR = "tensor"
S_FSDP = "fsdp"
S_CONTEXT = "context"


HDIM = 64
NSTATE = 128
KCONV = 4
NORM_EPS = 1e-05
ROPE_BASE = 100000000000.0
EXACT = lax.Precision.HIGHEST
BF = jnp.bfloat16
F32 = jnp.float32


def swap_pair(block):
    return lax.ppermute(block, S_TENSOR, [(0, 1), (1, 0)])


def join_pair(own, other, place, axis):
    low = jnp.where(place == 0, own, other)
    high = jnp.where(place == 0, other, own)
    return jnp.stack([low, high], axis=axis)


def exchange(blocks, axis):
    return lax.all_to_all(blocks, axis, 0, 0, tiled=True)


def spread(block, axis):
    return exchange(jnp.broadcast_to(block[None], (lax.axis_size(axis),) + block.shape), axis)


def hops(axis):
    count = lax.axis_size(axis)
    place = lax.axis_index(axis)
    for step in range(1, count):
        route = [(i, (i + step) % count) for i in range(count)]
        yield route, (place + step) % count, (place - step) % count


def spread_async(block, axis):
    count = lax.axis_size(axis)
    got = [(lax.ppermute(block, axis, route), source) for route, _, source in hops(axis)]
    if block.size > 1 << 18:
        whole = jnp.zeros((count,) + block.shape, block.dtype)
        whole = lax.dynamic_update_index_in_dim(whole, block, lax.axis_index(axis), 0)
        for piece, source in got:
            whole = lax.dynamic_update_index_in_dim(whole, piece, source, 0)
        return whole
    place = lax.axis_index(axis)
    pieces = [block] + [piece for piece, _ in got]
    return jnp.stack(
        [lax.select_n((place - i) % count, *pieces) for i in range(count)], axis=0
    )


def reduce_async(blocks, axis):
    got = [
        lax.ppermute(lax.dynamic_index_in_dim(blocks, target, 0, False), axis, route)
        for route, target, _ in hops(axis)
    ]
    total = lax.dynamic_index_in_dim(blocks, lax.axis_index(axis), 0, False).astype(F32)
    for piece in got:
        total = total + piece.astype(F32)
    return total


def beside(step):
    return [(i, i ^ step) for i in range(4)]


def plane_gather(block):
    if lax.axis_size(S_FSDP) != 4:
        return spread_async(block, S_FSDP)
    half = block.shape[0] // 2
    place = lax.axis_index(S_FSDP)
    near = lax.ppermute(block, S_FSDP, beside(1))
    side = lax.ppermute(block, S_FSDP, beside(2))
    far_top = lax.ppermute(side[:half], S_FSDP, beside(1))
    far_low = lax.ppermute(near[half:], S_FSDP, beside(2))
    whole = jnp.zeros((4, 2, half) + block.shape[1:], block.dtype)
    parts = ((block, place), (near, place ^ 1), (side, place ^ 2))
    for piece, index in parts:
        piece = piece.reshape((1, 2, half) + block.shape[1:])
        whole = lax.dynamic_update_slice(whole, piece, (index, 0, 0, 0))
    for row, piece in enumerate((far_top, far_low)):
        whole = lax.dynamic_update_slice(whole, piece[None, None], (place ^ 3, row, 0, 0))
    return whole


def plane_reduce(make):
    def whole(target):
        return jnp.concatenate([make(target, 0), make(target, 1)], axis=0)

    if lax.axis_size(S_FSDP) != 4:
        sent = [(route, whole(target).astype(BF)) for route, target, _ in hops(S_FSDP)]
        own = whole(lax.axis_index(S_FSDP))
        for route, piece in sent:
            own = own + lax.ppermute(piece, S_FSDP, route).astype(F32)
        return own.astype(BF)
    place = lax.axis_index(S_FSDP)
    got_side = lax.ppermute(make(place ^ 3, 0).astype(BF), S_FSDP, beside(1))
    got_near = lax.ppermute(make(place ^ 3, 1).astype(BF), S_FSDP, beside(2))
    near_top = lax.ppermute(make(place ^ 1, 0).astype(BF), S_FSDP, beside(1))
    side_low = lax.ppermute(make(place ^ 2, 1).astype(BF), S_FSDP, beside(2))
    own_top = make(place, 0).astype(BF)
    own_low = make(place, 1).astype(BF)
    side_top = make(place ^ 2, 0).astype(BF)
    near_low = make(place ^ 1, 1).astype(BF)
    side_top = (side_top.astype(F32) + got_side.astype(F32)).astype(BF)
    near_low = (near_low.astype(F32) + got_near.astype(F32)).astype(BF)
    side_top = lax.ppermute(side_top, S_FSDP, beside(2))
    near_low = lax.ppermute(near_low, S_FSDP, beside(1))
    top = own_top.astype(F32) + near_top.astype(F32) + side_top.astype(F32)
    low = own_low.astype(F32) + near_low.astype(F32) + side_low.astype(F32)
    return jnp.concatenate([top, low], axis=0).astype(BF)


def sigmoid(values):
    return 1.0 / (1.0 + jnp.exp(-values))


def silu_grad(values, sigma):
    return sigma * (1.0 + values * (1.0 - sigma))


def rms_forward(values):
    inv_rms = lax.rsqrt(jnp.mean(values * values, axis=-1, keepdims=True) + NORM_EPS)
    return values * inv_rms, inv_rms


def rms_backward(grad_out, normed, inv_rms, gain_vec):
    grad_normed = grad_out * gain_vec[None, :]
    return inv_rms * (grad_normed - normed * jnp.mean(grad_normed * normed, axis=-1, keepdims=True))


def dot(left, right, exact=None):
    return lax.dot_general(
        left, right, (((1,), (0,)), ((), ())), precision=exact, preferred_element_type=F32
    )


def dot_nt(left, right, exact=None):
    return lax.dot_general(
        left, right, (((1,), (1,)), ((), ())), precision=exact, preferred_element_type=F32
    )


def dot_tn(left, right, exact=None):
    return lax.dot_general(
        left, right, (((0,), (0,)), ((), ())), precision=exact, preferred_element_type=F32
    )


def pad_to(array, axis, size):
    if array.shape[axis] == size:
        return array
    widths = [(0, 0)] * array.ndim
    widths[axis] = (0, size - array.shape[axis])
    return jnp.pad(array, widths)


def ceil_to(value, unit):
    return -(-value // unit) * unit


def split(values, pieces, wide=True):
    parts = []
    for _ in range(pieces):
        high = lax.reduce_precision(values, 8, 7)
        parts.append(high.astype(BF))
        values = values - high
    joined = jnp.concatenate(parts, axis=-1)
    return pad_to(joined, joined.ndim - 1, 128) if wide else joined


class Plan:
    def __init__(self, group, rows, width, d_loc, heads, total, cc, mc):
        self.group, self.rows, self.width, self.d_loc = group, rows, width, d_loc
        self.heads, self.total, self.cc, self.mc = heads, total, cc, mc
        self.half = rows // 2
        self.chan = heads * HDIM
        self.wide = ceil_to(self.chan, 128)
        self.off = self.chan % 128
        self.conv = 2 * NSTATE + self.wide
        self.o_x = 2 * NSTATE
        self.o_v = self.o_x + self.chan
        self.o_z = ceil_to(self.o_v + HDIM, 128)
        self.o_dt = self.o_z + self.chan
        self.o_s = self.o_dt + heads
        self.n_small = KCONV + 4 + heads
        self.o_end = self.o_s + 2 * self.n_small
        self.o_q = ceil_to(self.o_end, 128)
        self.o_k = self.o_q + HDIM
        self.a_w = self.o_q + 2 * HDIM
        self.o_mo = self.a_w
        self.o_ao = self.a_w + self.chan
        self.p_w = ceil_to(self.o_ao + HDIM, 128)
        self.s_v = self.o_v - self.off
        self.s_dt = self.o_dt - self.off
        self.s_ao = self.o_ao - self.off
        self.row = self.off + heads


def lanes(count):
    return lax.broadcasted_iota(jnp.int32, (1, count), 1)


def first_rows(lengths_ref, index):
    start = jnp.zeros_like(index)
    edge = jnp.int32(0)
    for i in range(lengths_ref.shape[1] - 1):
        edge = edge + lengths_ref[0, i]
        start = jnp.where(index >= edge, edge, start)
    return start


def head_row(plan, head_ref, which):
    lane = lanes(128)
    row = jnp.zeros((1, 128), F32)
    for j in range(plan.heads):
        row = jnp.where(lane == plan.off + j, head_ref[which, j], row)
    return row


def head_wide(plan, values):
    lane = lanes(plan.wide)
    row = jnp.zeros((1, plan.wide), F32)
    for j in range(plan.heads):
        row = jnp.where(lane // HDIM == j, values[j], row)
    return row


def steps_of(plan, head_ref, slab):
    lane = lanes(128)
    live = (lane >= plan.off) & (lane < plan.row)
    shifted = jnp.where(live, slab + head_row(plan, head_ref, 0), 0.0)
    soft = jnp.maximum(shifted, 0.0) + jnp.log1p(jnp.exp(-jnp.abs(shifted)))
    dt_step = jnp.where(live, soft, 0.0)
    rate = jnp.where(live, jnp.exp(head_row(plan, head_ref, 1)), 0.0)
    return dt_step, rate, shifted, live


def small_rows(plan, w_ref, sel_ref):
    slab = w_ref[:, plan.s_dt : plan.s_dt + 128]
    turned = slab.astype(F32).T
    picked = dot_tn(slab, sel_ref[...])
    row = plan.row
    lane = lanes(plan.wide)
    taps = []
    for k in range(KCONV + 2):
        low = 2 * NSTATE + k * plan.wide
        piece = jnp.zeros((1, plan.wide), F32)
        for j in range(plan.heads):
            at = row + KCONV + 3 + j
            piece = jnp.where(lane // HDIM == j, picked[at : at + 1, low : low + plan.wide], piece)
        if k <= KCONV:
            piece = jnp.concatenate(
                [picked[row + 2 + k : row + 3 + k, : 2 * NSTATE], piece], axis=1
            )
        taps.append(piece)
    return turned[row : row + 1], turned[row + 1 : row + 2], taps


def lower_tri(group):
    return (
        lax.broadcasted_iota(jnp.int32, (group, group), 0)
        >= lax.broadcasted_iota(jnp.int32, (group, group), 1)
    ).astype(F32)


def linked_rows(plan, lengths_ref, low):
    index = lax.broadcasted_iota(jnp.int32, (plan.rows, 1), 0) + low
    start = first_rows(lengths_ref, index)
    cols = lanes(plan.group)
    return (cols <= index) & (cols >= start), index - start


def turn(values, cosine, sine):
    lane = lanes(2 * HDIM)
    moved = jnp.where(
        lane % HDIM < HDIM // 2, -pltpu.roll(values, 2 * HDIM - HDIM // 2, 1),
        pltpu.roll(values, HDIM // 2, 1),
    )
    return values * cosine + moved * sine


def split_rows(plan, values, t_id):
    low = values[: plan.half]
    high = values[plan.half :]
    return jnp.where(t_id == 0, low, high), jnp.where(t_id == 0, high, low)


def views(plan, trig_ref, wide_ref, thin_ref):
    def part(ref, low, size):
        return ref.at[:, low : low + size]

    wide = plan.wide
    return (
        part(trig_ref, 0, 128),
        part(trig_ref, 128, 128),
        part(wide_ref, 0, wide),
        part(wide_ref, wide, 128),
        part(wide_ref, wide + 128, 128),
        part(thin_ref, 0, 128),
        part(thin_ref, 128, 128),
        part(thin_ref, 256, 128),
    )


def forward_kernel(
    plan, lengths_ref, head_ref, t_ref, x_ref, w_ref, sel_ref, trig_ref,
    keep_ref, give_ref, gain1_ref, gain2_ref, taps_ref, norm_ref, proj_ref, pre_ref, wide_ref, thin_ref,
    act_ref, ext_ref, dt_ref,
):
    cos_ref, sin_ref, ssm_ref, cum_ref, lse_ref, attn_ref, qk_ref, kq_ref = views(
        plan, trig_ref, wide_ref, thin_ref
    )
    rows, group, wide = plan.rows, plan.group, plan.wide
    gain, gain_two, taps = small_rows(plan, w_ref, sel_ref)
    gain1_ref[...] = gain
    gain2_ref[...] = gain_two
    for k in range(KCONV + 1):
        taps_ref[k : k + 1, :] = taps[k]
    taps_ref[KCONV + 1 : KCONV + 2, plan.o_x :] = taps[KCONV + 1]
    blocks = group // rows
    t_id = t_ref[0]
    ext_ref[0:8, :] = jnp.zeros((8, plan.conv), F32)

    lower = lower_tri(rows)

    def project(b, before):
        at = pl.ds(pl.multiple_of(b * rows, rows), rows)
        values = x_ref[at, :].astype(F32)
        normed = rms_forward(values)[0]
        norm = (normed * gain).astype(BF)
        norm_ref[at, :] = norm
        proj = dot(norm, w_ref[:, : plan.a_w])
        proj_ref[at, :] = proj
        ext_ref[pl.ds(pl.multiple_of(b * rows + 8, 8), rows), :] = (
            proj[:, : plan.conv].astype(BF).astype(F32)
        )
        rot = turn(proj[:, plan.o_q :], cos_ref[at, :], sin_ref[at, :])
        qk_ref[at, :] = rot.astype(BF)
        kq_ref[at, :] = pltpu.roll(rot, HDIM, 1).astype(BF)
        dt_step, rate, _, _ = steps_of(plan, head_ref, proj[:, plan.s_dt : plan.s_dt + 128])
        dt_ref[at, :] = dt_step
        cum = dot(lower, -dt_step * rate, EXACT) + before
        cum_ref[at, :] = cum
        return cum[rows - 1 : rows]

    lax.fori_loop(0, blocks, project, jnp.zeros((1, 128), F32))
    cum_t = cum_ref[...].T
    dt_t = dt_ref[...].T

    def convolve(b, _):
        low = pl.multiple_of(b * rows, rows)
        at = pl.ds(low, rows)
        pos = linked_rows(plan, lengths_ref, low)[1]
        ext = ext_ref[pl.ds(low, rows + 8), :]
        total = jnp.broadcast_to(taps[KCONV], (rows, plan.conv))
        for k in range(KCONV):
            step = KCONV - 1 - k
            total = total + taps[k] * (ext[8 - step : 8 - step + rows] * (pos >= step).astype(F32))
        pre_ref[at, :] = total
        act_ref[at, :] = (total * sigmoid(total)).astype(BF)
        return 0

    lax.fori_loop(0, blocks, convolve, 0)

    lane_w = lanes(wide)
    lane = lanes(128)
    in_v = (lane >= plan.off) & (lane < plan.off + HDIM)
    b_all = act_ref[:, :NSTATE]
    x_all = act_ref[:, plan.o_x : plan.o_x + wide]
    v_all = jnp.where(in_v, proj_ref[:, plan.s_v : plan.s_v + 128], 0.0).astype(BF)
    k_all = kq_ref[...]
    skip = head_wide(plan, [head_ref[2, j] for j in range(plan.heads)])
    w_m = w_ref[:, plan.o_mo : plan.o_mo + wide]
    w_o = w_ref[:, plan.s_ao : plan.s_ao + 128]

    def mix(b, _):
        low = pl.multiple_of(b * rows, rows)
        at = pl.ds(low, rows)
        linked = linked_rows(plan, lengths_ref, low)[0]
        cross = dot_nt(act_ref[at, NSTATE : 2 * NSTATE], b_all)
        cum_b = cum_ref[at, :]
        core = jnp.zeros((rows, wide), F32)
        for j in range(plan.heads):
            col = cum_b[:, plan.off + j : plan.off + j + 1]
            gaps = jnp.where(linked, col - cum_t[plan.off + j : plan.off + j + 1], -1e30)
            mixing = jnp.exp(gaps) * cross * dt_t[plan.off + j : plan.off + j + 1]
            core = jnp.where(lane_w // HDIM == j, dot(mixing.astype(BF), x_all), core)
        pre = pre_ref[at, plan.o_x : plan.o_x + wide]
        ssm = core + skip * (pre * sigmoid(pre))
        ssm_ref[at, :] = ssm
        z_gate = proj_ref[at, plan.o_z : plan.o_z + wide].astype(BF).astype(F32)
        gated = jnp.where(lane_w < plan.chan, ssm * (z_gate * sigmoid(z_gate)), 0.0)
        norm_in = (gated * taps[KCONV + 1]).astype(BF)
        square = jnp.sum(gated * gated, axis=1, keepdims=True)
        high = square.astype(BF).astype(F32)
        square = jnp.where(
            lane == 2 * t_id, high, jnp.where(lane == 2 * t_id + 1, square - high, 0.0)
        )

        query = jnp.where(lane < HDIM, qk_ref[at, :].astype(F32), 0.0).astype(BF)
        scores = jnp.where(linked, dot_nt(query, k_all) * HDIM ** (-0.5), -1e30)
        top = jnp.max(scores, axis=1, keepdims=True)
        exps = jnp.exp(scores - top)
        total = jnp.sum(exps, axis=1, keepdims=True)
        values = dot((exps / total).astype(BF), v_all).astype(BF)
        attn_ref[at, :] = values
        lse_ref[at, :] = jnp.broadcast_to(top + jnp.log(total), (rows, 128))

        out = pl.ds(pl.multiple_of(b * plan.half, plan.half), plan.half)
        width = plan.width
        for start, piece in (
            (0, dot_nt(norm_in, w_m)),
            (width, dot_nt(values, w_o)),
            (2 * width, square),
        ):
            keep, give = split_rows(plan, piece, t_id)
            keep_ref[out, start : start + piece.shape[1]] = keep.astype(BF)
            give_ref[out, start : start + piece.shape[1]] = give.astype(BF)
        return 0

    lax.fori_loop(0, blocks, mix, 0)


def backward_kernel(
    plan, lengths_ref, head_ref, t_ref, x_ref, w_ref, sel_ref, trig_ref,
    taps_ref, norm_ref, proj_ref, pre_ref, wide_ref, thin_ref, mine_ref,
    other_ref, gain2_ref,
    keep_ref, give_ref, pack_ref,
    act_ref, ext_ref, gs_ref, ni_ref, gy_ref, ga_ref, gact_ref, gext_ref, gv_ref, gk_ref, gat_ref,
    row_ref, col_ref, dtt_ref, cumt_ref, small_ref, dt_ref, got_ref,
):
    cos_ref, sin_ref, ssm_ref, cum_ref, lse_ref, attn_ref, qk_ref, kq_ref = views(
        plan, trig_ref, wide_ref, thin_ref
    )
    rows, group, wide, width = plan.rows, plan.group, plan.wide, plan.width
    heads, off, row = plan.heads, plan.off, plan.row
    taps = [taps_ref[k : k + 1, :] for k in range(KCONV + 1)]
    blocks = group // rows
    t_id = t_ref[0]
    lane_w = lanes(wide)
    lane = lanes(128)
    in_v = (lane >= off) & (lane < off + HDIM)
    norm_gain = taps_ref[KCONV + 1 : KCONV + 2, plan.o_x :]
    w_m = w_ref[:, plan.o_mo : plan.o_mo + wide]
    w_o = w_ref[:, plan.s_ao : plan.s_ao + 128]
    ext_ref[0:8, :] = jnp.zeros((8, plan.conv), F32)
    gext_ref[group : group + 8, :] = jnp.zeros((8, plan.conv), F32)
    skip = head_wide(plan, [head_ref[2, j] for j in range(heads)])
    scale = HDIM ** (-0.5)

    cumt_ref[...] = cum_ref[...].T

    def gate(b, sums):
        at = pl.ds(pl.multiple_of(b * rows, rows), rows)
        for low, t_low in ((b * rows, 0), (b * rows + plan.half, 1)):
            half_at = pl.ds(pl.multiple_of(low, plan.half), plan.half)
            got_ref[half_at, :] = jnp.where(t_id == t_low, mine_ref[b], other_ref[b])
        grad_round = got_ref[at, :width]
        factor = got_ref[at, width : width + 128].astype(F32)
        grad_rs = factor[:, 0:1] + factor[:, 2:3]
        row_scale = factor[:, 1:2] + factor[:, 3:4]
        grad_scaled = (grad_round.astype(F32) * row_scale).astype(BF)
        gs_ref[at, :] = grad_scaled
        grad_in = jnp.where(lane_w < plan.chan, dot(grad_scaled, w_m), 0.0)
        gat_ref[at, :] = jnp.where(in_v, dot(grad_round, w_o), 0.0)
        z_gate = proj_ref[at, plan.o_z : plan.o_z + wide].astype(BF).astype(F32)
        z_gate = jnp.where(lane_w < plan.chan, z_gate, 0.0)
        z_sig = sigmoid(z_gate)
        silu_z = z_gate * z_sig
        ssm = ssm_ref[at, :]
        gated = ssm * silu_z
        ni_ref[at, :] = (gated * norm_gain).astype(BF)
        grad_gated = grad_in * norm_gain - gated * (
            grad_rs * row_scale * row_scale * row_scale / plan.total
        )
        grad_y = grad_gated * silu_z
        gy_ref[at, :] = grad_y
        grad_z = grad_gated * ssm * silu_grad(z_gate, z_sig)
        ga_ref[at, plan.o_z : plan.o_z + wide] = grad_z.astype(BF)
        pre = pre_ref[at, :]
        active = pre * sigmoid(pre)
        act_ref[at, :] = active.astype(BF)
        ext_ref[pl.ds(pl.multiple_of(b * rows + 8, 8), rows), :] = (
            proj_ref[at, : plan.conv].astype(BF).astype(F32)
        )
        gact_ref[at, plan.o_x : plan.o_x + wide] = jnp.zeros((rows, wide), F32)
        gact_ref[at, :NSTATE] = jnp.zeros((rows, NSTATE), F32)
        gv_ref[at, :] = jnp.zeros((rows, 128), F32)
        gk_ref[at, :] = jnp.zeros((rows, 128), F32)
        dt_ref[at, :] = steps_of(plan, head_ref, proj_ref[at, plan.s_dt : plan.s_dt + 128])[0]
        return (
            sums[0] + jnp.sum(grad_in * gated, axis=0, keepdims=True),
            sums[1]
            + jnp.sum(grad_y * active[:, plan.o_x : plan.o_x + wide], axis=0, keepdims=True),
        )

    blank = jnp.zeros((1, wide), F32)
    g_norm_gain, skip_sum = lax.fori_loop(0, blocks, gate, (blank, blank))
    col_ref[...] = jnp.zeros((128, group), F32)
    dtt_ref[...] = dt_ref[...].T

    b_all = act_ref[:, :NSTATE]
    x_all = act_ref[:, plan.o_x : plan.o_x + wide]
    v_all = jnp.where(in_v, proj_ref[:, plan.s_v : plan.s_v + 128], 0.0).astype(BF)
    k_all = kq_ref[...]

    def mix(b, _):
        low = pl.multiple_of(b * rows, rows)
        at = pl.ds(low, rows)
        linked = linked_rows(plan, lengths_ref, low)[0]
        c_blk = act_ref[at, NSTATE : 2 * NSTATE]
        cross = dot_nt(c_blk, b_all)
        cum_b = cum_ref[at, :]
        grad_y = gy_ref[at, :]
        grad_cross = jnp.zeros((rows, group), F32)
        grad_x = jnp.zeros((group, wide), F32)
        row_slab = jnp.zeros((rows, 128), F32)
        y_round = grad_y.astype(BF)
        for j in range(heads):
            col = cum_b[:, off + j : off + j + 1]
            dt_row = dtt_ref[off + j : off + j + 1, :]
            gaps = jnp.where(linked, col - cumt_ref[off + j : off + j + 1, :], -1e30)
            decays = jnp.exp(gaps)
            weights = decays * cross
            mine = lane_w // HDIM == j
            grad_mix = dot_nt(jnp.where(mine, grad_y, 0.0).astype(BF), x_all)
            flow = grad_mix * weights
            col_ref[off + j : off + j + 1, :] += jnp.sum(flow, axis=0, keepdims=True)
            row_slab = jnp.where(
                lane == off + j, jnp.sum(flow * dt_row, axis=1, keepdims=True), row_slab
            )
            grad_cross = grad_cross + grad_mix * (decays * dt_row)
            grad_x = jnp.where(mine, dot_tn((weights * dt_row).astype(BF), y_round), grad_x)
        row_ref[at, :] = row_slab
        grad_cross = grad_cross.astype(BF)
        gact_ref[:, plan.o_x : plan.o_x + wide] += grad_x
        gact_ref[at, NSTATE : 2 * NSTATE] = dot(grad_cross, b_all)
        gact_ref[:, :NSTATE] += dot_tn(grad_cross, c_blk)

        query = jnp.where(lane < HDIM, qk_ref[at, :].astype(F32), 0.0).astype(BF)
        scores = jnp.where(linked, dot_nt(query, k_all) * scale, -1e30)
        probs = jnp.exp(scores - lse_ref[at, 0:1])
        grad_attn = gat_ref[at, :]
        delta = jnp.sum(grad_attn * attn_ref[at, :].astype(F32), axis=1, keepdims=True)
        attn_round = grad_attn.astype(BF)
        grad_prob = dot_nt(attn_round, v_all)
        grad_scores = (probs * (grad_prob - delta)).astype(BF)
        grad_q = dot(grad_scores, k_all) * scale
        gk_ref[...] += dot_tn(grad_scores, kq_ref[at, :]) * scale
        gv_ref[...] += dot_tn(probs.astype(BF), attn_round)
        gat_ref[at, :] = grad_q
        return 0

    lax.fori_loop(0, blocks, mix, 0)

    dt_ref[...] = col_ref[...].T
    lower = lower_tri(rows)

    def unwind(i, sums):
        at = pl.ds(pl.multiple_of((blocks - 1 - i) * rows, rows), rows)
        after, bias_sum, rate_sum = sums
        slab = slice(plan.s_dt, plan.s_dt + 128)
        dt_step, rate, shifted, live = steps_of(plan, head_ref, proj_ref[at, slab])
        col_slab = dt_ref[at, :]
        grad_cum = row_ref[at, :] - dt_step * col_slab
        grad_decay = dot_tn(lower, grad_cum, EXACT) + after
        grad_dt = jnp.where(live, (col_slab - rate * grad_decay) * sigmoid(shifted), 0.0)
        z_part = ga_ref[at, slab].astype(F32)
        ga_ref[at, slab] = (jnp.where(lane < off, z_part, 0.0) + grad_dt).astype(BF)
        return (
            after + jnp.sum(grad_cum, axis=0, keepdims=True),
            bias_sum + jnp.sum(grad_dt, axis=0, keepdims=True),
            rate_sum + jnp.sum(grad_decay * (-dt_step * rate), axis=0, keepdims=True),
        )

    blank = jnp.zeros((1, 128), F32)
    _, bias_sum, rate_sum = lax.fori_loop(0, blocks, unwind, (blank, blank, blank))

    def finish(b, sums):
        low = pl.multiple_of(b * rows, rows)
        at = pl.ds(low, rows)
        pre = pre_ref[at, :]
        grad_act = gact_ref[at, :]
        grad_x = grad_act[:, plan.o_x :] + skip * gy_ref[at, :]
        grad_act = jnp.concatenate([grad_act[:, : plan.o_x], grad_x], axis=1)
        grad_pre = grad_act * silu_grad(pre, sigmoid(pre))
        gext_ref[at, :] = grad_pre
        pos = linked_rows(plan, lengths_ref, low)[1]
        ext = ext_ref[pl.ds(low, rows + 8), :]
        new = []
        for k in range(KCONV):
            step = KCONV - 1 - k
            moved = ext[8 - step : 8 - step + rows] * (pos >= step).astype(F32)
            new.append(sums[k] + jnp.sum(grad_pre * moved, axis=0, keepdims=True))
        new.append(sums[KCONV] + jnp.sum(grad_pre, axis=0, keepdims=True))
        grad_q = gat_ref[at, :]
        grad_k = gk_ref[at, :]
        both = turn(jnp.where(lane < HDIM, grad_q, grad_k), cos_ref[at, :], -sin_ref[at, :])
        ga_ref[at, plan.o_q :] = both.astype(BF)
        return tuple(new)

    blank = jnp.zeros((1, plan.conv), F32)
    g_taps = lax.fori_loop(0, blocks, finish, (blank,) * (KCONV + 1))

    def close(b, total):
        low = pl.multiple_of(b * rows, rows)
        at = pl.ds(low, rows)
        ext = gext_ref[pl.ds(low, rows + 8), :]
        index = lax.broadcasted_iota(jnp.int32, (rows, 1), 0) + low
        grad_conv = jnp.zeros((rows, plan.conv), F32)
        for k in range(KCONV):
            step = KCONV - 1 - k
            later = index + step
            fits = (later - first_rows(lengths_ref, later) >= step).astype(F32)
            grad_conv = grad_conv + taps[k] * (ext[step : step + rows] * fits)
        ga_ref[at, : plan.conv] = grad_conv.astype(BF)
        v_part = jnp.where(in_v, gv_ref[at, :], 0.0)
        if plan.s_v < plan.conv:
            v_part = v_part + jnp.where(in_v, 0.0, grad_conv[:, plan.s_v : plan.s_v + 128])
        ga_ref[at, plan.s_v : plan.s_v + 128] = v_part.astype(BF)
        partial = dot_nt(ga_ref[at, :], w_ref[:, : plan.a_w])
        normed = rms_forward(x_ref[at, :].astype(F32))[0]
        keep, give = split_rows(plan, partial, t_id)
        out = pl.ds(pl.multiple_of(b * plan.half, plan.half), plan.half)
        keep_ref[out, :] = keep.astype(BF)
        give_ref[out, :] = give.astype(BF)
        return total + jnp.sum(partial * normed, axis=0, keepdims=True)

    g_gain = lax.fori_loop(0, blocks, close, jnp.zeros((1, width), F32))

    def rows_at(entries, count):
        index = lax.broadcasted_iota(jnp.int32, (128, 1), 0)
        total = jnp.zeros((128, count), F32)
        for i, value in entries:
            high = value.astype(BF).astype(F32)
            total = jnp.where(index == row + i, high, total)
            total = jnp.where(index == row + plan.n_small + i, value - high, total)
        return total

    lane_d = lanes(width) % plan.d_loc
    head_vals = jnp.zeros((1, width), F32)
    for j in range(heads):
        picks = (
            jnp.sum(jnp.where(lane == off + j, bias_sum, 0.0), axis=1, keepdims=True),
            jnp.sum(jnp.where(lane == off + j, rate_sum, 0.0), axis=1, keepdims=True),
            jnp.sum(jnp.where(lane_w // HDIM == j, skip_sum, 0.0), axis=1, keepdims=True),
        )
        for i in range(3):
            head_vals = jnp.where(lane_d == i * heads + j, picks[i], head_vals)
    direct = rows_at([(0, g_gain), (1, gain2_ref[...]), (plan.n_small - 1, head_vals)], width)
    selected = [
        rows_at([(2 + k, g_taps[k][:, : 2 * NSTATE]) for k in range(KCONV + 1)], 2 * NSTATE)
    ]
    for k in range(KCONV + 2):
        source = g_taps[k][:, plan.o_x :] if k <= KCONV else g_norm_gain
        selected.append(
            rows_at(
                [
                    (KCONV + 3 + j, jnp.where(lane_w // HDIM == j, source, 0.0))
                    for j in range(heads)
                ],
                wide,
            )
        )
    selected = jnp.concatenate(selected, axis=1).astype(BF)
    small = direct.T + dot_nt(sel_ref[...], selected)
    small_ref[...] = small
    chunk = 256

    def weigh(i, _):
        part = pl.ds(pl.multiple_of(i * chunk, chunk), chunk)
        pack_ref[part, : plan.a_w] = dot_tn(norm_ref[:, part], ga_ref[...]).astype(BF)
        slab = slice(plan.s_dt, plan.s_dt + 128)
        pack_ref[part, slab] = jnp.where(
            lane < row, pack_ref[part, slab].astype(F32), small_ref[part, :]
        ).astype(BF)
        pack_ref[part, plan.o_mo : plan.o_mo + wide] = dot_tn(
            gs_ref[:, part], ni_ref[...]
        ).astype(BF)
        slab = slice(plan.s_ao, plan.s_ao + 128)
        attn = dot_tn(got_ref[:, part], attn_ref[...])
        if plan.off:
            attn = jnp.where(in_v, attn, pack_ref[part, slab].astype(F32))
        pack_ref[part, slab] = attn.astype(BF)
        return 0

    lax.fori_loop(0, width // chunk, weigh, 0)


def sum_kernel(plan, got_ref, out_ref):
    lane = lanes(128)
    row, count = plan.row, plan.n_small
    slab = slice(plan.s_dt, plan.s_dt + 128)

    def one(c, _):
        at = pl.ds(pl.multiple_of(c * plan.d_loc, plan.d_loc), plan.d_loc)
        total = got_ref[0, at, :].astype(F32)
        for f in range(1, got_ref.shape[0]):
            total = total + got_ref[f, at, :].astype(F32)
        out_ref[at, :] = total.astype(BF)
        part = total[:, slab]
        small = part + pltpu.roll(part, 128 - count, 1)
        high = small.astype(BF).astype(F32)
        low = pltpu.roll(small - high, count, 1)
        part = jnp.where(
            lane < row, part, jnp.where(lane < row + count, high, low)
        )
        out_ref[at, slab] = jnp.where(lane < row + 2 * count, part, 0.0).astype(BF)
        return 0

    lax.fori_loop(0, got_ref.shape[1] // plan.d_loc, one, 0)


def pack_kernel(plan, inner_ref, kv_ref, query_ref, dt_ref, bc_ref, gain_ref, conv_ref, chan_ref,
                mout_ref, aout_ref, out_ref, turn_ref):
    heads, chan, row = plan.heads, plan.chan, plan.row
    count = out_ref.shape[0]
    heads_t, q_t = mout_ref.shape[1] // HDIM, aout_ref.shape[1] // HDIM
    dts = dt_ref[...].astype(F32)
    chans = chan_ref[...].astype(F32)
    query = query_ref[...].astype(F32)
    turn_ref[...] = jnp.zeros(turn_ref.shape, F32)
    turn_ref[row : row + 2, : plan.d_loc] = gain_ref[...].astype(F32)
    turn_ref[row + 2 : row + KCONV + 3, : plan.cc] = conv_ref[...].astype(F32)
    for c in range(count):
        live = max(0, min(heads, heads_t - c * heads))
        wide = live * HDIM
        out_ref[c] = jnp.zeros(out_ref.shape[1:], BF)
        out_ref[c, :, : 2 * NSTATE] = bc_ref[...]
        low = row + KCONV + 3
        if live:
            at = c * heads
            turn_ref[low : low + live, : plan.mc] = chans[at : at + live]
            turn_ref[plan.off : plan.off + live, : plan.d_loc] = dts[at : at + live]
        else:
            turn_ref[low : low + heads, :] = jnp.zeros((heads, 128), F32)
            turn_ref[plan.off : plan.off + heads, :] = jnp.zeros((heads, 128), F32)
        slab = turn_ref[...].T[: plan.d_loc]
        out_ref[c, :, plan.s_dt : plan.s_dt + 128] = slab.astype(BF)
        if live:
            at = c * chan
            out_ref[c, :, plan.o_z : plan.o_z + wide] = inner_ref[:, at : at + wide]
            at = at + heads_t * HDIM
            out_ref[c, :, plan.o_x : plan.o_x + wide] = inner_ref[:, at : at + wide]
            at = c * chan
            out_ref[c, :, plan.o_mo : plan.o_mo + wide] = mout_ref[:, at : at + wide]
        if c < q_t:
            at = c * HDIM
            out_ref[c, :, plan.o_q : plan.o_q + HDIM] = query[:, at : at + HDIM].astype(BF)
            out_ref[c, :, plan.o_ao : plan.o_ao + HDIM] = aout_ref[:, at : at + HDIM]
        out_ref[c, :, plan.o_k : plan.o_k + HDIM] = kv_ref[:, :HDIM]
        out_ref[c, :, plan.o_v : plan.o_v + HDIM] = kv_ref[:, HDIM:]


def unpack_kernel(plan, heads_t, q_t, got_ref, inner_ref, query_ref, dt_ref, kv_ref, mout_ref,
                  aout_ref, chan_ref, head_ref, tail_ref):
    heads, chan, off, row = plan.heads, plan.chan, plan.off, plan.row
    count = got_ref.shape[0]
    kv_sum = jnp.zeros((plan.d_loc, 128), F32)
    bc_sum = jnp.zeros((plan.d_loc, 2 * NSTATE), F32)
    small_sum = jnp.zeros((plan.d_loc, 128), F32)
    lane = lanes(128)
    for c in range(count):
        live = max(0, min(heads, heads_t - c * heads))
        wide = live * HDIM
        query = got_ref[c, :, plan.o_q :].astype(F32)[:, :128]
        value = got_ref[c, :, plan.s_v : plan.s_v + 128].astype(F32)
        value = value if off == HDIM else pltpu.roll(value, HDIM, 1)
        kv_sum = kv_sum + jnp.where(lane < HDIM, pltpu.roll(query, HDIM, 1), value)
        bc_sum = bc_sum + got_ref[c, :, : 2 * NSTATE].astype(F32)
        slab = got_ref[c, :, plan.s_dt : plan.s_dt + 128].astype(F32)
        small = slab + pltpu.roll(slab, 128 - plan.n_small, 1)
        small_sum = small_sum + small
        if c < q_t:
            query_ref[:, c * HDIM : (c + 1) * HDIM] = query[:, :HDIM]
            out = got_ref[c, :, plan.s_ao : plan.s_ao + 128].astype(F32)
            aout_ref[:, c * HDIM : (c + 1) * HDIM] = out[:, off : off + HDIM]
        if live:
            low = c * chan
            for i, start in enumerate((plan.o_z, plan.o_x)):
                part = got_ref[c, :, start : start + plan.wide].astype(F32)
                at = i * heads_t * HDIM + low
                inner_ref[:, at : at + wide] = part[:, :wide]
            out = got_ref[c, :, plan.o_mo : plan.o_mo + plan.wide].astype(F32)
            mout_ref[:, low : low + wide] = out[:, :wide]
            turned = jnp.where(lane < row, slab, small).T
            at = c * heads
            dt_ref[at : at + live, :] = turned[off : off + live, : plan.d_loc]
            low = row + KCONV + 3
            chan_ref[at : at + live, :] = turned[low : low + live, : plan.mc]
            last = turned[row + plan.n_small - 1 : row + plan.n_small]
            for i in range(3):
                head_ref[i : i + 1, at : at + live] = last[:, i * heads : i * heads + live]
    kv_ref[...] = kv_sum
    tail_ref[:, : 2 * NSTATE] = bc_sum
    tail_ref[:, 2 * NSTATE :] = small_sum


def call(kernel, plan, outs, scratch, scalars, arrays):
    smem = pl.BlockSpec(memory_space=pltpu.SMEM)
    vmem = pl.BlockSpec(memory_space=pltpu.VMEM)
    return pl.pallas_call(
        lambda *refs: kernel(plan, *refs),
        out_shape=[jax.ShapeDtypeStruct(shape, kind) for shape, kind in outs],
        in_specs=[smem] * len(scalars) + [vmem] * len(arrays),
        out_specs=[vmem] * len(outs),
        scratch_shapes=[pltpu.VMEM(shape, kind) for shape, kind in scratch],
        compiler_params=pltpu.CompilerParams(vmem_limit_bytes=48 << 20),
    )(*scalars, *arrays)


def per_device(
    inputs,
    seq_lengths,
    norm_gains,
    mamba_in,
    dt_proj,
    bc_proj,
    mamba_chan,
    bc_conv,
    head_params,
    query_proj,
    kv_proj,
    attn_out,
    mamba_out,
    mlp_in,
    mlp_out,
    out_grad,
):
    n_f = lax.axis_size(S_FSDP)
    n_c = lax.axis_size(S_CONTEXT)
    c_id = lax.axis_index(S_CONTEXT)
    t_id = lax.axis_index(S_TENSOR)
    shards = n_f * n_c
    rows = inputs.shape[0]
    group = rows * n_c
    half = rows // 2
    d_loc = mamba_in.shape[0]
    width = d_loc * shards
    heads_t = head_params.shape[1]
    heads = -(-heads_t // n_c)
    heads_pad = heads * n_c
    q_t = query_proj.shape[1] // HDIM
    ff = mlp_in.shape[2]
    cc = bc_conv.shape[1]
    mc = mamba_chan.shape[1]
    plan = Plan(group, rows, width, d_loc, heads, 2 * heads_t * HDIM, cc, mc)
    bc_w = 2 * NSTATE
    p_w = plan.p_w

    (pack,) = call(
        pack_kernel,
        plan,
        [((n_c, d_loc, p_w), BF)],
        [((128, 128), F32)],
        (),
        (
            mamba_in.reshape(d_loc, 2 * heads_t * HDIM),
            kv_proj.reshape(d_loc, 2 * HDIM),
            query_proj,
            dt_proj.T,
            bc_proj,
            norm_gains,
            bc_conv,
            mamba_chan,
            mamba_out.T,
            attn_out.T,
        ),
    )

    mine = lax.dynamic_slice_in_dim(inputs, t_id * half, half, 0)
    part = exchange(pack, S_CONTEXT).reshape(n_c * d_loc, p_w)
    got_in = spread_async(mine, S_CONTEXT)
    w_all = spread(part, S_FSDP).reshape(width, p_w)
    rows_in = join_pair(got_in, swap_pair(got_in), t_id, 1).reshape(group, width)
    part_mi = spread_async(mlp_in.reshape(d_loc, 2 * ff), S_CONTEXT)
    part_mo = spread_async(mlp_out.T, S_CONTEXT)
    w_mi = plane_gather(part_mi.reshape(n_c * d_loc, 2 * ff)).reshape(width, 2 * ff)
    w_mo = plane_gather(part_mo.reshape(n_c * d_loc, ff)).reshape(width, ff)

    starts = jnp.cumsum(seq_lengths[0]) - seq_lengths[0]
    row_ids = jnp.arange(group, dtype=jnp.int32)
    inside = row_ids[:, None] >= starts[None, :]
    positions = row_ids - jnp.max(jnp.where(inside, starts[None, :], 0), axis=1)
    freqs = jnp.power(ROPE_BASE, -jnp.arange(HDIM // 2).astype(F32) * (2.0 / HDIM))
    angles = positions.astype(F32)[:, None] * jnp.concatenate([freqs] * 4)[None, :]
    trig = jnp.concatenate([jnp.cos(angles), jnp.sin(angles)], axis=1)
    head_vec = lax.dynamic_slice_in_dim(
        pad_to(head_params, 1, heads_pad), c_id * heads, heads, 1
    )
    feature = jnp.arange(width, dtype=jnp.int32)[:, None]
    place = feature % d_loc
    shard = feature // d_loc
    lane = jnp.arange(plan.wide, dtype=jnp.int32)[None, :] % HDIM
    sel = [(place < cc) & (shard * cc + place == jnp.arange(bc_w, dtype=jnp.int32)[None, :])]
    for k in range(KCONV + 2):
        sel.append((place < mc) & (shard * mc + place == k * HDIM + lane))
    sel = jnp.concatenate(sel, axis=1).astype(BF)
    scalars = (seq_lengths, head_vec, t_id.reshape(1))
    slab_w = 2 * width + 128
    part_rows = n_c * half
    keep, give, gain_one, gain_two, taps, norm, proj, pre, wide, thin = call(
        forward_kernel,
        plan,
        [
            ((part_rows, slab_w), BF),
            ((part_rows, slab_w), BF),
            ((1, width), F32),
            ((1, width), F32),
            ((8, plan.conv), F32),
            ((group, width), BF),
            ((group, plan.a_w), F32),
            ((group, plan.conv), F32),
            ((group, plan.wide + 256), F32),
            ((group, 384), BF),
        ],
        [((group, plan.conv), BF), ((group + 8, plan.conv), F32), ((group, 128), F32)],
        scalars,
        (rows_in, w_all, sel, trig),
    )
    gain_mlp = gain_two[0]

    def pair_parts(values, lead):
        parts = values.reshape(lead + (2, half) + values.shape[1:])
        keep = lax.dynamic_index_in_dim(parts, t_id, len(lead), False)
        return keep, lax.dynamic_index_in_dim(parts, 1 - t_id, len(lead), False)

    def pair_sum(values, lead):
        keep, give = pair_parts(values, lead)
        return keep + swap_pair(give.astype(BF)).astype(F32)

    def pair_add(keep, give):
        return (keep.astype(F32) + swap_pair(give).astype(F32)).astype(BF)

    summed = pair_add(keep, give).reshape(n_c, half, slab_w)
    both = jnp.sum(exchange(summed, S_CONTEXT).astype(F32), axis=0)
    squares = jnp.sum(both[:, 2 * width : 2 * width + 4], axis=1, keepdims=True)
    scale_own = lax.rsqrt(squares / plan.total + NORM_EPS)
    mamba_own = both[:, :width]
    in_own = mine.astype(F32)
    residual = in_own + scale_own * mamba_own + both[:, width : 2 * width]

    normed_two, inv_two = rms_forward(residual)
    norm_two_own = (normed_two * gain_mlp[None, :]).astype(BF)
    norm_two = join_pair(norm_two_own, swap_pair(norm_two_own), t_id, 0).reshape(rows, width)
    stacked = jnp.concatenate([norm_two, out_grad], axis=0)
    first = dot(norm_two, w_mi)
    gate_val = first[:, :ff]
    up_val = first[:, ff:]
    grad_act = dot(out_grad, w_mo)
    gate_sig = sigmoid(gate_val)
    gate_act = gate_val * gate_sig
    mlp_act = (gate_act * up_val).astype(BF)
    grad_gate = (grad_act * up_val * silu_grad(gate_val, gate_sig)).astype(BF)
    grad_up = (grad_act * gate_act).astype(BF)
    blank = jnp.zeros((rows, ff), BF)
    mixed = jnp.concatenate(
        [
            jnp.concatenate([grad_gate, grad_up, blank], axis=1),
            jnp.concatenate([blank, blank, mlp_act], axis=1),
        ],
        axis=0,
    )
    grad_two = pair_sum(dot_nt(mixed[:rows, : 2 * ff], w_mi), ())
    top_own = lax.dynamic_slice_in_dim(out_grad, t_id * half, half, 0).astype(F32)
    g_gain_mlp = jnp.sum(grad_two * normed_two, axis=0)
    grad_res = top_own + rms_backward(grad_two, normed_two, inv_two, gain_mlp)
    grad_rs_own = jnp.sum(grad_res * mamba_own, axis=1, keepdims=True)
    factor = split(jnp.concatenate([grad_rs_own, scale_own], axis=1), 2)
    got = spread(jnp.concatenate([grad_res.astype(BF), factor], axis=1), S_CONTEXT)
    got_other = swap_pair(got)
    block = n_c * d_loc

    def mlp_block(target, part):
        low = target * block + part * (block // 2)
        cols = lax.dynamic_slice_in_dim(stacked, low, block // 2, 1)
        return dot_tn(cols, mixed)

    own = plane_reduce(mlp_block)
    own = reduce_async(own.reshape(n_c, d_loc, 3 * ff), S_CONTEXT)
    out_mi = own[:, : 2 * ff].reshape(d_loc, 2, ff)
    out_mo = own[:, 2 * ff :].T

    keep, give, g_pack = call(
        backward_kernel,
        plan,
        [((part_rows, width), BF), ((part_rows, width), BF), ((width, p_w), BF)],
        [
            ((group, plan.conv), BF),
            ((group + 8, plan.conv), F32),
            ((group, width), BF),
            ((group, plan.wide), BF),
            ((group, plan.wide), F32),
            ((group, plan.a_w), BF),
            ((group, plan.conv), F32),
            ((group + 8, plan.conv), F32),
            ((group, 128), F32),
            ((group, 128), F32),
            ((group, 128), F32),
            ((group, 128), F32),
            ((128, group), F32),
            ((128, group), F32),
            ((128, group), F32),
            ((width, 128), F32),
            ((group, 128), F32),
            ((group, width + 128), BF),
        ],
        scalars,
        (
            rows_in, w_all, sel, trig, taps, norm, proj, pre, wide, thin, got,
            got_other,
            g_gain_mlp[None],
        ),
    )
    mlp_act, residual, keep = lax.optimization_barrier((mlp_act, residual, keep))
    out_own = (residual + pair_sum(dot_nt(mlp_act, w_mo), ())).astype(BF)
    partial = pair_add(keep, give).reshape(n_c, half, width)
    grad_one = reduce_async(partial, S_CONTEXT)
    gain_mix = gain_one[0]
    normed_own, inv_own = rms_forward(in_own)
    grad_in_own = grad_res + rms_backward(grad_one, normed_own, inv_own, gain_mix)
    output = join_pair(out_own, swap_pair(out_own), t_id, 0).reshape(rows, width)
    input_grad = join_pair(grad_in_own, swap_pair(grad_in_own), t_id, 0).reshape(rows, width)

    got = exchange(g_pack.reshape(n_f, block, p_w), S_FSDP)
    (g_pack,) = call(sum_kernel, plan, [((block, p_w), BF)], [], (), (got,))
    got = exchange(g_pack.reshape(n_c, d_loc, p_w), S_CONTEXT)
    out_inner, out_query, out_dt, out_kv, out_mout, out_aout, out_chan, out_heads, tail = call(
        lambda plan, *refs: unpack_kernel(plan, heads_t, q_t, *refs),
        plan,
        [
            ((d_loc, 2 * heads_t * HDIM), F32),
            ((d_loc, q_t * HDIM), F32),
            ((heads_t, d_loc), F32),
            ((d_loc, 2 * HDIM), F32),
            ((d_loc, heads_t * HDIM), F32),
            ((d_loc, q_t * HDIM), F32),
            ((heads_t, mc), F32),
            ((3, heads_t), F32),
            ((d_loc, bc_w + 128), F32),
        ],
        [],
        (),
        (got,),
    )
    tail = tail + swap_pair(tail)
    out_inner = out_inner.reshape(d_loc, 2, heads_t * HDIM)
    out_kv = out_kv.reshape(d_loc, 2, HDIM)
    out_dt, out_mout, out_aout = out_dt.T, out_mout.T, out_aout.T
    out_bc = tail[:, :bc_w]
    low = bc_w + plan.row
    out_gains = tail[:, low : low + 2].T
    out_convbc = tail[:cc, low + 2 : low + KCONV + 3].T

    return (
        output,
        input_grad,
        out_gains,
        out_inner,
        out_dt,
        out_bc,
        out_chan,
        out_convbc,
        out_heads,
        out_query,
        out_kv,
        out_aout,
        out_mout,
        out_mi,
        out_mo,
    )


def solution(mesh):
    both = (S_FSDP, S_CONTEXT)
    rows = P(both, None)

    return jax.shard_map(
        per_device,
        mesh=mesh,
        in_specs=(
            rows,
            P(S_FSDP, None),
            P(None, both),
            P(both, None, S_TENSOR),
            P(both, S_TENSOR),
            rows,
            P(S_TENSOR, both),
            P(None, both),
            P(None, S_TENSOR),
            P(both, S_TENSOR),
            P(both, None, S_TENSOR),
            P(S_TENSOR, both),
            P(S_TENSOR, both),
            P(both, None, S_TENSOR),
            P(S_TENSOR, both),
            rows,
        ),
        out_specs=(
            rows,
            rows,
            P(None, both),
            P(both, None, S_TENSOR),
            P(both, S_TENSOR),
            rows,
            P(S_TENSOR, both),
            P(None, both),
            P(None, S_TENSOR),
            P(both, S_TENSOR),
            P(both, None, S_TENSOR),
            P(S_TENSOR, both),
            P(S_TENSOR, both),
            P(both, None, S_TENSOR),
            P(S_TENSOR, both),
        ),
        check_vma=False,
    )
```
